32 devices in a mesh: batch: 8 (over z, x), seq: 4 (over y, core).
Axes of the slice: x: 2, y: 2, z: 4, core: 2. Of those that a mesh axis runs over, the one named last changes fastest.
Arguments:
- tokens: bfloat16 [8, 1024, 1024], P('batch', 'seq'), may hold values from -6 to 6
- cotangent: bfloat16 [8, 1024, 1024], P('batch', 'seq'), may hold values from -6 to 6
- image_tokens: bfloat16 [8, 1025, 768], P('batch'), may hold values from -6 to 6
- image_lengths: int32 [8], P('batch'), may hold values from 512 to 1025, as said below
- key_mask: int32 [8, 1025], P('batch'), may hold values 0 or 1
- camera: bfloat16 [8, 1024], P(None, 'batch'), may hold values from -6 to 6
- modulation: bfloat16 [1024, 6144], P('batch'), may hold values from -0.1875 to 0.1875
- q_cross: bfloat16 [1024, 1024], P('batch'), may hold values from -0.1875 to 0.1875
- kv_image: bfloat16 [768, 2048], P('batch'), may hold values from -0.21875 to 0.21875
- out_cross: bfloat16 [1024, 1024], P('batch'), may hold values from -3.5 to 3.5
- qkv_self: bfloat16 [1024, 3072], P('batch'), may hold values from -0.1875 to 0.1875
- out_self: bfloat16 [1024, 1024], P('batch'), may hold values from -6 to 6
- mlp_in: bfloat16 [1024, 4096], P('batch'), may hold values from -0.1875 to 0.1875
- mlp_out: bfloat16 [4096, 1024], P('batch'), may hold values from -0.09375 to 0.09375
Outputs:
- output: bfloat16 [8, 1024, 1024], P('batch', 'seq')
- grad_tokens: float32 [8, 1024, 1024], P('batch', 'seq')
- grad_modulation: float32 [1024, 6144], P('batch')
- grad_q_cross: float32 [1024, 1024], P('batch')
- grad_kv_image: float32 [768, 2048], P('batch')
- grad_out_cross: float32 [1024, 1024], P('batch')
- grad_qkv_self: float32 [1024, 3072], P('batch')
- grad_out_self: float32 [1024, 1024], P('batch')
- grad_mlp_in: float32 [1024, 4096], P('batch')
- grad_mlp_out: float32 [4096, 1024], P('batch')
The draws below stay inside these ranges and needn't reach their ends.
Inputs may be any that keep to these rules, and one draw needn't show every extreme that they name: `image_lengths`: some object has 1025 valid image tokens and some has 512.
All inputs are finite; a program needn't handle non-finite values. No bound on the sum of `key_mask` on one device may be relied on, other than what follows from the above.
Results may differ from the reference program's by a relative error of at most 0.025.
The reference program's roundings to bfloat16 on the way count: a program that leaves them out, or rounds other values in their place, can miss the bound.
Values may be sent and summed in bfloat16 or wider, within the bound.
A program may use at most 256 MiB of HBM per device.

```python
import jax
import jax.numpy as jnp
from jax import lax

D = 1024
HEADS = 16
HEAD_DIM = 64
FF = 4096
DI = 768
CAM = 1024
IMG = 1025
TRI = 1024
OBJ = 8


def draw_image_lengths(key, part):
    draw_key, pick_key = jax.random.split(jax.random.fold_in(key, 7))
    lengths = jax.random.randint(draw_key, (OBJ,), IMG // 2, IMG + 1)
    order = jax.random.permutation(pick_key, OBJ)
    lengths = lengths.at[order[0]].set(IMG).at[order[1]].set(IMG // 2)
    return lengths.astype(jnp.int32)


def place_ends(entries, key, smallest, high):
    place = [jax.random.randint(jax.random.fold_in(key, axis), (), 0, length) for axis, length in enumerate(entries.shape)]
    longest = entries.shape.index(max(entries.shape))
    beside = place[:longest] + [(place[longest] + 1) % entries.shape[longest]] + place[longest + 1:]
    return entries.at[tuple(place)].set(smallest).at[tuple(beside)].set(high)


def block_levels(own_key, dims, cuts, low, high):
    def one(dim, blocks):
        steps = jax.random.uniform(jax.random.fold_in(jax.random.fold_in(own_key, 6), dim), (blocks,), jnp.float32, low / len(cuts), high / len(cuts))
        return jnp.repeat(jnp.exp(steps), dims[dim] // blocks).reshape((-1,) + (1,) * (len(dims) - dim - 1))

    factor_of = one(*cuts[0])
    for cut in cuts[1:]:
        factor_of = factor_of * one(*cut)
    return factor_of


def centred(stream_key, shape, deviation, limit, shards=(), held_as=jnp.bfloat16):
    array = jax.random.normal(stream_key, shape, jnp.float32) * deviation
    if len(shards) > 0:
        array = block_levels(stream_key, shape, shards, -0.22, 0.18) * array
    return jnp.clip(array, min=-limit, max=limit).astype(held_as)


def setup_inputs(seed: int = 0) -> dict:
    key_of = jax.random.split(jax.random.key(seed), 15)
    tokens = centred(key_of[0], (OBJ, TRI, D), 1.0, 6.0, ((0, 8), (1, 4)))
    cotangent = centred(key_of[1], (OBJ, TRI, D), 1.0, 6.0, ((0, 8), (1, 4)))
    image_tokens = centred(key_of[2], (OBJ, IMG, DI), 1.0, 6.0, ((0, 8),))
    image_lengths = draw_image_lengths(jax.random.fold_in(key_of[14], 71), 0)
    key_mask = place_ends((jax.random.randint(key_of[4], (OBJ, IMG), 0, 4) < 3).astype(jnp.int32), jax.random.fold_in(key_of[4], 1), 0, 1)
    camera = centred(key_of[5], (OBJ, CAM), 1.0, 6.0, ((1, 8),))
    modulation = centred(key_of[6], (CAM, 6 * D), CAM ** -0.5, 0.1875, ((0, 8),))
    q_cross = centred(key_of[7], (D, D), D ** -0.5, 0.1875, ((0, 8),))
    kv_image = centred(key_of[8], (DI, 2 * D), DI ** -0.5, 0.21875, ((0, 8),))
    out_cross = centred(key_of[9], (D, D), 3.0 ** -0.5, 3.5, ((0, 8),))
    qkv_self = centred(key_of[10], (D, 3 * D), D ** -0.5, 0.1875, ((0, 8),))
    out_self = centred(key_of[11], (D, D), 1.0 ** -0.5, 6.0, ((0, 8),))
    mlp_in = centred(key_of[12], (D, FF), D ** -0.5, 0.1875, ((0, 8),))
    mlp_out = centred(key_of[13], (FF, D), FF ** -0.5, 0.09375, ((0, 8),))
    return {"tokens": tokens, "cotangent": cotangent, "image_tokens": image_tokens, "image_lengths": image_lengths, "key_mask": key_mask, "camera": camera, "modulation": modulation, "q_cross": q_cross, "kv_image": kv_image, "out_cross": out_cross, "qkv_self": qkv_self, "out_self": out_self, "mlp_in": mlp_in, "mlp_out": mlp_out}


@jax.custom_vjp
def low(v):
    return lax.optimization_barrier(v.astype(jnp.bfloat16)).astype(jnp.float32)

@jax.custom_vjp
def low_back(v):
    return v

def low_keep(v):
    return (low(v), None)

def low_pass(kept, grad):
    return (grad,)

def back_keep(v):
    return (v, None)

def back_low(kept, grad):
    return (low(grad),)
low.defvjp(low_keep, low_pass)
low_back.defvjp(back_keep, back_low)
highest = lax.Precision.HIGHEST
epsilon = 1e-06

def matmul(left, right):
    return jnp.dot(left, right, precision=highest)

def both_ways(value):
    return low(low_back(value))

def modulated_norm(values, shift, scale):
    center = values - lax.optimization_barrier(jnp.mean(values, axis=-1, keepdims=True))
    normed = center * lax.rsqrt(lax.optimization_barrier(jnp.mean(center * center, axis=-1, keepdims=True)) + epsilon)
    return normed * (1.0 + scale) + shift

def attention(query, key_rows, value_rows, valid):
    rows = query.shape[0]
    count = key_rows.shape[0]
    query_heads = query.reshape(rows, HEADS, HEAD_DIM).transpose(1, 0, 2)
    key_heads = key_rows.reshape(count, HEADS, HEAD_DIM).transpose(1, 0, 2)
    value_heads = value_rows.reshape(count, HEADS, HEAD_DIM).transpose(1, 0, 2)

    def one_head(pieces):
        query_one, key_one, value_one = pieces
        scores = low_back(jnp.dot(query_one, key_one.T, precision=highest) * HEAD_DIM ** (-0.5))
        scores = jnp.where(valid[None, :], scores, -1000000000.0)
        probs = low(jax.nn.softmax(scores, axis=-1))
        return jnp.dot(probs, value_one, precision=highest)
    outputs = lax.map(jax.checkpoint(one_head), (query_heads, key_heads, value_heads))
    return outputs.transpose(1, 0, 2).reshape(rows, HEADS * HEAD_DIM)

def block(token_rows, image_rows, valid, modulation_row, weights):
    q_cross, kv_image, out_cross, qkv_self, out_self, mlp_in, mlp_out = weights
    width = token_rows.shape[1]
    shifts = modulation_row.reshape(6, width)
    normed = low(modulated_norm(token_rows, shifts[0], shifts[1]))
    query = both_ways(matmul(normed, q_cross))
    image_kv = matmul(image_rows, kv_image)
    image_keys = low(image_kv[:, :width])
    image_values = low(image_kv[:, width:])
    attended = both_ways(attention(query, image_keys, image_values, valid))
    after_cross = token_rows + low_back(matmul(attended, out_cross))
    normed = low(modulated_norm(after_cross, shifts[2], shifts[3]))
    packed = matmul(normed, qkv_self)
    query = both_ways(packed[:, :width])
    self_keys = both_ways(packed[:, width:2 * width])
    self_values = both_ways(packed[:, 2 * width:])
    everywhere = jnp.ones((token_rows.shape[0],), dtype=jnp.bool_)
    attended = both_ways(attention(query, self_keys, self_values, everywhere))
    after_self = after_cross + low_back(matmul(attended, out_self))
    normed = low(modulated_norm(after_self, shifts[4], shifts[5]))
    hidden = low(jax.nn.gelu(low_back(matmul(normed, mlp_in))))
    return after_self + low_back(matmul(hidden, mlp_out))

def forward(token_all, image_all, valid_all, camera, modulation, weights):
    modulation_rows = matmul(low(jax.nn.silu(camera)), modulation)

    def one_object(pieces):
        token_rows, image_rows, valid, modulation_row = pieces
        return block(token_rows, image_rows, valid, modulation_row, weights)
    return lax.map(jax.checkpoint(one_object), (token_all, image_all, valid_all, modulation_rows))

def reference(tokens, cotangent, image_tokens, image_lengths, key_mask, camera, modulation, q_cross, kv_image, out_cross, qkv_self, out_self, mlp_in, mlp_out):
    positions = jnp.arange(IMG, dtype=jnp.int32)
    valid_all = (positions[None, :] < image_lengths[:, None]) & ((key_mask == 1) | (positions[None, :] == 0))
    weights = tuple((matrix.astype(jnp.float32) for matrix in (q_cross, kv_image, out_cross, qkv_self, out_self, mlp_in, mlp_out)))
    image_float = image_tokens.astype(jnp.float32)
    camera_float = camera.astype(jnp.float32)

    def run(token_all, modulation_all, weights_all):
        return forward(token_all, image_float, valid_all, camera_float, modulation_all, weights_all)
    output, pullback = jax.vjp(run, tokens.astype(jnp.float32), modulation.astype(jnp.float32), weights)
    grad_tokens, grad_modulation, grad_weights = pullback(cotangent.astype(jnp.float32))
    return (output.astype(jnp.bfloat16), grad_tokens, grad_modulation, grad_weights[0], grad_weights[1], grad_weights[2], grad_weights[3], grad_weights[4], grad_weights[5], grad_weights[6])
```

```python
import functools

import jax
import jax.numpy as jnp
from jax import lax
from jax.experimental import pallas as pl
from jax.experimental.pallas import tpu as pltpu
from jax.sharding import PartitionSpec as P

HEADS = 16
HEAD_DIM = 64


epsilon = 1e-06
group_heads = 4
highest = lax.Precision.HIGHEST
LIMIT = 64 * 1024 * 1024 - 64 * 1024


def modulated_norm(values, shift, scale):
    center = values - jnp.mean(values, axis=-1, keepdims=True)
    normed = center * lax.rsqrt(jnp.mean(center * center, axis=-1, keepdims=True) + epsilon)
    return normed * (1.0 + scale) + shift


def product(left, right):
    return jnp.dot(left, right, preferred_element_type=jnp.float32)


def contract_rows(left, right):
    return lax.dot_general(
        left, right, (((0,), (0,)), ((), ())), preferred_element_type=jnp.float32
    )


def times_transposed(left, right):
    return lax.dot_general(
        left, right, (((1,), (1,)), ((), ())), preferred_element_type=jnp.float32
    )


def split_heads(values):
    rows = values.shape[0]
    grouped = values.reshape(rows, HEADS // group_heads, group_heads, HEAD_DIM)
    return grouped.transpose(1, 2, 0, 3)


def join_heads(values):
    groups, inner, rows, depth = values.shape
    return values.transpose(2, 0, 1, 3).reshape(rows, groups * inner * depth)


def scores_of(query_group, key_group, valid):
    scores = jnp.einsum(
        "hqd,hkd->hqk", query_group, key_group, preferred_element_type=jnp.float32
    ) * HEAD_DIM ** (-0.5)
    return jnp.where(valid[None, None, :], scores, -1000000000.0)


def attend_forward(query, key_rows, value_rows, valid):

    def one_group(pieces):
        query_group, key_group, value_group = pieces
        scores = scores_of(query_group, key_group, valid)
        top = jnp.max(scores, axis=-1, keepdims=True)
        expo = jnp.exp(scores - top)
        total = jnp.sum(expo, axis=-1, keepdims=True)
        probs = (expo / total).astype(jnp.bfloat16)
        result = jnp.einsum("hqk,hkd->hqd", probs, value_group, preferred_element_type=jnp.float32)
        return (result, top, total)

    results, tops, totals = lax.map(
        one_group, (split_heads(query), split_heads(key_rows), split_heads(value_rows))
    )
    return (join_heads(results), (tops, totals))


def attend_backward(query, key_rows, value_rows, valid, stats, grad_output):
    tops, totals = stats

    def one_group(pieces):
        query_group, key_group, value_group, top, total, grad_group = pieces
        scores = scores_of(query_group, key_group, valid)
        probs = jnp.exp(scores - top) / total
        grad_probs = jnp.einsum(
            "hqd,hkd->hqk", grad_group, value_group, preferred_element_type=jnp.float32
        )
        inner = jnp.sum(probs * grad_probs, axis=-1, keepdims=True)
        grad_scores = (probs * (grad_probs - inner)).astype(jnp.bfloat16)
        factor = HEAD_DIM ** (-0.5)
        grad_query = (
            jnp.einsum("hqk,hkd->hqd", grad_scores, key_group, preferred_element_type=jnp.float32)
            * factor
        )
        grad_keys = (
            jnp.einsum("hqk,hqd->hkd", grad_scores, query_group, preferred_element_type=jnp.float32)
            * factor
        )
        grad_values = jnp.einsum(
            "hqk,hqd->hkd",
            probs.astype(jnp.bfloat16),
            grad_group,
            preferred_element_type=jnp.float32,
        )
        return (grad_query, inner, grad_keys, grad_values)

    results = lax.map(
        one_group,
        (
            split_heads(query),
            split_heads(key_rows),
            split_heads(value_rows),
            tops,
            totals,
            split_heads(grad_output),
        ),
    )
    return (join_heads(results[0]), results[1], join_heads(results[2]), join_heads(results[3]))


def local(
    tokens,
    cotangent,
    image_tokens,
    image_lengths,
    key_mask,
    camera,
    modulation,
    q_cross,
    kv_image,
    out_cross,
    qkv_self,
    out_self,
    mlp_in,
    mlp_out,
):
    q_full, kv_full, out_cross_full, qkv_full, out_self_full, mlp_in_full, mlp_out_full = (
        lax.all_gather(q_cross, "batch", axis=0, tiled=True),
        lax.all_gather(kv_image, "batch", axis=0, tiled=True),
        lax.all_gather(out_cross, "batch", axis=0, tiled=True),
        lax.all_gather(qkv_self, "batch", axis=0, tiled=True),
        lax.all_gather(out_self, "batch", axis=0, tiled=True),
        lax.all_gather(mlp_in, "batch", axis=0, tiled=True),
        lax.all_gather(mlp_out, "batch", axis=0, tiled=True),
    )
    camera_gate = jax.nn.silu(camera.astype(jnp.float32)).astype(jnp.bfloat16)
    modulation_all = lax.psum(product(camera_gate, modulation), "batch")
    object_index = lax.axis_index("batch")
    width = tokens.shape[2]
    shifts = lax.dynamic_index_in_dim(modulation_all, object_index, 0, keepdims=False).reshape(
        6, width
    )
    stream = tokens[0].astype(jnp.float32)
    image_rows = image_tokens[0]
    positions = jnp.arange(image_rows.shape[0], dtype=jnp.int32)
    valid = (positions < image_lengths[0]) & ((key_mask[0] == 1) | (positions == 0))
    everywhere = jnp.ones((lax.axis_size("seq") * stream.shape[0],), dtype=jnp.bool_)
    normed_cross, cross_pullback = jax.vjp(modulated_norm, stream, shifts[0], shifts[1])
    normed_cross = normed_cross.astype(jnp.bfloat16)
    query_cross = product(normed_cross, q_full).astype(jnp.bfloat16)
    image_kv = product(image_rows, kv_full)
    image_keys = image_kv[:, :width].astype(jnp.bfloat16)
    image_values = image_kv[:, width:].astype(jnp.bfloat16)
    attended_cross, cross_stats = attend_forward(query_cross, image_keys, image_values, valid)
    attended_cross = attended_cross.astype(jnp.bfloat16)
    after_cross = stream + product(attended_cross, out_cross_full)
    normed_self, self_pullback = jax.vjp(modulated_norm, after_cross, shifts[2], shifts[3])
    normed_self = normed_self.astype(jnp.bfloat16)
    packed = product(normed_self, qkv_full).astype(jnp.bfloat16)
    query_self = packed[:, :width]
    key_local = packed[:, width : 2 * width]
    value_local = packed[:, 2 * width :]
    key_whole, value_whole = (
        lax.all_gather(key_local, "seq", axis=0, tiled=True),
        lax.all_gather(value_local, "seq", axis=0, tiled=True),
    )
    attended_self, self_stats = attend_forward(query_self, key_whole, value_whole, everywhere)
    attended_self = attended_self.astype(jnp.bfloat16)
    after_self = after_cross + product(attended_self, out_self_full)
    normed_mlp, mlp_pullback = jax.vjp(modulated_norm, after_self, shifts[4], shifts[5])
    normed_mlp = normed_mlp.astype(jnp.bfloat16)
    up_rows = product(normed_mlp, mlp_in_full)
    hidden, gelu_pullback = jax.vjp(jax.nn.gelu, up_rows)
    hidden = hidden.astype(jnp.bfloat16)
    output = after_self + product(hidden, mlp_out_full)
    grad_stream = cotangent[0].astype(jnp.float32)
    grad_branch = grad_stream.astype(jnp.bfloat16)
    grad_mlp_out = contract_rows(hidden, grad_branch)
    (grad_up,) = gelu_pullback(times_transposed(grad_branch, mlp_out_full))
    grad_up = grad_up.astype(jnp.bfloat16)
    grad_mlp_in = contract_rows(normed_mlp, grad_up)
    grad_from, shift_mlp, scale_mlp = mlp_pullback(times_transposed(grad_up, mlp_in_full))
    grad_stream = grad_stream + grad_from
    grad_branch = grad_stream.astype(jnp.bfloat16)
    grad_out_self = contract_rows(attended_self, grad_branch)
    grad_attended = times_transposed(grad_branch, out_self_full).astype(jnp.bfloat16)
    grad_query, inner_local, key_terms, value_terms = attend_backward(
        query_self, key_whole, value_whole, everywhere, self_stats, grad_attended
    )
    grad_key, grad_value = (
        lax.psum_scatter(key_terms, "seq", scatter_dimension=0, tiled=True),
        lax.psum_scatter(value_terms, "seq", scatter_dimension=0, tiled=True),
    )
    grad_packed = jnp.concatenate([grad_query, grad_key, grad_value], axis=1).astype(jnp.bfloat16)
    grad_qkv_self = contract_rows(normed_self, grad_packed)
    grad_from, shift_self, scale_self = self_pullback(times_transposed(grad_packed, qkv_full))
    grad_stream = grad_stream + grad_from
    grad_branch = grad_stream.astype(jnp.bfloat16)
    grad_out_cross = contract_rows(attended_cross, grad_branch)
    grad_attended = times_transposed(grad_branch, out_cross_full).astype(jnp.bfloat16)
    grad_query, inner_cross, key_terms, value_terms = attend_backward(
        query_cross, image_keys, image_values, valid, cross_stats, grad_attended
    )
    image_float = image_rows.astype(jnp.float32)
    image_key_grad, image_value_grad = (
        lax.psum_scatter(
            key_terms.astype(jnp.bfloat16), "seq", scatter_dimension=1, tiled=True
        ).astype(jnp.float32),
        lax.psum_scatter(
            value_terms.astype(jnp.bfloat16), "seq", scatter_dimension=1, tiled=True
        ).astype(jnp.float32),
    )
    block_width = image_key_grad.shape[1]
    column_start = lax.axis_index("seq") * block_width
    image_grads = jnp.concatenate([image_key_grad, image_value_grad], axis=1)
    kv_block = lax.dot_general(
        image_float,
        image_grads,
        (((0,), (0,)), ((), ())),
        precision=highest,
        preferred_element_type=jnp.float32,
    )
    grad_kv_image = jnp.zeros((image_rows.shape[1], 2 * width), jnp.float32)
    grad_kv_image = lax.dynamic_update_slice(
        grad_kv_image, kv_block[:, :block_width], (jnp.int32(0), column_start)
    )
    grad_kv_image = lax.dynamic_update_slice(
        grad_kv_image, kv_block[:, block_width:], (jnp.int32(0), column_start + width)
    )
    grad_query = grad_query.astype(jnp.bfloat16)
    grad_q_cross = contract_rows(normed_cross, grad_query)
    grad_from, shift_cross, scale_cross = cross_pullback(times_transposed(grad_query, q_full))
    grad_input = grad_stream + grad_from
    grad_row = jnp.concatenate(
        [shift_cross, scale_cross, shift_self, scale_self, shift_mlp, scale_mlp]
    )
    grad_table = lax.dynamic_update_slice(
        jnp.zeros(modulation_all.shape, jnp.float32),
        grad_row[None, :],
        (object_index, jnp.int32(0)),
    )
    grad_table = lax.psum(grad_table, ("batch", "seq"))
    grad_modulation = lax.dot_general(
        camera_gate.astype(jnp.float32),
        grad_table,
        (((0,), (0,)), ((), ())),
        precision=highest,
        preferred_element_type=jnp.float32,
    )
    terms = (
        grad_q_cross,
        grad_kv_image,
        grad_out_cross,
        grad_qkv_self,
        grad_out_self,
        grad_mlp_in,
        grad_mlp_out,
    )
    shares = (
        lax.psum_scatter(
            terms[0].astype(jnp.bfloat16), "batch", scatter_dimension=0, tiled=True
        ).astype(jnp.float32),
        lax.psum_scatter(
            terms[1].astype(jnp.bfloat16), "batch", scatter_dimension=0, tiled=True
        ).astype(jnp.float32),
        lax.psum_scatter(
            terms[2].astype(jnp.bfloat16), "batch", scatter_dimension=0, tiled=True
        ).astype(jnp.float32),
        lax.psum_scatter(
            terms[3].astype(jnp.bfloat16), "batch", scatter_dimension=0, tiled=True
        ).astype(jnp.float32),
        lax.psum_scatter(
            terms[4].astype(jnp.bfloat16), "batch", scatter_dimension=0, tiled=True
        ).astype(jnp.float32),
        lax.psum_scatter(
            terms[5].astype(jnp.bfloat16), "batch", scatter_dimension=0, tiled=True
        ).astype(jnp.float32),
        lax.psum_scatter(
            terms[6].astype(jnp.bfloat16), "batch", scatter_dimension=0, tiled=True
        ).astype(jnp.float32),
    )
    totals = (
        lax.psum(shares[0].astype(jnp.bfloat16), "seq").astype(jnp.float32),
        lax.psum(shares[1].astype(jnp.bfloat16), "seq").astype(jnp.float32),
        lax.psum(shares[2].astype(jnp.bfloat16), "seq").astype(jnp.float32),
        lax.psum(shares[3].astype(jnp.bfloat16), "seq").astype(jnp.float32),
        lax.psum(shares[4].astype(jnp.bfloat16), "seq").astype(jnp.float32),
        lax.psum(shares[5].astype(jnp.bfloat16), "seq").astype(jnp.float32),
        lax.psum(shares[6].astype(jnp.bfloat16), "seq").astype(jnp.float32),
    )
    return (
        output.astype(jnp.bfloat16)[None],
        grad_input[None],
        grad_modulation,
        totals[0],
        totals[1],
        totals[2],
        totals[3],
        totals[4],
        totals[5],
        totals[6],
    )


bf16 = jnp.bfloat16
f32 = jnp.float32
MESH = pl.DeviceIdType.MESH
BELOW = -3.0e38


def nn(a, b):
    return jnp.dot(a, b, preferred_element_type=f32)


def nt(a, b):
    return lax.dot_general(a, b, (((1,), (1,)), ((), ())), preferred_element_type=f32)


def tn(a, b):
    return lax.dot_general(a, b, (((0,), (0,)), ((), ())), preferred_element_type=f32)


def one_head(pair, side):
    lane = lax.broadcasted_iota(jnp.int32, pair.shape, 1)
    return jnp.where(lane // HEAD_DIM == side, pair, jnp.zeros_like(pair))


def two_heads(first, second):
    lane = lax.broadcasted_iota(jnp.int32, first.shape, 1)
    return jnp.where(lane < HEAD_DIM, first, second)


def softmax_rows(scores, mask):
    if mask is not None:
        scores = jnp.where(mask[0:1, :] > 0.5, scores, mask[1:2, :])
    expo = jnp.exp(scores - jnp.max(scores, axis=-1, keepdims=True))
    return expo * (1.0 / jnp.sum(expo, axis=-1, keepdims=True))


def norm_stats(rows):
    center = rows - jnp.mean(rows, axis=-1, keepdims=True)
    inverse = lax.rsqrt(jnp.mean(center * center, axis=-1, keepdims=True) + epsilon)
    return center * inverse, inverse


def norm_forward(rows, shift, scale):
    return norm_stats(rows)[0] * (1.0 + scale) + shift


def norm_backward(rows, scale, grad):
    normed, inverse = norm_stats(rows)
    inner = grad * (1.0 + scale)
    mean_inner = jnp.mean(inner, axis=-1, keepdims=True)
    mean_cross = jnp.mean(inner * normed, axis=-1, keepdims=True)
    grad_rows = inverse * (inner - mean_inner - normed * mean_cross)
    return (
        grad_rows,
        jnp.sum(grad, axis=0, keepdims=True),
        jnp.sum(grad * normed, axis=0, keepdims=True),
    )


Q, KV, OC, QKV, OS, UP, DOWN, CAMERA, TABLE, TOKENS, OWN, IMAGE, COTANGENT = range(13)


class Sizes:
    def __init__(self, mesh_shape, inputs):
        self.batch, self.seq = mesh_shape["batch"], mesh_shape["seq"]
        self.own, self.width = inputs[0].shape[1:]
        self.image_rows, self.image_width = inputs[2].shape[1:]
        self.chunks = 4
        self.part = self.own // self.chunks
        self.rows = self.seq * self.part
        self.tokens = self.seq * self.own
        self.columns = self.width // self.seq
        self.hidden = inputs[12].shape[1] // self.seq
        self.keys = -(-self.image_rows // 128) * 128
        self.whole_rows = self.image_rows // 16 * 16
        self.block = self.width // self.batch
        self.image_block = self.image_width // self.batch
        self.weights = (
            (self.block, self.columns),
            (self.image_block, 2 * self.columns),
            (self.block, self.width),
            (self.block, 3 * self.columns),
            (self.block, self.width),
            (self.block, self.hidden),
            (self.hidden // self.batch, self.width),
        )


class Refs:
    def __init__(self, refs):
        rest = iter(refs)
        self.tokens = next(rest)
        self.cotangent = next(rest)
        self.image = next(rest)
        self.tail = next(rest)
        self.mask = next(rest)
        self.camera = next(rest)
        self.modulation = next(rest)
        self.q_cross = next(rest)
        self.kv_image = next(rest)
        self.out_cross = next(rest)
        self.qkv_self = next(rest)
        self.out_self = next(rest)
        self.mlp_in = next(rest)
        self.mlp_out = next(rest)
        self.output = next(rest)
        self.grad_tokens = next(rest)
        self.table = next(rest)
        self.gout = [next(rest) for _ in range(7)]
        self.weights = [next(rest) for _ in range(7)]
        self.firsts = [next(rest) for _ in range(7)]
        self.seconds = [next(rest) for _ in range(7)]
        self.buf_a = next(rest)
        self.buf_b = next(rest)
        self.buf_h2 = next(rest)
        self.buf_b2 = next(rest)
        self.part_main = next(rest)
        self.core_main = next(rest)
        self.send_main = next(rest)
        self.line_main = next(rest)
        self.part_side = next(rest)
        self.core_side = next(rest)
        self.send_side = next(rest)
        self.line_side = next(rest)
        self.image_all = next(rest)
        self.mask_all = next(rest)
        self.camera_own = next(rest)
        self.mods_all = next(rest)
        self.mods = next(rest)
        self.sums = next(rest)
        self.sums_seq = next(rest)
        self.normed1 = next(rest)
        self.query1 = next(rest)
        self.key1 = next(rest)
        self.value1 = next(rest)
        self.att1 = next(rest)
        self.packed2 = next(rest)
        self.att2 = next(rest)
        self.hidden = next(rest)
        self.grad_up = next(rest)
        self.grad_key = next(rest)
        self.grad_value = next(rest)
        self.x0 = next(rest)
        self.x1 = next(rest)
        self.x2 = next(rest)
        self.grads_a = next(rest)
        self.grads_b = next(rest)
        self.grads_c = next(rest)
        self.sem_load = next(rest)
        self.sem_wz_s = next(rest)
        self.sem_wz_r = next(rest)
        self.sem_wx_s = next(rest)
        self.sem_wx_r = next(rest)
        self.sem_gx_s = next(rest)
        self.sem_gx_r = next(rest)
        self.sem_gz_s = next(rest)
        self.sem_gz_r = next(rest)
        self.sem_gs_s = next(rest)
        self.sem_gs_r = next(rest)
        self.sem_in_s = next(rest)
        self.sem_in_r = next(rest)
        self.sem_ag_s = next(rest)
        self.sem_ag_r = next(rest)
        self.sem_rs_s = next(rest)
        self.sem_rs_r = next(rest)
        self.sem_m_s = next(rest)
        self.sem_m_r = next(rest)
        self.sem_d_s = next(rest)
        self.sem_d_r = next(rest)
        self.sem_t_s = next(rest)
        self.sem_t_r = next(rest)
        self.sem_out = next(rest)


def whole_layer(z, *refs):
    r = Refs(refs)
    W, FIRST, SECOND, GOUT = r.weights, r.firsts, r.seconds, r.gout
    n, S, B = z.chunks, z.seq, z.batch
    part, rows, D, C = z.part, z.rows, z.width, z.columns
    Z = B // 2
    b = lax.axis_index("batch")
    s = lax.axis_index("seq")
    zz = b // 2
    x = lax.rem(b, 2)
    y = s // 2
    c = lax.rem(s, 2)
    other_x = 1 - x
    other_c = 1 - c
    other_y = 1 - y
    x_peer = (2 * zz + other_x, s)
    core_peer = (b, 2 * y + other_c)
    line_peer = (b, 2 * other_y + c)
    line_slot = 2 * other_y + c
    core_slot = 2 * y + other_c
    far_slot = 2 * other_y + other_c

    def z_of(j):
        return lax.rem(zz + j, Z)

    def remote(src, dst, send, recv, device):
        return pltpu.make_async_remote_copy(
            src_ref=src,
            dst_ref=dst,
            send_sem=send,
            recv_sem=recv,
            device_id=device,
            device_id_type=MESH,
        )

    def arrived(dst, send, recv, device):
        remote(dst, dst, send, recv, device).wait_recv()

    barrier = pltpu.get_barrier_semaphore()
    for j in range(1, B):
        pl.semaphore_signal(barrier, inc=1, device_id=(lax.rem(b + j, B), s), device_id_type=MESH)
    for j in range(1, S):
        pl.semaphore_signal(barrier, inc=1, device_id=(b, lax.rem(s + j, S)), device_id_type=MESH)

    loads = {}

    def load(key, src, dst, when=None):
        count = sum(len(copies) for copies in loads.values())
        copy = pltpu.make_async_copy(src, dst, r.sem_load.at[count])
        loads.setdefault(key, []).append(copy)
        if when is None:
            copy.start()
        else:
            pl.when(when)(copy.start)

    def col(index, width):
        return pl.ds(pl.multiple_of(index * width, 128), width)

    load(CAMERA, r.camera, r.camera_own)
    for k in range(6):
        load(
            TABLE,
            r.modulation.at[:, pl.ds(k * D, D)],
            r.hidden.at[pl.ds(k * z.block, z.block)],
        )
    for j in range(2):
        load(
            KV,
            r.kv_image.at[:, pl.ds(pl.multiple_of(j * D + s * C, 128), C)],
            W[KV].at[b, :, pl.ds(j * C, C)],
        )
    load(TOKENS, r.tokens, r.buf_a.at[:, s])
    load(Q, r.q_cross.at[:, col(s, C)], W[Q].at[b])
    load(IMAGE, r.image.at[pl.ds(0, z.whole_rows)], r.image_all.at[pl.ds(0, z.whole_rows)])
    load(IMAGE, r.tail, r.image_all.at[pl.ds(z.whole_rows, z.keys - z.whole_rows)])
    load(IMAGE, r.mask, r.mask_all)
    load(OWN, r.tokens, r.x0)
    load(OC, r.out_cross, W[OC].at[x], zz == s)
    for j in range(3):
        load(
            QKV,
            r.qkv_self.at[:, pl.ds(pl.multiple_of(j * D + s * C, 128), C)],
            W[QKV].at[b, :, pl.ds(j * C, C)],
        )
    load(OS, r.out_self, W[OS].at[x], zz == s)
    wide = z.hidden // B
    for j in range(B):
        load(
            UP,
            r.mlp_in.at[:, pl.ds(pl.multiple_of(j * (z.hidden * S // B) + s * wide, 128), wide)],
            W[UP].at[b, :, pl.ds(j * wide, wide)],
        )
    load(DOWN, r.mlp_out.at[pl.ds(pl.multiple_of(s * wide, 128), wide), :], W[DOWN].at[b])
    load(COTANGENT, r.cotangent, r.buf_b.at[:, s])

    pl.semaphore_wait(barrier, B - 1 + S - 1)

    by_rows = (OC, OS)
    def loaded(key):
        for copy in loads[key]:
            copy.wait()

    def z_send(w, j):
        slot = x if w in by_rows else b
        mark = 0 if w in by_rows else zz
        return remote(
            W[w].at[slot],
            W[w].at[slot],
            r.sem_wz_s.at[w, j - 1],
            r.sem_wz_r.at[w, mark],
            (2 * z_of(j) + x, s),
        )

    def x_send(w, from_z):
        slot = x if w in by_rows else 2 * from_z + x
        mark = 0 if w in by_rows else from_z
        return remote(
            W[w].at[slot],
            W[w].at[slot],
            r.sem_wx_s.at[w, mark],
            r.sem_wx_r.at[w, mark],
            x_peer,
        )

    def weight_start(w):
        def go():
            loaded(w)
            for j in range(1, Z):
                z_send(w, j).start()
            x_send(w, zz).start()

        if w in by_rows:
            pl.when(zz == s)(go)
        else:
            go()

    def weight_pass(w):
        if w in by_rows:

            @pl.when(zz != s)
            def _():
                arrived(
                    W[w].at[x], r.sem_wz_s.at[w, 0], r.sem_wz_r.at[w, 0], (2 * s + x, s)
                )
                x_send(w, zz).start()

        else:
            for j in range(1, Z):
                from_z = z_of(j)
                arrived(
                    W[w].at[2 * from_z + x],
                    r.sem_wz_s.at[w, 0],
                    r.sem_wz_r.at[w, from_z],
                    (2 * from_z + x, s),
                )
                x_send(w, from_z).start()

    def weight_wait(w):
        for from_z in [0] if w in by_rows else range(Z):
            slot = other_x if w in by_rows else 2 * from_z + other_x
            arrived(W[w].at[slot], r.sem_wx_s.at[w, 0], r.sem_wx_r.at[w, from_z], x_peer)

    def weight_drain(w):
        if w in by_rows:

            @pl.when(zz == s)
            def _():
                for j in range(1, Z):
                    z_send(w, j).wait_send()

            x_send(w, zz).wait_send()
        else:
            for j in range(1, Z):
                z_send(w, j).wait_send()
            for j in range(Z):
                x_send(w, z_of(j)).wait_send()

    def give(buf, i, k):
        slot, peer = [(s, core_peer), (s, line_peer), (line_slot, core_peer)][k]
        return remote(
            buf.at[i, slot], buf.at[i, slot], r.sem_ag_s.at[i, k], r.sem_ag_r.at[i, k], peer
        )

    def gather_start(buf, i):
        give(buf, i, 1).start()
        give(buf, i, 0).start()

    def gather_pass(buf, i):
        arrived(buf.at[i, line_slot], r.sem_ag_s.at[i, 1], r.sem_ag_r.at[i, 1], line_peer)
        give(buf, i, 2).start()

    def gather_wait(buf, i):
        arrived(buf.at[i, core_slot], r.sem_ag_s.at[i, 0], r.sem_ag_r.at[i, 0], core_peer)
        arrived(buf.at[i, far_slot], r.sem_ag_s.at[i, 2], r.sem_ag_r.at[i, 2], core_peer)
        for k in range(3):
            give(buf, i, k).wait_send()

    def give_input(buf, m, k):
        slot, peer = [(s, core_peer), (s, line_peer), (line_slot, core_peer)][k]
        return remote(
            buf.at[:, slot], buf.at[:, slot], r.sem_in_s.at[m, k], r.sem_in_r.at[m, k], peer
        )

    def input_start(buf, m):
        give_input(buf, m, 1).start()
        give_input(buf, m, 0).start()

    def input_pass(buf, m):
        arrived(buf.at[:, line_slot], r.sem_in_s.at[m, 1], r.sem_in_r.at[m, 1], line_peer)
        give_input(buf, m, 2).start()

    def input_wait(buf, m):
        arrived(buf.at[:, core_slot], r.sem_in_s.at[m, 0], r.sem_in_r.at[m, 0], core_peer)
        arrived(buf.at[:, far_slot], r.sem_in_s.at[m, 2], r.sem_in_r.at[m, 2], core_peer)
        for k in range(3):
            give_input(buf, m, k).wait_send()

    lanes = (
        (r.part_main, r.core_main, r.send_main, r.line_main),
        (r.part_side, r.core_side, r.send_side, r.line_side),
    )

    def sum_core(lane, i):
        mine, core, _, _ = lanes[lane]
        return remote(
            mine.at[i, :, other_c],
            core.at[i],
            r.sem_rs_s.at[lane, i, 0],
            r.sem_rs_r.at[lane, i, 0],
            core_peer,
        )

    def sum_line(lane, i):
        _, _, send, line = lanes[lane]
        return remote(
            send.at[i],
            line.at[i],
            r.sem_rs_s.at[lane, i, 1],
            r.sem_rs_r.at[lane, i, 1],
            line_peer,
        )

    def sum_start(lane, i, value):
        lanes[lane][0][i] = value.astype(bf16).reshape(2, 2, part, D)
        sum_core(lane, i).start()

    def sum_pass(lane, i):
        mine, core, send, _ = lanes[lane]
        sum_core(lane, i).wait_recv()
        send[i] = (mine[i, other_y, c].astype(f32) + core[i, other_y].astype(f32)).astype(bf16)
        sum_line(lane, i).start()

    def sum_end(lane, i):
        mine, core, _, line = lanes[lane]
        sum_line(lane, i).wait_recv()
        total = mine[i, y, c].astype(f32) + core[i, y].astype(f32) + line[i].astype(f32)
        sum_core(lane, i).wait_send()
        sum_line(lane, i).wait_send()
        return total

    def grad_place(w):
        return {
            Q: r.grads_b.at[:, :, :, pl.ds(0, C)],
            KV: r.grads_b.at[:, :, pl.ds(0, z.image_block), pl.ds(C, 2 * C)],
            OC: r.grads_c.at[0],
            QKV: r.grads_a.at[:, :, :, pl.ds(0, 3 * C)],
            OS: r.grads_c.at[1],
            UP: r.grads_a,
            DOWN: r.grads_b,
        }[w]

    def grad_x(w):
        place = grad_place(w)
        src = place.at[other_x] if w in by_rows else place.at[:, other_x]
        return remote(src, FIRST[w], r.sem_gx_s.at[w], r.sem_gx_r.at[w], x_peer)

    def grad_z(w, j):
        if w in by_rows:
            return remote(
                FIRST[w],
                SECOND[w].at[lax.rem(zz - s + Z, Z) - 1],
                r.sem_gz_s.at[w, 0],
                r.sem_gz_r.at[w, zz],
                (2 * s + x, s),
            )
        return remote(
            FIRST[w].at[z_of(j)],
            SECOND[w].at[Z - j - 1],
            r.sem_gz_s.at[w, j - 1],
            r.sem_gz_r.at[w, zz],
            (2 * z_of(j) + x, s),
        )

    def grad_s(w, j):
        src = FIRST[w] if w in by_rows else FIRST[w].at[zz]
        dst = GOUT[w] if w in by_rows else GOUT[w].at[s]
        mark = 0 if w in by_rows else s
        return remote(
            src,
            dst,
            r.sem_gs_s.at[w, j - 1],
            r.sem_gs_r.at[w, mark],
            (b, lax.rem(s + j, S)),
        )

    def grad_own(w):
        src = FIRST[w] if w in by_rows else FIRST[w].at[zz]
        dst = GOUT[w] if w in by_rows else GOUT[w].at[s]
        return pltpu.make_async_copy(src, dst, r.sem_out.at[w])

    def grad_start(w):
        grad_x(w).start()

    def grad_pass(w):
        grad_x(w).wait_recv()
        place = grad_place(w)
        if w in by_rows:
            FIRST[w][...] = (FIRST[w][...].astype(f32) + place[x].astype(f32)).astype(bf16)

            @pl.when(zz != s)
            def _():
                grad_z(w, 0).start()

        else:
            for k in range(Z):
                FIRST[w][k] = (FIRST[w][k].astype(f32) + place[k, x].astype(f32)).astype(bf16)
            for j in range(1, Z):
                grad_z(w, j).start()
        grad_x(w).wait_send()

    def grad_end(w):
        if w in by_rows:

            @pl.when(zz == s)
            def _():
                total = FIRST[w][...].astype(f32)
                for j in range(1, Z):
                    k = z_of(j)
                    arrived(SECOND[w].at[j - 1], r.sem_gz_s.at[w, 0], r.sem_gz_r.at[w, k], (2 * k + x, s))
                    total = total + SECOND[w][j - 1].astype(f32)
                FIRST[w][...] = total.astype(bf16)
                for j in range(1, S):
                    grad_s(w, j).start()
                grad_own(w).start()

            @pl.when(zz != s)
            def _():
                grad_z(w, 0).wait_send()

        else:
            total = FIRST[w][zz].astype(f32)
            for j in range(1, Z):
                k = z_of(j)
                arrived(SECOND[w].at[j - 1], r.sem_gz_s.at[w, 0], r.sem_gz_r.at[w, k], (2 * k + x, s))
                total = total + SECOND[w][j - 1].astype(f32)
            for j in range(1, Z):
                grad_z(w, j).wait_send()
            FIRST[w][zz] = total.astype(bf16)
            for j in range(1, S):
                grad_s(w, j).start()
            grad_own(w).start()

    def grad_drain(w):
        if w in by_rows:

            @pl.when(zz == s)
            def _():
                for j in range(1, S):
                    grad_s(w, j).wait_send()
                grad_own(w).wait()

            @pl.when(zz != s)
            def _():
                arrived(GOUT[w], r.sem_gs_s.at[w, 0], r.sem_gs_r.at[w, 0], (b, zz))

        else:
            for j in range(1, S):
                k = lax.rem(s + j, S)
                arrived(GOUT[w].at[k], r.sem_gs_s.at[w, 0], r.sem_gs_r.at[w, k], (b, k))
            for j in range(1, S):
                grad_s(w, j).wait_send()
            grad_own(w).wait()

    def mods_send(j):
        to = lax.rem(b + j, B)
        return remote(
            r.x2.at[0, pl.ds(pl.multiple_of(8 * to, 8), 8)],
            r.mods_all.at[b],
            r.sem_m_s.at[j - 1],
            r.sem_m_r.at[b],
            (to, s),
        )

    loaded(CAMERA)
    loaded(TABLE)
    camera = r.camera_own[...].astype(f32)
    gate = (camera * jax.nn.sigmoid(camera)).astype(bf16)
    for k in range(6):
        term = nn(gate, r.hidden[k * z.block : (k + 1) * z.block, :])
        for o in range(B):
            r.x2[0, 8 * o + k : 8 * o + k + 1, :] = term[o : o + 1, :]
    weight_start(KV)
    loaded(TOKENS)
    input_start(r.buf_a, 0)
    for j in range(1, B):
        mods_send(j).start()
    weight_start(Q)
    loaded(COTANGENT)
    input_start(r.buf_b, 1)
    weight_start(OC)
    weight_start(QKV)
    loaded(IMAGE)
    loaded(OWN)

    mods = r.x2[0, pl.ds(pl.multiple_of(8 * b, 8), 8)]
    for j in range(1, B):
        k = lax.rem(b + j, B)
        arrived(r.mods_all.at[k], r.sem_m_s.at[0], r.sem_m_r.at[k], (k, s))
        mods = mods + r.mods_all[k]
    r.mods[...] = mods
    for j in range(1, B):
        mods_send(j).wait_send()

    def mod(k):
        return r.mods[k : k + 1, :]

    weight_pass(KV)
    input_pass(r.buf_a, 0)
    weight_pass(Q)
    weight_wait(KV)
    scale_q = HEAD_DIM ** (-0.5)
    step = z.keys // 3 if z.keys % 48 == 0 else z.keys

    def project_image(k, _):
        part_rows = pl.ds(pl.multiple_of(k * step, 16), step)
        both = nn(r.image_all[part_rows, :], W[KV][...].reshape(z.image_width, 2 * C))
        r.key1[part_rows, :] = both[:, :C].astype(bf16)
        r.value1[part_rows, :] = both[:, C:].astype(bf16)
        return 0

    lax.fori_loop(0, z.keys // step, project_image, 0)
    input_wait(r.buf_a, 0)
    weight_wait(Q)

    def chunk(i):
        return pl.ds(pl.multiple_of(i * rows, rows), rows)

    def project_query(i):
        rows_in = r.buf_a[i].reshape(rows, D).astype(f32)
        normed = norm_forward(rows_in, mod(0), mod(1)).astype(bf16)
        r.normed1[chunk(i), :] = normed
        query = nn(normed, W[Q][...].reshape(D, C)).astype(bf16)
        r.query1[chunk(i), :] = (query * scale_q).astype(bf16)

    def attend(i, query, key, value, att, mask):
        for p in range(C // 128):
            lane = slice(128 * p, 128 * p + 128)
            pair = query(i, lane)
            keys, values = key(lane), value(lane)
            result = []
            for side in range(2):
                probs = softmax_rows(nt(one_head(pair, side), keys), mask).astype(bf16)
                result.append(nn(probs, values))
            att[chunk(i), lane] = two_heads(*result).astype(bf16)

    def attend_back(i, query, key, value, grad, mask, grad_query):
        query_t = query(i, slice(0, C)).T
        grad_t = grad.T
        for p in range(C // 128):
            lane = slice(128 * p, 128 * p + 128)
            pair, grad_pair = query(i, lane), grad[:, lane]
            keys, values = key(lane), value(lane)
            result = []
            for side in range(2):
                head = slice(128 * p + HEAD_DIM * side, 128 * p + HEAD_DIM * (side + 1))
                probs = softmax_rows(nt(one_head(pair, side), keys), mask)
                grad_probs = nt(one_head(grad_pair, side), values)
                inner = jnp.sum(probs * grad_probs, axis=-1, keepdims=True)
                scores = (probs * (grad_probs - inner)).astype(bf16)
                count = keys.shape[0]
                value_term = nn(grad_t[head, :], probs.astype(bf16))
                key_term = nn(query_t[head, :], scores)
                r.grad_value[head, :count] += value_term
                r.grad_key[head, :count] += key_term
                result.append(nn(scores, keys))
            grad_query[chunk(i), lane] = (two_heads(*result) * scale_q).astype(bf16)

    cross = (
        lambda i, lane: r.query1[chunk(i), lane],
        lambda lane: r.key1[:, lane],
        lambda lane: r.value1[:, lane],
    )

    def plus(lane, offset):
        return slice(lane.start + offset, lane.stop + offset)

    own = (
        lambda i, lane: r.packed2[chunk(i), lane],
        lambda lane: r.packed2[:, plus(lane, C)],
        lambda lane: r.packed2[:, plus(lane, 2 * C)],
    )
    mask_rows = r.mask_all

    def pipeline(*stages):
        last = max(offset for offset, _ in stages)

        def body(step, _):
            for offset, stage in stages:
                i = step - offset

                @pl.when((i >= 0) & (i < n))
                def _():
                    stage(i)

            return 0

        lax.fori_loop(0, n + last, body, 0)

    def at(i, value, stage):
        pl.when(i == value)(stage)

    def weights_on(*steps):
        def run():
            for step, w in steps:
                step(w)

        return run

    def cross_forward(i):
        project_query(i)
        attend(i, *cross, r.att1, mask_rows)
        at(i, 0, weights_on((weight_start, OS), (weight_pass, OC), (weight_wait, OC)))
        at(i, 1, weights_on((weight_start, UP)))
        at(i, 2, weights_on((weight_pass, QKV), (weight_start, DOWN)))
        at(i, 3, weights_on((weight_pass, OS)))
        sum_start(0, i, nn(r.att1[chunk(i), :], W[OC][...].reshape(C, D)))

    def after_cross(i):
        total = r.x0[i].astype(f32) + sum_end(0, i)
        r.x1[i] = total
        r.buf_h2[i, s] = norm_forward(total, mod(2), mod(3)).astype(bf16)
        gather_start(r.buf_h2, i)

    def project_self(i):
        at(i, 0, weights_on((weight_wait, QKV)))
        gather_wait(r.buf_h2, i)
        packed = nn(r.buf_h2[i].reshape(rows, D), W[QKV][...].reshape(D, 3 * C)).astype(bf16)
        r.packed2[chunk(i), :C] = (packed[:, :C] * scale_q).astype(bf16)
        r.packed2[chunk(i), C:] = packed[:, C:]

    pipeline(
        (0, cross_forward),
        (1, lambda i: sum_pass(0, i)),
        (2, after_cross),
        (3, lambda i: gather_pass(r.buf_h2, i)),
        (4, project_self),
    )

    weight_wait(OS)
    input_pass(r.buf_b, 1)
    input_wait(r.buf_b, 1)
    r.sums[...] = jnp.zeros_like(r.sums)

    def clear_keys():
        r.grad_key[...] = jnp.zeros_like(r.grad_key)
        r.grad_value[...] = jnp.zeros_like(r.grad_value)

    clear_keys()

    def output_copy(i):
        return pltpu.make_async_copy(
            r.part_side.at[i, 0, 0], r.output.at[i], r.sem_out.at[9 + i]
        )

    def self_forward(i):
        attend(i, *own, r.att2, None)
        at(i, 0, weights_on((weight_pass, UP)))
        at(i, 2, weights_on((weight_pass, DOWN)))
        sum_start(0, i, nn(r.att2[chunk(i), :], W[OS][...].reshape(C, D)))

    def after_self(i):
        total = r.x1[i] + sum_end(0, i)
        r.x2[i] = total
        r.buf_a[i, s] = norm_forward(total, mod(4), mod(5)).astype(bf16)
        gather_start(r.buf_a, i)

    def feed(i):
        at(i, 0, weights_on((weight_wait, UP), (weight_wait, DOWN)))
        gather_wait(r.buf_a, i)
        rows_in = r.buf_a[i].reshape(rows, D)
        grad_out = r.buf_b[i].reshape(rows, D)
        up = W[UP]
        down = W[DOWN]
        forward = backward = None
        pieces = 2
        wide_piece = z.hidden // pieces
        for k in range(pieces):
            lane = slice(k * wide_piece, (k + 1) * wide_piece)
            up_piece = up[:, :, lane].reshape(D, wide_piece)
            down_piece = down[k * (B // pieces) : (k + 1) * (B // pieces)].reshape(wide_piece, D)
            u = nn(rows_in, up_piece)
            square = u * u
            root = 0.7978845608028654
            tanh = jnp.tanh(root * u * (1.0 + 0.044715 * square))
            half = 0.5 * (1.0 + tanh)
            hidden = (u * half).astype(bf16)
            slope = half + 0.5 * u * (1.0 - tanh * tanh) * (root * (1.0 + 0.134145 * square))
            grad_up = (nt(grad_out, down_piece) * slope).astype(bf16)
            r.hidden[chunk(i), lane] = hidden
            r.grad_up[chunk(i), lane] = grad_up
            first = nn(hidden, down_piece)
            second = nt(grad_up, up_piece)
            forward = first if forward is None else forward + first
            backward = second if backward is None else backward + second
        sum_start(0, i, backward)
        sum_start(1, i, forward)

    def keep_sums(k, shift, scale):
        r.sums[k : k + 1, :] += shift
        r.sums[k + 1 : k + 2, :] += scale

    def after_feed(i):
        stream = r.x2[i]
        grad, shift, scale = norm_backward(stream, mod(5), sum_end(0, i))
        keep_sums(4, shift, scale)
        grad = r.buf_b[i, s].astype(f32) + grad
        r.buf_b2[i, s] = grad.astype(bf16)
        gather_start(r.buf_b2, i)
        r.part_side[i, 0, 0] = (r.x2[i] + sum_end(1, i)).astype(bf16)
        r.x2[i] = grad
        output_copy(i).start()

    def self_back(i):
        gather_wait(r.buf_b2, i)
        grad = nt(r.buf_b2[i].reshape(rows, D), W[OS][...].reshape(C, D)).astype(bf16)
        attend_back(i, *own, grad, None, r.grad_up)

    def grads_into(place, lhs, rhs, block, width):
        pieces = 4
        count = lhs.shape[1] // pieces
        for k in range(pieces):
            value = tn(lhs[:, k * count : (k + 1) * count], rhs).astype(bf16)
            lead = count // block
            for m in range(lead):
                o = k * lead + m
                place[o // 2, o % 2, :, :width] = value[m * block : (m + 1) * block]

    def feed_grads():
        grads_into(
            r.grads_b,
            r.hidden,
            r.buf_b[...].reshape(z.tokens, D),
            z.block,
            D,
        )
        grad_start(DOWN)
        grads_into_blocks(r.grads_a, r.buf_a, r.grad_up, z.hidden)
        grad_start(UP)

    def grads_into_blocks(place, lhs4, rhs, width):
        for o in range(B):
            left = lhs4[:, :, :, o * z.block : (o + 1) * z.block].reshape(z.tokens, z.block)
            place[o // 2, o % 2, :, :width] = tn(left, rhs[:, :width]).astype(bf16)

    pipeline(
        (0, self_forward),
        (1, lambda i: sum_pass(0, i)),
        (2, after_self),
        (3, lambda i: gather_pass(r.buf_a, i)),
        (4, feed),
        (4, lambda i: at(i, n - 1, feed_grads)),
        (5, lambda i: (sum_pass(0, i), sum_pass(1, i))),
        (6, after_feed),
        (7, lambda i: gather_pass(r.buf_b2, i)),
        (8, self_back),
    )
    grad_pass(DOWN)
    grad_pass(UP)

    r.grad_up[:, C : 2 * C] = r.grad_key[:, : z.tokens].T.astype(bf16)
    r.grad_up[:, 2 * C : 3 * C] = r.grad_value[:, : z.tokens].T.astype(bf16)

    clear_keys()

    def self_down(i):
        sum_start(0, i, nt(r.grad_up[chunk(i), : 3 * C], W[QKV][...].reshape(D, 3 * C)))

        @functools.partial(at, i, 0)
        def _():
            value = tn(r.att2[...], r.buf_b2[...].reshape(z.tokens, D)).astype(bf16)
            r.grads_c[1] = value.reshape(2, z.block, D)
            grad_start(OS)

        @functools.partial(at, i, n - 1)
        def _():
            grads_into_blocks(r.grads_a, r.buf_h2, r.grad_up, 3 * C)
            grad_start(QKV)

    def after_self_down(i):
        grad, shift, scale = norm_backward(r.x1[i], mod(3), sum_end(0, i))
        keep_sums(2, shift, scale)
        grad = r.x2[i] + grad
        r.x2[i] = grad
        r.buf_b[i, s] = grad.astype(bf16)
        gather_start(r.buf_b, i)

    def cross_back(i):
        gather_wait(r.buf_b, i)
        grad = nt(r.buf_b[i].reshape(rows, D), W[OC][...].reshape(C, D)).astype(bf16)
        attend_back(i, *cross, grad, mask_rows, r.hidden)
        sum_start(0, i, nt(r.hidden[chunk(i), :C], W[Q][...].reshape(D, C)))
        at(i, 0, weights_on((grad_pass, OS), (grad_end, DOWN)))
        at(i, 1, weights_on((grad_end, UP)))
        at(i, 2, weights_on((grad_pass, QKV)))

    def after_cross_back(i):
        grad, shift, scale = norm_backward(r.x0[i].astype(f32), mod(1), sum_end(0, i))
        keep_sums(0, shift, scale)
        r.x2[i] += grad

    def last_grads():
        value = tn(r.att1[...], r.buf_b[...].reshape(z.tokens, D)).astype(bf16)
        r.grads_c[0] = value.reshape(2, z.block, D)
        grad_start(OC)
        for side, rest in enumerate((r.grad_key[...], r.grad_value[...])):
            total = None
            for _ in range(3):
                term = rest.astype(bf16)
                rest = rest - term.astype(f32)
                product_term = nn(term, r.image_all[...])
                total = product_term if total is None else total + product_term
            value = total.T.astype(bf16)
            for o in range(B):
                r.grads_b[o // 2, o % 2, : z.image_block, C + side * C : C + (side + 1) * C] = value[
                    o * z.image_block : (o + 1) * z.image_block
                ]
        grad_start(KV)
        for o in range(B):
            left = r.normed1[:, o * z.block : (o + 1) * z.block]
            r.grads_b[o // 2, o % 2, :, :C] = tn(left, r.hidden[:, :C]).astype(bf16)
        grad_start(Q)

    pipeline(
        (0, self_down),
        (1, lambda i: sum_pass(0, i)),
        (2, after_self_down),
        (3, lambda i: gather_pass(r.buf_b, i)),
        (4, cross_back),
        (4, lambda i: at(i, n - 1, last_grads)),
        (5, lambda i: sum_pass(0, i)),
        (6, after_cross_back),
    )
    grad_copy = pltpu.make_async_copy(r.x2, r.grad_tokens, r.sem_out.at[7])
    grad_copy.start()

    def sums_send(j):
        return remote(
            r.sums, r.sums_seq.at[s], r.sem_d_s.at[j - 1], r.sem_d_r.at[s], (b, lax.rem(s + j, S))
        )

    for j in range(1, S):
        sums_send(j).start()
    grad_pass(OC)
    grad_end(OS)
    grad_end(QKV)
    total = r.sums[...]
    for j in range(1, S):
        k = lax.rem(s + j, S)
        arrived(r.sums_seq.at[k], r.sem_d_s.at[0], r.sem_d_r.at[k], (b, k))
        total = total + r.sums_seq[k]
    r.mods_all[b] = total

    def table_send(j):
        return remote(
            r.mods_all.at[b],
            r.mods_all.at[b],
            r.sem_t_s.at[j - 1],
            r.sem_t_r.at[b],
            (lax.rem(b + j, B), s),
        )

    for j in range(1, B):
        table_send(j).start()
    grad_pass(KV)
    grad_pass(Q)
    for j in range(1, B):
        k = lax.rem(b + j, B)
        arrived(r.mods_all.at[k], r.sem_t_s.at[0], r.sem_t_r.at[k], (k, s))
    table_copy = pltpu.make_async_copy(r.mods_all, r.table, r.sem_out.at[8])
    table_copy.start()
    grad_end(OC)
    grad_end(KV)
    grad_end(Q)
    for j in range(1, S):
        sums_send(j).wait_send()
    for j in range(1, B):
        table_send(j).wait_send()
    for w in range(7):
        weight_drain(w)
    for w in (DOWN, UP, OS, QKV, OC, KV, Q):
        grad_drain(w)
    for i in range(n):
        output_copy(i).wait()
    grad_copy.wait()
    table_copy.wait()


def layer_call(z, args):
    n, part, D, C, S, B = z.chunks, z.part, z.width, z.columns, z.seq, z.batch
    Z = B // 2
    own = (n, part, D)
    full = (n, S, part, D)
    vmem = pltpu.VMEM
    dma = pltpu.SemaphoreType.DMA
    by_rows = (OC, OS)
    weights = [
        vmem(((2,) if w in by_rows else (B,)) + shape, bf16) for w, shape in enumerate(z.weights)
    ]
    firsts = [
        vmem((() if w in by_rows else (Z,)) + shape, bf16) for w, shape in enumerate(z.weights)
    ]
    seconds = [vmem((Z - 1,) + shape, bf16) for shape in z.weights]
    lane = [
        vmem((n, 2, 2, part, D), bf16),
        vmem((n, 2, part, D), bf16),
        vmem((n, part, D), bf16),
        vmem((n, part, D), bf16),
    ]
    scratch = (
        weights
        + firsts
        + seconds
        + [vmem(full, bf16)] * 4
        + lane
        + lane
        + [
            vmem((z.keys, z.image_width), bf16),
            vmem((8, z.keys), f32),
            vmem(args[5].shape, bf16),
            vmem((B, 8, D), f32),
            vmem((8, D), f32),
            vmem((8, D), f32),
            vmem((S, 8, D), f32),
            vmem((z.tokens, D), bf16),
            vmem((z.tokens, C), bf16),
            vmem((z.keys, C), bf16),
            vmem((z.keys, C), bf16),
            vmem((z.tokens, C), bf16),
            vmem((z.tokens, 3 * C), bf16),
            vmem((z.tokens, C), bf16),
            vmem((z.tokens, z.hidden), bf16),
            vmem((z.tokens, z.hidden), bf16),
            vmem((C, z.keys), f32),
            vmem((C, z.keys), f32),
            vmem(own, bf16),
            vmem(own, f32),
            vmem(own, f32),
            vmem((Z, 2, z.block, D), bf16),
            vmem((Z, 2, z.block, D), bf16),
            vmem((2, 2, z.block, D), bf16),
            dma((33,)),
            dma((7, 3)),
            dma((7, Z)),
            dma((7, Z)),
            dma((7, Z)),
            dma((7,)),
            dma((7,)),
            dma((7, 3)),
            dma((7, Z)),
            dma((7, 3)),
            dma((7, S)),
            dma((2, 3)),
            dma((2, 3)),
            dma((n, 3)),
            dma((n, 3)),
            dma((2, n, 2)),
            dma((2, n, 2)),
            dma((B - 1,)),
            dma((B,)),
            dma((S - 1,)),
            dma((S,)),
            dma((B - 1,)),
            dma((B,)),
            dma((9 + n,)),
        ]
    )
    shape = jax.ShapeDtypeStruct
    outs = [shape(own, bf16), shape(own, f32), shape((B, 8, D), f32)] + [
        shape((() if w in by_rows else (S,)) + size, bf16) for w, size in enumerate(z.weights)
    ]
    anywhere = pl.BlockSpec(memory_space=pl.ANY)
    return pl.pallas_call(
        functools.partial(whole_layer, z),
        out_shape=outs,
        in_specs=[anywhere] * len(args),
        out_specs=[anywhere] * len(outs),
        scratch_shapes=scratch,
        compiler_params=pltpu.CompilerParams(
            collective_id=0, has_side_effects=True, vmem_limit_bytes=LIMIT
        ),
        name="whole_layer",
    )(*args)


def local_kernel(sizes, *inputs):
    (
        tokens,
        cotangent,
        image_tokens,
        image_lengths,
        key_mask,
        camera,
        modulation,
        q_cross,
        kv_image,
        out_cross,
        qkv_self,
        out_self,
        mlp_in,
        mlp_out,
    ) = inputs
    z = sizes
    n, part, D, C, S, B = z.chunks, z.part, z.width, z.columns, z.seq, z.batch
    positions = jnp.arange(z.keys, dtype=jnp.int32)
    marked = jnp.pad(key_mask[0], (0, z.keys - z.image_rows)) == 1
    valid = (positions < image_lengths[0]) & (marked | (positions == 0))
    fill = jnp.where(positions < z.image_rows, -1000000000.0, BELOW)
    mask = jnp.concatenate(
        [valid.astype(f32)[None], fill[None], jnp.zeros((6, z.keys), f32)], axis=0
    )
    tail = jnp.pad(
        image_tokens[0, z.whole_rows :], ((0, z.keys - z.image_rows), (0, 0))
    )
    results = layer_call(
        z,
        (
            tokens[0].reshape(n, part, D),
            cotangent[0].reshape(n, part, D),
            image_tokens[0],
            tail,
            mask,
            camera,
            modulation,
            q_cross,
            kv_image,
            out_cross,
            qkv_self,
            out_self,
            mlp_in,
            mlp_out,
        ),
    )
    output, grad_tokens, table, *grads = results
    gate = jax.nn.silu(camera.astype(f32)).astype(bf16).astype(f32)
    grad_modulation = lax.dot_general(
        gate,
        table[:, :6, :].reshape(B, 6 * D),
        (((0,), (0,)), ((), ())),
        precision=highest,
        preferred_element_type=f32,
    )

    def across(grad, groups):
        rows, width = grad.shape[1:]
        split = grad.reshape(S, rows, groups, width // groups).transpose(1, 2, 0, 3)
        return split.reshape(rows, S * width).astype(f32)

    return (
        output.reshape(1, z.own, D),
        grad_tokens.reshape(1, z.own, D),
        grad_modulation,
        across(grads[Q], 1),
        across(grads[KV], 2),
        grads[OC].astype(f32),
        across(grads[QKV], 3),
        grads[OS].astype(f32),
        across(grads[UP], B),
        grads[DOWN].reshape(-1, D).astype(f32),
    )


def fits(mesh, inputs):
    batch, seq = mesh.shape["batch"], mesh.shape["seq"]
    own, width = inputs[0].shape[1:]
    return (
        batch == 8
        and seq == 4
        and own % 64 == 0
        and width == HEADS * HEAD_DIM
        and (width // seq) % 128 == 0
        and (inputs[12].shape[1] // seq // batch) % 128 == 0
    )


def choose(mesh, *inputs):
    if not fits(mesh, inputs):
        return local(*inputs)
    return local_kernel(Sizes(mesh.shape, inputs), *inputs)


def solution(mesh):
    return jax.shard_map(
        functools.partial(choose, mesh),
        mesh=mesh,
        in_specs=(
            P("batch", "seq", None),
            P("batch", "seq", None),
            P("batch", None, None),
            P("batch"),
            P("batch", None),
            P(None, "batch"),
            P("batch", None),
            P("batch", None),
            P("batch", None),
            P("batch", None),
            P("batch", None),
            P("batch", None),
            P("batch", None),
            P("batch", None),
        ),
        out_specs=(
            P("batch", "seq", None),
            P("batch", "seq", None),
            P("batch", None),
            P("batch", None),
            P("batch", None),
            P("batch", None),
            P("batch", None),
            P("batch", None),
            P("batch", None),
            P("batch", None),
        ),
        check_vma=False,
    )
```

```python
import functools

import jax
import jax.numpy as jnp
from jax import lax
from jax.experimental import pallas as pl
from jax.experimental.pallas import tpu as pltpu
from jax.sharding import PartitionSpec as P

HEADS = 16
HEAD_DIM = 64


epsilon = 1e-06
group_heads = 4
highest = lax.Precision.HIGHEST
LIMIT = 64 * 1024 * 1024 - 64 * 1024


def modulated_norm(values, shift, scale):
    center = values - jnp.mean(values, axis=-1, keepdims=True)
    normed = center * lax.rsqrt(jnp.mean(center * center, axis=-1, keepdims=True) + epsilon)
    return normed * (1.0 + scale) + shift


def product(left, right):
    return jnp.dot(left, right, preferred_element_type=jnp.float32)


def contract_rows(left, right):
    return lax.dot_general(
        left, right, (((0,), (0,)), ((), ())), preferred_element_type=jnp.float32
    )


def times_transposed(left, right):
    return lax.dot_general(
        left, right, (((1,), (1,)), ((), ())), preferred_element_type=jnp.float32
    )


def split_heads(values):
    rows = values.shape[0]
    grouped = values.reshape(rows, HEADS // group_heads, group_heads, HEAD_DIM)
    return grouped.transpose(1, 2, 0, 3)


def join_heads(values):
    groups, inner, rows, depth = values.shape
    return values.transpose(2, 0, 1, 3).reshape(rows, groups * inner * depth)


def scores_of(query_group, key_group, valid):
    scores = jnp.einsum(
        "hqd,hkd->hqk", query_group, key_group, preferred_element_type=jnp.float32
    ) * HEAD_DIM ** (-0.5)
    return jnp.where(valid[None, None, :], scores, -1000000000.0)


def attend_forward(query, key_rows, value_rows, valid):

    def one_group(pieces):
        query_group, key_group, value_group = pieces
        scores = scores_of(query_group, key_group, valid)
        top = jnp.max(scores, axis=-1, keepdims=True)
        expo = jnp.exp(scores - top)
        total = jnp.sum(expo, axis=-1, keepdims=True)
        probs = (expo / total).astype(jnp.bfloat16)
        result = jnp.einsum("hqk,hkd->hqd", probs, value_group, preferred_element_type=jnp.float32)
        return (result, top, total)

    results, tops, totals = lax.map(
        one_group, (split_heads(query), split_heads(key_rows), split_heads(value_rows))
    )
    return (join_heads(results), (tops, totals))


def attend_backward(query, key_rows, value_rows, valid, stats, grad_output):
    tops, totals = stats

    def one_group(pieces):
        query_group, key_group, value_group, top, total, grad_group = pieces
        scores = scores_of(query_group, key_group, valid)
        probs = jnp.exp(scores - top) / total
        grad_probs = jnp.einsum(
            "hqd,hkd->hqk", grad_group, value_group, preferred_element_type=jnp.float32
        )
        inner = jnp.sum(probs * grad_probs, axis=-1, keepdims=True)
        grad_scores = (probs * (grad_probs - inner)).astype(jnp.bfloat16)
        factor = HEAD_DIM ** (-0.5)
        grad_query = (
            jnp.einsum("hqk,hkd->hqd", grad_scores, key_group, preferred_element_type=jnp.float32)
            * factor
        )
        grad_keys = (
            jnp.einsum("hqk,hqd->hkd", grad_scores, query_group, preferred_element_type=jnp.float32)
            * factor
        )
        grad_values = jnp.einsum(
            "hqk,hqd->hkd",
            probs.astype(jnp.bfloat16),
            grad_group,
            preferred_element_type=jnp.float32,
        )
        return (grad_query, inner, grad_keys, grad_values)

    results = lax.map(
        one_group,
        (
            split_heads(query),
            split_heads(key_rows),
            split_heads(value_rows),
            tops,
            totals,
            split_heads(grad_output),
        ),
    )
    return (join_heads(results[0]), results[1], join_heads(results[2]), join_heads(results[3]))


def local(
    tokens,
    cotangent,
    image_tokens,
    image_lengths,
    key_mask,
    camera,
    modulation,
    q_cross,
    kv_image,
    out_cross,
    qkv_self,
    out_self,
    mlp_in,
    mlp_out,
):
    q_full, kv_full, out_cross_full, qkv_full, out_self_full, mlp_in_full, mlp_out_full = (
        lax.all_gather(q_cross, "batch", axis=0, tiled=True),
        lax.all_gather(kv_image, "batch", axis=0, tiled=True),
        lax.all_gather(out_cross, "batch", axis=0, tiled=True),
        lax.all_gather(qkv_self, "batch", axis=0, tiled=True),
        lax.all_gather(out_self, "batch", axis=0, tiled=True),
        lax.all_gather(mlp_in, "batch", axis=0, tiled=True),
        lax.all_gather(mlp_out, "batch", axis=0, tiled=True),
    )
    camera_gate = jax.nn.silu(camera.astype(jnp.float32)).astype(jnp.bfloat16)
    modulation_all = lax.psum(product(camera_gate, modulation), "batch")
    object_index = lax.axis_index("batch")
    width = tokens.shape[2]
    shifts = lax.dynamic_index_in_dim(modulation_all, object_index, 0, keepdims=False).reshape(
        6, width
    )
    stream = tokens[0].astype(jnp.float32)
    image_rows = image_tokens[0]
    positions = jnp.arange(image_rows.shape[0], dtype=jnp.int32)
    valid = (positions < image_lengths[0]) & ((key_mask[0] == 1) | (positions == 0))
    everywhere = jnp.ones((lax.axis_size("seq") * stream.shape[0],), dtype=jnp.bool_)
    normed_cross, cross_pullback = jax.vjp(modulated_norm, stream, shifts[0], shifts[1])
    normed_cross = normed_cross.astype(jnp.bfloat16)
    query_cross = product(normed_cross, q_full).astype(jnp.bfloat16)
    image_kv = product(image_rows, kv_full)
    image_keys = image_kv[:, :width].astype(jnp.bfloat16)
    image_values = image_kv[:, width:].astype(jnp.bfloat16)
    attended_cross, cross_stats = attend_forward(query_cross, image_keys, image_values, valid)
    attended_cross = attended_cross.astype(jnp.bfloat16)
    after_cross = stream + product(attended_cross, out_cross_full)
    normed_self, self_pullback = jax.vjp(modulated_norm, after_cross, shifts[2], shifts[3])
    normed_self = normed_self.astype(jnp.bfloat16)
    packed = product(normed_self, qkv_full).astype(jnp.bfloat16)
    query_self = packed[:, :width]
    key_local = packed[:, width : 2 * width]
    value_local = packed[:, 2 * width :]
    key_whole, value_whole = (
        lax.all_gather(key_local, "seq", axis=0, tiled=True),
        lax.all_gather(value_local, "seq", axis=0, tiled=True),
    )
    attended_self, self_stats = attend_forward(query_self, key_whole, value_whole, everywhere)
    attended_self = attended_self.astype(jnp.bfloat16)
    after_self = after_cross + product(attended_self, out_self_full)
    normed_mlp, mlp_pullback = jax.vjp(modulated_norm, after_self, shifts[4], shifts[5])
    normed_mlp = normed_mlp.astype(jnp.bfloat16)
    up_rows = product(normed_mlp, mlp_in_full)
    hidden, gelu_pullback = jax.vjp(jax.nn.gelu, up_rows)
    hidden = hidden.astype(jnp.bfloat16)
    output = after_self + product(hidden, mlp_out_full)
    grad_stream = cotangent[0].astype(jnp.float32)
    grad_branch = grad_stream.astype(jnp.bfloat16)
    grad_mlp_out = contract_rows(hidden, grad_branch)
    (grad_up,) = gelu_pullback(times_transposed(grad_branch, mlp_out_full))
    grad_up = grad_up.astype(jnp.bfloat16)
    grad_mlp_in = contract_rows(normed_mlp, grad_up)
    grad_from, shift_mlp, scale_mlp = mlp_pullback(times_transposed(grad_up, mlp_in_full))
    grad_stream = grad_stream + grad_from
    grad_branch = grad_stream.astype(jnp.bfloat16)
    grad_out_self = contract_rows(attended_self, grad_branch)
    grad_attended = times_transposed(grad_branch, out_self_full).astype(jnp.bfloat16)
    grad_query, inner_local, key_terms, value_terms = attend_backward(
        query_self, key_whole, value_whole, everywhere, self_stats, grad_attended
    )
    grad_key, grad_value = (
        lax.psum_scatter(key_terms, "seq", scatter_dimension=0, tiled=True),
        lax.psum_scatter(value_terms, "seq", scatter_dimension=0, tiled=True),
    )
    grad_packed = jnp.concatenate([grad_query, grad_key, grad_value], axis=1).astype(jnp.bfloat16)
    grad_qkv_self = contract_rows(normed_self, grad_packed)
    grad_from, shift_self, scale_self = self_pullback(times_transposed(grad_packed, qkv_full))
    grad_stream = grad_stream + grad_from
    grad_branch = grad_stream.astype(jnp.bfloat16)
    grad_out_cross = contract_rows(attended_cross, grad_branch)
    grad_attended = times_transposed(grad_branch, out_cross_full).astype(jnp.bfloat16)
    grad_query, inner_cross, key_terms, value_terms = attend_backward(
        query_cross, image_keys, image_values, valid, cross_stats, grad_attended
    )
    image_float = image_rows.astype(jnp.float32)
    image_key_grad, image_value_grad = (
        lax.psum_scatter(
            key_terms.astype(jnp.bfloat16), "seq", scatter_dimension=1, tiled=True
        ).astype(jnp.float32),
        lax.psum_scatter(
            value_terms.astype(jnp.bfloat16), "seq", scatter_dimension=1, tiled=True
        ).astype(jnp.float32),
    )
    block_width = image_key_grad.shape[1]
    column_start = lax.axis_index("seq") * block_width
    image_grads = jnp.concatenate([image_key_grad, image_value_grad], axis=1)
    kv_block = lax.dot_general(
        image_float,
        image_grads,
        (((0,), (0,)), ((), ())),
        precision=highest,
        preferred_element_type=jnp.float32,
    )
    grad_kv_image = jnp.zeros((image_rows.shape[1], 2 * width), jnp.float32)
    grad_kv_image = lax.dynamic_update_slice(
        grad_kv_image, kv_block[:, :block_width], (jnp.int32(0), column_start)
    )
    grad_kv_image = lax.dynamic_update_slice(
        grad_kv_image, kv_block[:, block_width:], (jnp.int32(0), column_start + width)
    )
    grad_query = grad_query.astype(jnp.bfloat16)
    grad_q_cross = contract_rows(normed_cross, grad_query)
    grad_from, shift_cross, scale_cross = cross_pullback(times_transposed(grad_query, q_full))
    grad_input = grad_stream + grad_from
    grad_row = jnp.concatenate(
        [shift_cross, scale_cross, shift_self, scale_self, shift_mlp, scale_mlp]
    )
    grad_table = lax.dynamic_update_slice(
        jnp.zeros(modulation_all.shape, jnp.float32),
        grad_row[None, :],
        (object_index, jnp.int32(0)),
    )
    grad_table = lax.psum(grad_table, ("batch", "seq"))
    grad_modulation = lax.dot_general(
        camera_gate.astype(jnp.float32),
        grad_table,
        (((0,), (0,)), ((), ())),
        precision=highest,
        preferred_element_type=jnp.float32,
    )
    terms = (
        grad_q_cross,
        grad_kv_image,
        grad_out_cross,
        grad_qkv_self,
        grad_out_self,
        grad_mlp_in,
        grad_mlp_out,
    )
    shares = (
        lax.psum_scatter(
            terms[0].astype(jnp.bfloat16), "batch", scatter_dimension=0, tiled=True
        ).astype(jnp.float32),
        lax.psum_scatter(
            terms[1].astype(jnp.bfloat16), "batch", scatter_dimension=0, tiled=True
        ).astype(jnp.float32),
        lax.psum_scatter(
            terms[2].astype(jnp.bfloat16), "batch", scatter_dimension=0, tiled=True
        ).astype(jnp.float32),
        lax.psum_scatter(
            terms[3].astype(jnp.bfloat16), "batch", scatter_dimension=0, tiled=True
        ).astype(jnp.float32),
        lax.psum_scatter(
            terms[4].astype(jnp.bfloat16), "batch", scatter_dimension=0, tiled=True
        ).astype(jnp.float32),
        lax.psum_scatter(
            terms[5].astype(jnp.bfloat16), "batch", scatter_dimension=0, tiled=True
        ).astype(jnp.float32),
        lax.psum_scatter(
            terms[6].astype(jnp.bfloat16), "batch", scatter_dimension=0, tiled=True
        ).astype(jnp.float32),
    )
    totals = (
        lax.psum(shares[0].astype(jnp.bfloat16), "seq").astype(jnp.float32),
        lax.psum(shares[1].astype(jnp.bfloat16), "seq").astype(jnp.float32),
        lax.psum(shares[2].astype(jnp.bfloat16), "seq").astype(jnp.float32),
        lax.psum(shares[3].astype(jnp.bfloat16), "seq").astype(jnp.float32),
        lax.psum(shares[4].astype(jnp.bfloat16), "seq").astype(jnp.float32),
        lax.psum(shares[5].astype(jnp.bfloat16), "seq").astype(jnp.float32),
        lax.psum(shares[6].astype(jnp.bfloat16), "seq").astype(jnp.float32),
    )
    return (
        output.astype(jnp.bfloat16)[None],
        grad_input[None],
        grad_modulation,
        totals[0],
        totals[1],
        totals[2],
        totals[3],
        totals[4],
        totals[5],
        totals[6],
    )


bf16 = jnp.bfloat16
f32 = jnp.float32
MESH = pl.DeviceIdType.MESH
BELOW = -3.0e38


def nn(a, b):
    return jnp.dot(a, b, preferred_element_type=f32)


def nt(a, b):
    return lax.dot_general(a, b, (((1,), (1,)), ((), ())), preferred_element_type=f32)


def tn(a, b):
    return lax.dot_general(a, b, (((0,), (0,)), ((), ())), preferred_element_type=f32)


def one_head(pair, side):
    lane = lax.broadcasted_iota(jnp.int32, pair.shape, 1)
    return jnp.where(lane // HEAD_DIM == side, pair, jnp.zeros_like(pair))


def two_heads(first, second):
    lane = lax.broadcasted_iota(jnp.int32, first.shape, 1)
    return jnp.where(lane < HEAD_DIM, first, second)


def softmax_rows(scores, mask):
    if mask is not None:
        scores = jnp.where(mask[0:1, :] > 0.5, scores, mask[1:2, :])
    expo = jnp.exp(scores - jnp.max(scores, axis=-1, keepdims=True))
    return expo * (1.0 / jnp.sum(expo, axis=-1, keepdims=True))


def norm_stats(rows):
    center = rows - jnp.mean(rows, axis=-1, keepdims=True)
    inverse = lax.rsqrt(jnp.mean(center * center, axis=-1, keepdims=True) + epsilon)
    return center * inverse, inverse


def norm_forward(rows, shift, scale):
    return norm_stats(rows)[0] * (1.0 + scale) + shift


def norm_backward(rows, scale, grad):
    normed, inverse = norm_stats(rows)
    inner = grad * (1.0 + scale)
    mean_inner = jnp.mean(inner, axis=-1, keepdims=True)
    mean_cross = jnp.mean(inner * normed, axis=-1, keepdims=True)
    grad_rows = inverse * (inner - mean_inner - normed * mean_cross)
    return (
        grad_rows,
        jnp.sum(grad, axis=0, keepdims=True),
        jnp.sum(grad * normed, axis=0, keepdims=True),
    )


Q, KV, OC, QKV, OS, UP, DOWN, CAMERA, TABLE, TOKENS, OWN, IMAGE, COTANGENT = range(13)


GATHER = (
    (KV, 0, 1),
    (Q, 0, 1),
    (OC, 0, 1),
    (QKV, 0, 2),
    (QKV, 1, 2),
    (OS, 0, 1),
    (UP, 0, 4),
    (UP, 1, 4),
    (UP, 2, 4),
    (UP, 3, 4),
    (DOWN, 0, 4),
    (DOWN, 1, 4),
    (DOWN, 2, 4),
    (DOWN, 3, 4),
)
SCATTER = (
    (DOWN, 0, 4),
    (DOWN, 1, 4),
    (DOWN, 2, 4),
    (DOWN, 3, 4),
    (UP, 0, 4),
    (UP, 1, 4),
    (UP, 2, 4),
    (UP, 3, 4),
    (OS, 0, 1),
    (QKV, 0, 2),
    (QKV, 1, 2),
    (OC, 0, 1),
    (Q, 0, 1),
    (KV, 0, 1),
)
BY_ROWS = (OC, OS)
AHEAD = 2


class Sizes:
    def __init__(self, mesh_shape, inputs):
        self.batch, self.seq = mesh_shape["batch"], mesh_shape["seq"]
        self.own, self.width = inputs[0].shape[1:]
        self.image_rows, self.image_width = inputs[2].shape[1:]
        self.chunks = 4
        self.part = self.own // self.chunks
        self.rows = self.seq * self.part
        self.tokens = self.seq * self.own
        self.columns = self.width // self.seq
        self.hidden = inputs[12].shape[1] // self.seq
        self.keys = -(-self.image_rows // 128) * 128
        self.whole_rows = self.image_rows // 128 * 128
        self.block = self.width // self.batch
        self.image_block = self.image_width // self.batch
        self.weights = (
            (self.block, self.columns),
            (self.image_block, 2 * self.columns),
            (self.block // self.seq, self.width),
            (self.block, 3 * self.columns),
            (self.block // self.seq, self.width),
            (self.block, self.hidden),
            (self.hidden // self.batch, self.width),
        )


class Refs:
    def __init__(self, refs):
        rest = iter(refs)
        self.tokens = next(rest)
        self.cotangent = next(rest)
        self.image = next(rest)
        self.marks = next(rest)
        self.lengths = next(rest)
        self.camera = next(rest)
        self.modulation = next(rest)
        self.q_cross = next(rest)
        self.kv_image = next(rest)
        self.out_cross = next(rest)
        self.qkv_self = next(rest)
        self.out_self = next(rest)
        self.mlp_in = next(rest)
        self.mlp_out = next(rest)
        self.output = next(rest)
        self.grad_tokens = next(rest)
        self.table = next(rest)
        self.gout = [next(rest) for _ in range(7)]
        self.weights = [next(rest) for _ in range(7)]
        self.firsts = [next(rest) for _ in range(7)]
        self.seconds = [next(rest) for _ in range(7)]
        self.buf_a = next(rest)
        self.buf_b = next(rest)
        self.buf_h2 = next(rest)
        self.buf_b2 = next(rest)
        self.part_main = next(rest)
        self.core_main = next(rest)
        self.send_main = next(rest)
        self.line_main = next(rest)
        self.part_side = next(rest)
        self.core_side = next(rest)
        self.send_side = next(rest)
        self.line_side = next(rest)
        self.turn_in = [next(rest) for _ in range(2)]
        self.turn_out = [next(rest) for _ in range(2)]
        self.image_all = next(rest)
        self.tail = next(rest)
        self.marks_own = next(rest)
        self.mask_all = next(rest)
        self.camera_own = next(rest)
        self.mods_all = next(rest)
        self.mods = next(rest)
        self.sums = next(rest)
        self.sums_seq = next(rest)
        self.normed1 = next(rest)
        self.query1 = next(rest)
        self.key1 = next(rest)
        self.value1 = next(rest)
        self.att1 = next(rest)
        self.packed2 = next(rest)
        self.att2 = next(rest)
        self.hidden = next(rest)
        self.grad_up = next(rest)
        self.grad_key = next(rest)
        self.grad_value = next(rest)
        self.x0 = next(rest)
        self.x1 = next(rest)
        self.x2 = next(rest)
        self.grads_a = next(rest)
        self.grads_b = next(rest)
        self.grads_c = next(rest)
        self.sem_load = next(rest)
        self.sem_wz_s = next(rest)
        self.sem_wz_r = next(rest)
        self.sem_wx_s = next(rest)
        self.sem_wx_r = next(rest)
        self.sem_gx_s = next(rest)
        self.sem_gx_r = next(rest)
        self.sem_gz_s = next(rest)
        self.sem_gz_r = next(rest)
        self.sem_gs_s = next(rest)
        self.sem_gs_r = next(rest)
        self.sem_own = next(rest)
        self.sem_ti_s = next(rest)
        self.sem_ti_r = next(rest)
        self.sem_to_s = next(rest)
        self.sem_to_r = next(rest)
        self.sem_in_s = next(rest)
        self.sem_in_r = next(rest)
        self.sem_ag_s = next(rest)
        self.sem_ag_r = next(rest)
        self.sem_rs_s = next(rest)
        self.sem_rs_r = next(rest)
        self.sem_m_s = next(rest)
        self.sem_m_r = next(rest)
        self.sem_d_s = next(rest)
        self.sem_d_r = next(rest)
        self.sem_t_s = next(rest)
        self.sem_t_r = next(rest)
        self.sem_out = next(rest)


def whole_layer(z, *refs):
    r = Refs(refs)
    W, FIRST, SECOND, GOUT = r.weights, r.firsts, r.seconds, r.gout
    n, S, B = z.chunks, z.seq, z.batch
    part, rows, D, C = z.part, z.rows, z.width, z.columns
    Z = B // 2
    b = lax.axis_index("batch")
    s = lax.axis_index("seq")
    zz = b // 2
    x = lax.rem(b, 2)
    y = s // 2
    c = lax.rem(s, 2)
    other_x = 1 - x
    other_c = 1 - c
    other_y = 1 - y
    x_peer = (2 * zz + other_x, s)
    core_peer = (b, 2 * y + other_c)
    line_peer = (b, 2 * other_y + c)
    line_slot = 2 * other_y + c
    core_slot = 2 * y + other_c
    far_slot = 2 * other_y + other_c

    def z_of(j):
        return lax.rem(zz + j, Z)

    def remote(src, dst, send, recv, device):
        return pltpu.make_async_remote_copy(
            src_ref=src,
            dst_ref=dst,
            send_sem=send,
            recv_sem=recv,
            device_id=device,
            device_id_type=MESH,
        )

    def arrived(dst, send, recv, device):
        remote(dst, dst, send, recv, device).wait_recv()

    barrier = pltpu.get_barrier_semaphore()
    for j in range(1, B):
        pl.semaphore_signal(barrier, inc=1, device_id=(lax.rem(b + j, B), s), device_id_type=MESH)
    for j in range(1, S):
        pl.semaphore_signal(barrier, inc=1, device_id=(b, lax.rem(s + j, S)), device_id_type=MESH)

    loads = {}

    def load(key, src, dst):
        count = sum(len(copies) for copies in loads.values())
        copy = pltpu.make_async_copy(src, dst, r.sem_load.at[count])
        loads.setdefault(key, []).append(copy)
        copy.start()

    def col(index, width):
        return pl.ds(pl.multiple_of(index * width, 128), width)

    wide = z.hidden // B
    for j in range(2):
        load(
            KV,
            r.kv_image.at[:, pl.ds(pl.multiple_of(j * D + s * C, 128), C)],
            W[KV].at[b, :, pl.ds(j * C, C)],
        )
    load(Q, r.q_cross.at[:, col(s, C)], W[Q].at[b])
    load(TOKENS, r.tokens, r.buf_a.at[:, s])
    load(CAMERA, r.camera, r.camera_own)
    for k in range(6):
        load(TABLE, r.modulation.at[:, pl.ds(k * D, D)], r.hidden.at[pl.ds(k * z.block, z.block)])
    few = z.block // S
    load(OC, r.out_cross.at[pl.ds(pl.multiple_of(s * few, 16), few)], r.turn_in[0].at[zz])
    for j in range(3):
        load(
            QKV,
            r.qkv_self.at[:, pl.ds(pl.multiple_of(j * D + s * C, 128), C)],
            W[QKV].at[b, :, pl.ds(j * C, C)],
        )
    load(OS, r.out_self.at[pl.ds(pl.multiple_of(s * few, 16), few)], r.turn_in[1].at[zz])
    load(IMAGE, r.image, r.image_all)
    load(IMAGE, r.marks, r.marks_own)
    for j in range(B):
        load(
            UP,
            r.mlp_in.at[:, pl.ds(pl.multiple_of(j * (z.hidden * S // B) + s * wide, 128), wide)],
            W[UP].at[b, :, pl.ds(j * wide, wide)],
        )
    load(DOWN, r.mlp_out.at[pl.ds(pl.multiple_of(s * wide, 128), wide), :], W[DOWN].at[b])
    load(COTANGENT, r.cotangent, r.buf_b.at[:, s])
    load(OWN, r.tokens, r.x0)

    pl.semaphore_wait(barrier, B - 1 + S - 1)

    def loaded(key):
        for copy in loads[key]:
            copy.wait()

    def rows_of(piece):
        w, which, parts = piece
        count = z.weights[w][0] // parts
        return w, pl.ds(which * count, count)

    def turned(w):
        return 0 if w == OC else 1

    def quarter(index):
        return pl.ds(pl.multiple_of(index * few, 16), few)

    def z_place(k, from_z):
        w, span = rows_of(GATHER[k])
        return r.turn_in[turned(w)].at[from_z] if w in BY_ROWS else W[w].at[2 * from_z + x, span]

    def z_send(k, j):
        place = z_place(k, zz)
        return remote(
            place, place, r.sem_wz_s.at[k, j - 1], r.sem_wz_r.at[k, zz], (2 * z_of(j) + x, s)
        )

    def x_send(k, from_z):
        w, span = rows_of(GATHER[k])
        place, mark = (W[w].at[x], 0) if w in BY_ROWS else (z_place(k, from_z), from_z)
        return remote(place, place, r.sem_wx_s.at[k, mark], r.sem_wx_r.at[k, mark], x_peer)

    def turn_send(w, j):
        to = lax.rem(s + j, S)
        return remote(
            r.turn_in[turned(w)].at[to],
            W[w].at[x, quarter(s)],
            r.sem_ti_s.at[turned(w), j - 1],
            r.sem_ti_r.at[turned(w), s],
            (b, to),
        )

    def weight_start(k):
        if k >= len(GATHER):
            return
        w, which, _ = GATHER[k]
        if which == 0:
            loaded(w)
        for j in range(1, Z):
            z_send(k, j).start()
        if w not in BY_ROWS:
            x_send(k, zz).start()

    def weight_pass(k):
        w, _ = rows_of(GATHER[k])
        for j in range(1, Z):
            from_z = z_of(j)
            arrived(
                z_place(k, from_z),
                r.sem_wz_s.at[k, 0],
                r.sem_wz_r.at[k, from_z],
                (2 * from_z + x, s),
            )
            if w not in BY_ROWS:
                x_send(k, from_z).start()
        weight_start(k + AHEAD)
        if w in BY_ROWS:
            for j in range(1, S):
                turn_send(w, j).start()
            W[w][x, quarter(s), :] = r.turn_in[turned(w)][s]

    def weight_turn(k):
        w, _ = rows_of(GATHER[k])
        for j in range(1, S):
            m = lax.rem(s + j, S)
            arrived(
                W[w].at[x, quarter(m)], r.sem_ti_s.at[turned(w), 0], r.sem_ti_r.at[turned(w), m], (b, m)
            )
        x_send(k, zz).start()

    def weight_wait(w):
        for k in range(len(GATHER)):
            if GATHER[k][0] != w:
                continue
            _, span = rows_of(GATHER[k])
            if w in BY_ROWS:
                arrived(W[w].at[other_x], r.sem_wx_s.at[k, 0], r.sem_wx_r.at[k, 0], x_peer)
                continue
            for from_z in range(Z):
                place = W[w].at[2 * from_z + other_x, span]
                arrived(place, r.sem_wx_s.at[k, 0], r.sem_wx_r.at[k, from_z], x_peer)

    def weight_drain(k):
        w, _ = rows_of(GATHER[k])
        for j in range(1, Z):
            z_send(k, j).wait_send()
        if w in BY_ROWS:
            x_send(k, zz).wait_send()
            for j in range(1, S):
                turn_send(w, j).wait_send()
        else:
            for j in range(Z):
                x_send(k, z_of(j)).wait_send()

    def give(buf, i, k):
        slot, peer = [(s, core_peer), (s, line_peer), (line_slot, core_peer)][k]
        return remote(
            buf.at[i, slot], buf.at[i, slot], r.sem_ag_s.at[i, k], r.sem_ag_r.at[i, k], peer
        )

    def gather_start(buf, i):
        give(buf, i, 1).start()
        give(buf, i, 0).start()

    def gather_pass(buf, i):
        arrived(buf.at[i, line_slot], r.sem_ag_s.at[i, 1], r.sem_ag_r.at[i, 1], line_peer)
        give(buf, i, 2).start()

    def gather_wait(buf, i):
        arrived(buf.at[i, core_slot], r.sem_ag_s.at[i, 0], r.sem_ag_r.at[i, 0], core_peer)
        arrived(buf.at[i, far_slot], r.sem_ag_s.at[i, 2], r.sem_ag_r.at[i, 2], core_peer)
        for k in range(3):
            give(buf, i, k).wait_send()

    def give_input(buf, m, k):
        slot, peer = [(s, core_peer), (s, line_peer), (line_slot, core_peer)][k]
        return remote(
            buf.at[:, slot], buf.at[:, slot], r.sem_in_s.at[m, k], r.sem_in_r.at[m, k], peer
        )

    def input_start(buf, m):
        give_input(buf, m, 1).start()
        give_input(buf, m, 0).start()

    def input_pass(buf, m):
        arrived(buf.at[:, line_slot], r.sem_in_s.at[m, 1], r.sem_in_r.at[m, 1], line_peer)
        give_input(buf, m, 2).start()

    def input_wait(buf, m):
        arrived(buf.at[:, core_slot], r.sem_in_s.at[m, 0], r.sem_in_r.at[m, 0], core_peer)
        arrived(buf.at[:, far_slot], r.sem_in_s.at[m, 2], r.sem_in_r.at[m, 2], core_peer)
        for k in range(3):
            give_input(buf, m, k).wait_send()

    lanes = (
        (r.part_main, r.core_main, r.send_main, r.line_main),
        (r.part_side, r.core_side, r.send_side, r.line_side),
    )

    def sum_core(lane, i):
        mine, core, _, _ = lanes[lane]
        return remote(
            mine.at[i, :, other_c],
            core.at[i],
            r.sem_rs_s.at[lane, i, 0],
            r.sem_rs_r.at[lane, i, 0],
            core_peer,
        )

    def sum_line(lane, i):
        _, _, send, line = lanes[lane]
        return remote(
            send.at[i],
            line.at[i],
            r.sem_rs_s.at[lane, i, 1],
            r.sem_rs_r.at[lane, i, 1],
            line_peer,
        )

    def sum_start(lane, i, value):
        lanes[lane][0][i] = value.astype(bf16).reshape(2, 2, part, D)
        sum_core(lane, i).start()

    def sum_pass(lane, i):
        mine, core, send, _ = lanes[lane]
        sum_core(lane, i).wait_recv()
        send[i] = (mine[i, other_y, c].astype(f32) + core[i, other_y].astype(f32)).astype(bf16)
        sum_line(lane, i).start()

    def sum_end(lane, i):
        mine, core, _, line = lanes[lane]
        sum_line(lane, i).wait_recv()
        total = mine[i, y, c].astype(f32) + core[i, y].astype(f32) + line[i].astype(f32)
        sum_core(lane, i).wait_send()
        sum_line(lane, i).wait_send()
        return total

    def grad_place(w):
        return {
            Q: r.grads_a.at[:, :, :, pl.ds(0, C)],
            KV: r.grads_a.at[:, :, pl.ds(0, z.image_block), pl.ds(C, 2 * C)],
            OC: r.grads_c.at[0],
            QKV: r.grads_b.at[:, :, :, pl.ds(0, 3 * C)],
            OS: r.grads_c.at[1],
            UP: r.grads_a,
            DOWN: r.grads_b,
        }[w]

    def first_of(k):
        w, span = rows_of(SCATTER[k])
        return r.turn_out[turned(w)].at[zz] if w in BY_ROWS else FIRST[w].at[zz, span]

    def grad_x(k):
        w, span = rows_of(SCATTER[k])
        place = grad_place(w)
        src = place.at[other_x] if w in BY_ROWS else place.at[:, other_x, span]
        dst = FIRST[w] if w in BY_ROWS else FIRST[w].at[:, span]
        return remote(src, dst, r.sem_gx_s.at[k], r.sem_gx_r.at[k], x_peer)

    def turn_back(w, j):
        to = lax.rem(s + j, S)
        return remote(
            FIRST[w].at[quarter(to)],
            r.turn_out[turned(w)].at[s],
            r.sem_to_s.at[turned(w), j - 1],
            r.sem_to_r.at[turned(w), s],
            (b, to),
        )

    def grad_z(k, j):
        w, span = rows_of(SCATTER[k])
        to = z_of(j)
        src = r.turn_out[turned(w)].at[to] if w in BY_ROWS else FIRST[w].at[to, span]
        return remote(
            src,
            SECOND[w].at[Z - j - 1, span],
            r.sem_gz_s.at[k, j - 1],
            r.sem_gz_r.at[k, zz],
            (2 * to + x, s),
        )

    def shared(k, origin):
        w, span = rows_of(SCATTER[k])
        return GOUT[w].at[origin, span]

    def grad_s(k, way):
        mine = shared(k, line_slot) if way == 2 else first_of(k)
        origin = line_slot if way == 2 else s
        peer = line_peer if way == 1 else core_peer
        return remote(mine, shared(k, origin), r.sem_gs_s.at[k, way], r.sem_gs_r.at[k, way], peer)

    def grad_own(k):
        return pltpu.make_async_copy(first_of(k), shared(k, s), r.sem_own.at[k])

    def grad_relay(k):
        arrived(shared(k, line_slot), r.sem_gs_s.at[k, 1], r.sem_gs_r.at[k, 1], line_peer)
        grad_s(k, 2).start()

    def grad_start(k):
        grad_x(k).start()

    def grad_pass(k):
        w, span = rows_of(SCATTER[k])
        grad_x(k).wait_recv()
        place = grad_place(w)
        if w in BY_ROWS:
            FIRST[w][...] = (FIRST[w][...].astype(f32) + place[x].astype(f32)).astype(bf16)
            for j in range(1, S):
                turn_back(w, j).start()
            r.turn_out[turned(w)][s] = FIRST[w][quarter(s), :]
        else:
            for m in range(Z):
                term = FIRST[w][m, span].astype(f32) + place[m, x, span].astype(f32)
                FIRST[w][m, span] = term.astype(bf16)
            for j in range(1, Z):
                grad_z(k, j).start()
        grad_x(k).wait_send()

    def grad_turn(k):
        w, _ = rows_of(SCATTER[k])
        for j in range(1, S):
            m = lax.rem(s + j, S)
            arrived(
                r.turn_out[turned(w)].at[m],
                r.sem_to_s.at[turned(w), 0],
                r.sem_to_r.at[turned(w), m],
                (b, m),
            )
        for j in range(1, Z):
            grad_z(k, j).start()

    def grad_end(k):
        w, span = rows_of(SCATTER[k])
        mine = first_of(k)
        total = mine[...].astype(f32)
        for j in range(1, Z):
            m = z_of(j)
            term = SECOND[w].at[j - 1, span]
            arrived(term, r.sem_gz_s.at[k, 0], r.sem_gz_r.at[k, m], (2 * m + x, s))
            total = total + term[...].astype(f32)
        mine[...] = total.astype(bf16)
        grad_s(k, 1).start()
        grad_s(k, 0).start()
        grad_own(k).start()
        for j in range(1, Z):
            grad_z(k, j).wait_send()

    def grad_drain(k):
        w, _ = rows_of(SCATTER[k])
        arrived(shared(k, core_slot), r.sem_gs_s.at[k, 0], r.sem_gs_r.at[k, 0], core_peer)
        arrived(shared(k, far_slot), r.sem_gs_s.at[k, 2], r.sem_gs_r.at[k, 2], core_peer)
        for way in range(3):
            grad_s(k, way).wait_send()
        grad_own(k).wait()
        if w in BY_ROWS:
            for j in range(1, S):
                turn_back(w, j).wait_send()

    def mods_send(j):
        to = lax.rem(b + j, B)
        return remote(
            r.x2.at[0, pl.ds(pl.multiple_of(8 * to, 8), 8)],
            r.mods_all.at[b],
            r.sem_m_s.at[j - 1],
            r.sem_m_r.at[b],
            (to, s),
        )

    for k in range(AHEAD):
        weight_start(k)
    loaded(TOKENS)
    input_start(r.buf_a, 0)
    loaded(CAMERA)
    loaded(TABLE)
    camera = r.camera_own[...].astype(f32)
    gate = (camera * jax.nn.sigmoid(camera)).astype(bf16)
    for k in range(6):
        term = nn(gate, r.hidden[k * z.block : (k + 1) * z.block, :])
        for o in range(B):
            r.x2[0, 8 * o + k : 8 * o + k + 1, :] = term[o : o + 1, :]
    for j in range(1, B):
        mods_send(j).start()
    loaded(COTANGENT)
    input_start(r.buf_b, 1)
    loaded(IMAGE)
    loaded(OWN)
    places = lax.broadcasted_iota(jnp.int32, (1, z.image_rows), 1)
    valid = (places < r.lengths[0]) & ((r.marks_own[...] == 1) | (places == 0))
    places = lax.broadcasted_iota(jnp.int32, (1, z.keys), 1)
    r.mask_all[0:1, :] = jnp.zeros((1, z.keys), f32)
    r.mask_all[0:1, : z.image_rows] = jnp.where(valid, 1.0, 0.0)
    r.mask_all[1:2, :] = jnp.where(places < z.image_rows, -1000000000.0, BELOW)
    rest = z.image_rows - z.whole_rows
    last = r.image_all[z.whole_rows :, :]
    padding = jnp.zeros((z.keys - z.image_rows, z.image_width), bf16)
    r.tail[...] = jnp.concatenate([last, padding], axis=0) if rest else padding

    mods = r.x2[0, pl.ds(pl.multiple_of(8 * b, 8), 8)]
    for j in range(1, B):
        k = lax.rem(b + j, B)
        arrived(r.mods_all.at[k], r.sem_m_s.at[0], r.sem_m_r.at[k], (k, s))
        mods = mods + r.mods_all[k]
    r.mods[...] = mods
    for j in range(1, B):
        mods_send(j).wait_send()

    def mod(k):
        return r.mods[k : k + 1, :]

    def chunk(i):
        return pl.ds(pl.multiple_of(i * rows, rows), rows)

    scale_q = HEAD_DIM ** (-0.5)
    input_pass(r.buf_a, 0)
    weight_pass(0)
    weight_pass(1)
    input_wait(r.buf_a, 0)

    def normalize(i, _):
        rows_in = r.buf_a[i].reshape(rows, D).astype(f32)
        r.normed1[chunk(i), :] = norm_forward(rows_in, mod(0), mod(1)).astype(bf16)
        return 0

    lax.fori_loop(0, n, normalize, 0)
    weight_wait(KV)

    def project_rows(block, part_rows):
        both = nn(block, W[KV][...].reshape(z.image_width, 2 * C))
        r.key1[part_rows, :] = both[:, :C].astype(bf16)
        r.value1[part_rows, :] = both[:, C:].astype(bf16)

    def project_image(k, _):
        part_rows = pl.ds(pl.multiple_of(k * 128, 128), 128)
        project_rows(r.image_all[part_rows, :], part_rows)
        return 0

    lax.fori_loop(0, z.whole_rows // 128, project_image, 0)
    project_rows(r.tail[...], pl.ds(z.whole_rows, z.keys - z.whole_rows))
    weight_wait(Q)

    weight_pass(2)

    def project_query(i):
        query = nn(r.normed1[chunk(i), :], W[Q][...].reshape(D, C)).astype(bf16)
        r.query1[chunk(i), :] = (query * scale_q).astype(bf16)

    def attend(i, query, key, value, att, mask):
        for p in range(C // 128):
            lane = slice(128 * p, 128 * p + 128)
            pair = query(i, lane)
            keys, values = key(lane), value(lane)
            result = []
            for side in range(2):
                probs = softmax_rows(nt(one_head(pair, side), keys), mask).astype(bf16)
                result.append(nn(probs, values))
            att[chunk(i), lane] = two_heads(*result).astype(bf16)

    def attend_back(i, query, key, value, grad, mask, grad_query):
        query_t = query(i, slice(0, C)).T
        grad_t = grad.T
        for p in range(C // 128):
            lane = slice(128 * p, 128 * p + 128)
            pair, grad_pair = query(i, lane), grad[:, lane]
            keys, values = key(lane), value(lane)
            result = []
            for side in range(2):
                head = slice(128 * p + HEAD_DIM * side, 128 * p + HEAD_DIM * (side + 1))
                probs = softmax_rows(nt(one_head(pair, side), keys), mask)
                grad_probs = nt(one_head(grad_pair, side), values)
                inner = jnp.sum(probs * grad_probs, axis=-1, keepdims=True)
                scores = (probs * (grad_probs - inner)).astype(bf16)
                count = keys.shape[0]
                value_term = nn(grad_t[head, :], probs.astype(bf16))
                key_term = nn(query_t[head, :], scores)
                r.grad_value[head, :count] += value_term
                r.grad_key[head, :count] += key_term
                result.append(nn(scores, keys))
            grad_query[chunk(i), lane] = (two_heads(*result) * scale_q).astype(bf16)

    cross = (
        lambda i, lane: r.query1[chunk(i), lane],
        lambda lane: r.key1[:, lane],
        lambda lane: r.value1[:, lane],
    )

    def plus(lane, offset):
        return slice(lane.start + offset, lane.stop + offset)

    own = (
        lambda i, lane: r.packed2[chunk(i), lane],
        lambda lane: r.packed2[:, plus(lane, C)],
        lambda lane: r.packed2[:, plus(lane, 2 * C)],
    )
    mask_rows = r.mask_all

    def at(i, value, stage):
        pl.when(i == value)(stage)

    def run(calls):
        for call, *values in calls:
            call(*values)

    def pipeline(ticks, *stages):
        last = max(offset for offset, _ in stages)

        def body(step, _):
            for when, calls in ticks.items():
                at(step, when, functools.partial(run, calls))
            for offset, stage in stages:
                i = step - offset

                @pl.when((i >= 0) & (i < n))
                def _():
                    stage(i)

            return 0

        lax.fori_loop(0, n + last, body, 0)

    def cross_forward(i):
        project_query(i)
        attend(i, *cross, r.att1, mask_rows)
        at(i, 0, functools.partial(run, [(weight_turn, 2), (weight_wait, OC)]))
        sum_start(0, i, nn(r.att1[chunk(i), :], W[OC][...].reshape(C, D)))

    def after_cross(i):
        total = r.x0[i].astype(f32) + sum_end(0, i)
        r.x1[i] = total
        r.buf_h2[i, s] = norm_forward(total, mod(2), mod(3)).astype(bf16)
        gather_start(r.buf_h2, i)

    def project_self(i):
        at(i, 0, functools.partial(weight_wait, QKV))
        gather_wait(r.buf_h2, i)
        packed = nn(r.buf_h2[i].reshape(rows, D), W[QKV][...].reshape(D, 3 * C)).astype(bf16)
        r.packed2[chunk(i), :C] = (packed[:, :C] * scale_q).astype(bf16)
        r.packed2[chunk(i), C:] = packed[:, C:]

    pipeline(
        {
            1: [(weight_pass, 3)],
            2: [(weight_pass, 4)],
            3: [(weight_pass, 5)],
            4: [(weight_pass, 6)],
            5: [(weight_turn, 5), (weight_pass, 7)],
            6: [(weight_pass, 8)],
            7: [(weight_pass, 9)],
        },
        (0, cross_forward),
        (1, lambda i: sum_pass(0, i)),
        (2, after_cross),
        (3, lambda i: gather_pass(r.buf_h2, i)),
        (4, project_self),
    )

    weight_wait(OS)
    input_pass(r.buf_b, 1)
    input_wait(r.buf_b, 1)
    r.sums[...] = jnp.zeros_like(r.sums)

    def clear_keys():
        r.grad_key[...] = jnp.zeros_like(r.grad_key)
        r.grad_value[...] = jnp.zeros_like(r.grad_value)

    clear_keys()

    def output_copy(i):
        return pltpu.make_async_copy(
            r.part_side.at[i, 0, 0], r.output.at[i], r.sem_out.at[2 + i]
        )

    def self_forward(i):
        attend(i, *own, r.att2, None)
        sum_start(0, i, nn(r.att2[chunk(i), :], W[OS][...].reshape(C, D)))

    def after_self(i):
        total = r.x1[i] + sum_end(0, i)
        r.x2[i] = total
        r.buf_a[i, s] = norm_forward(total, mod(4), mod(5)).astype(bf16)
        gather_start(r.buf_a, i)

    def feed(i):
        at(i, 0, functools.partial(run, [(weight_wait, UP), (weight_wait, DOWN)]))
        gather_wait(r.buf_a, i)
        rows_in = r.buf_a[i].reshape(rows, D)
        grad_out = r.buf_b[i].reshape(rows, D)
        up = W[UP]
        down = W[DOWN]
        forward = backward = None
        pieces = 2
        wide_piece = z.hidden // pieces
        for k in range(pieces):
            lane = slice(k * wide_piece, (k + 1) * wide_piece)
            up_piece = up[:, :, lane].reshape(D, wide_piece)
            down_piece = down[k * (B // pieces) : (k + 1) * (B // pieces)].reshape(wide_piece, D)
            u = nn(rows_in, up_piece)
            square = u * u
            root = 0.7978845608028654
            tanh = jnp.tanh(root * u * (1.0 + 0.044715 * square))
            half = 0.5 * (1.0 + tanh)
            hidden = (u * half).astype(bf16)
            slope = half + 0.5 * u * (1.0 - tanh * tanh) * (root * (1.0 + 0.134145 * square))
            grad_up = (nt(grad_out, down_piece) * slope).astype(bf16)
            r.hidden[chunk(i), lane] = hidden
            r.grad_up[chunk(i), lane] = grad_up
            first = nn(hidden, down_piece)
            second = nt(grad_up, up_piece)
            forward = first if forward is None else forward + first
            backward = second if backward is None else backward + second
        sum_start(0, i, backward)
        sum_start(1, i, forward)

    def keep_sums(k, shift, scale):
        r.sums[k : k + 1, :] += shift
        r.sums[k + 1 : k + 2, :] += scale

    def after_feed(i):
        stream = r.x2[i]
        grad, shift, scale = norm_backward(stream, mod(5), sum_end(0, i))
        keep_sums(4, shift, scale)
        grad = r.buf_b[i, s].astype(f32) + grad
        r.buf_b2[i, s] = grad.astype(bf16)
        gather_start(r.buf_b2, i)
        r.part_side[i, 0, 0] = (r.x2[i] + sum_end(1, i)).astype(bf16)
        r.x2[i] = grad
        output_copy(i).start()

    def self_back(i):
        gather_wait(r.buf_b2, i)
        grad = nt(r.buf_b2[i].reshape(rows, D), W[OS][...].reshape(C, D)).astype(bf16)
        attend_back(i, *own, grad, None, r.grad_up)

    def grads_into(place, lhs, rhs, block, width):
        pieces = 4
        count = lhs.shape[1] // pieces
        for k in range(pieces):
            value = tn(lhs[:, k * count : (k + 1) * count], rhs).astype(bf16)
            lead = count // block
            for m in range(lead):
                o = k * lead + m
                place[o // 2, o % 2, :, :width] = value[m * block : (m + 1) * block]

    def feed_grads():
        grads_into(
            r.grads_b,
            r.hidden,
            r.buf_b[...].reshape(z.tokens, D),
            z.block,
            D,
        )
        for k in range(3):
            grad_start(k)
        grads_into_blocks(r.grads_a, r.buf_a, r.grad_up, z.hidden)

    def grads_into_blocks(place, lhs4, rhs, width):
        for o in range(B):
            left = lhs4[:, :, :, o * z.block : (o + 1) * z.block].reshape(z.tokens, z.block)
            place[o // 2, o % 2, :, :width] = tn(left, rhs[:, :width]).astype(bf16)

    pipeline(
        {
            0: [(weight_pass, 10)],
            1: [(weight_pass, 11)],
            2: [(weight_pass, 12)],
            4: [(weight_pass, 13)],
            9: [(grad_pass, 0), (grad_start, 3)],
            10: [(grad_pass, 1), (grad_start, 4)],
            11: [(grad_pass, 2), (grad_start, 5)],
        },
        (0, self_forward),
        (1, lambda i: sum_pass(0, i)),
        (2, after_self),
        (3, lambda i: gather_pass(r.buf_a, i)),
        (4, feed),
        (4, lambda i: at(i, n - 1, feed_grads)),
        (5, lambda i: (sum_pass(0, i), sum_pass(1, i))),
        (6, after_feed),
        (7, lambda i: gather_pass(r.buf_b2, i)),
        (8, self_back),
    )

    r.grad_up[:, C : 2 * C] = r.grad_key[:, : z.tokens].T.astype(bf16)
    r.grad_up[:, 2 * C : 3 * C] = r.grad_value[:, : z.tokens].T.astype(bf16)

    clear_keys()

    def self_down(i):
        sum_start(0, i, nt(r.grad_up[chunk(i), : 3 * C], W[QKV][...].reshape(D, 3 * C)))

        @functools.partial(at, i, 0)
        def _():
            value = tn(r.att2[...], r.buf_b2[...].reshape(z.tokens, D)).astype(bf16)
            r.grads_c[1] = value.reshape(2, z.block, D)

        @functools.partial(at, i, n - 1)
        def _():
            grads_into_blocks(r.grads_b, r.buf_h2, r.grad_up, 3 * C)

    def after_self_down(i):
        grad, shift, scale = norm_backward(r.x1[i], mod(3), sum_end(0, i))
        keep_sums(2, shift, scale)
        grad = r.x2[i] + grad
        r.x2[i] = grad
        r.buf_b[i, s] = grad.astype(bf16)
        gather_start(r.buf_b, i)

    def cross_back(i):
        gather_wait(r.buf_b, i)
        grad = nt(r.buf_b[i].reshape(rows, D), W[OC][...].reshape(C, D)).astype(bf16)
        attend_back(i, *cross, grad, mask_rows, r.hidden)
        sum_start(0, i, nt(r.hidden[chunk(i), :C], W[Q][...].reshape(D, C)))

    def after_cross_back(i):
        grad, shift, scale = norm_backward(r.x0[i].astype(f32), mod(1), sum_end(0, i))
        keep_sums(0, shift, scale)
        r.x2[i] += grad

    def last_grads():
        value = tn(r.att1[...], r.buf_b[...].reshape(z.tokens, D)).astype(bf16)
        r.grads_c[0] = value.reshape(2, z.block, D)
        grad_start(11)
        for o in range(B):
            left = r.normed1[:, o * z.block : (o + 1) * z.block]
            r.grads_a[o // 2, o % 2, :, :C] = tn(left, r.hidden[:, :C]).astype(bf16)
        grad_start(12)
        for side, rest in enumerate((r.grad_key[...], r.grad_value[...])):
            total = None
            for _ in range(3):
                term = rest.astype(bf16)
                rest = rest - term.astype(f32)
                product_term = nn(term[:, : z.whole_rows], r.image_all[: z.whole_rows, :])
                product_term = product_term + nn(term[:, z.whole_rows :], r.tail[...])
                total = product_term if total is None else total + product_term
            value = total.T.astype(bf16)
            for o in range(B):
                r.grads_a[o // 2, o % 2, : z.image_block, C + side * C : C + (side + 1) * C] = value[
                    o * z.image_block : (o + 1) * z.image_block
                ]
        grad_start(13)

    pipeline(
        {
            0: [(grad_pass, 3), (grad_start, 6), (grad_end, 0)],
            1: [(grad_pass, 4), (grad_start, 7), (grad_end, 1)],
            3: [(grad_pass, 5), (grad_start, 8)],
            4: [(grad_pass, 6), (grad_end, 2), (grad_start, 9)],
            5: [(grad_pass, 7), (grad_end, 3), (grad_start, 10)],
            6: [(grad_pass, 8), (grad_end, 4), (grad_end, 5)],
            7: [(grad_turn, 8), (grad_pass, 9), (grad_end, 6), (grad_relay, 0), (grad_relay, 1)],
            8: [(grad_pass, 10), (grad_end, 7), (grad_relay, 2), (grad_relay, 3)],
            9: [(grad_end, 8), (grad_end, 9), (grad_relay, 4), (grad_relay, 5)],
        },
        (0, self_down),
        (1, lambda i: sum_pass(0, i)),
        (2, after_self_down),
        (3, lambda i: gather_pass(r.buf_b, i)),
        (4, cross_back),
        (4, lambda i: at(i, n - 1, last_grads)),
        (5, lambda i: sum_pass(0, i)),
        (6, after_cross_back),
    )
    grad_copy = pltpu.make_async_copy(r.x2, r.grad_tokens, r.sem_out.at[0])
    grad_copy.start()

    def sums_send(j):
        return remote(
            r.sums, r.sums_seq.at[s], r.sem_d_s.at[j - 1], r.sem_d_r.at[s], (b, lax.rem(s + j, S))
        )

    for j in range(1, S):
        sums_send(j).start()
    run([(grad_pass, 11), (grad_end, 10)])
    total = r.sums[...]
    for j in range(1, S):
        k = lax.rem(s + j, S)
        arrived(r.sums_seq.at[k], r.sem_d_s.at[0], r.sem_d_r.at[k], (b, k))
        total = total + r.sums_seq[k]
    r.mods_all[b] = total

    def table_send(j):
        return remote(
            r.mods_all.at[b],
            r.mods_all.at[b],
            r.sem_t_s.at[j - 1],
            r.sem_t_r.at[b],
            (lax.rem(b + j, B), s),
        )

    for j in range(1, B):
        table_send(j).start()
    run([(grad_pass, 12), (grad_turn, 11), (grad_pass, 13)])
    for j in range(1, B):
        k = lax.rem(b + j, B)
        arrived(r.mods_all.at[k], r.sem_t_s.at[0], r.sem_t_r.at[k], (k, s))
    table_copy = pltpu.make_async_copy(r.mods_all, r.table, r.sem_out.at[1])
    table_copy.start()
    run([(grad_end, 11), (grad_end, 12), (grad_end, 13)])
    run([(grad_relay, k) for k in range(6, len(SCATTER))])
    for j in range(1, S):
        sums_send(j).wait_send()
    for j in range(1, B):
        table_send(j).wait_send()
    for k in range(len(GATHER)):
        weight_drain(k)
    for k in range(len(SCATTER)):
        grad_drain(k)
    for i in range(n):
        output_copy(i).wait()
    grad_copy.wait()
    table_copy.wait()


def layer_call(z, args):
    n, part, D, C, S, B = z.chunks, z.part, z.width, z.columns, z.seq, z.batch
    Z = B // 2
    own = (n, part, D)
    full = (n, S, part, D)
    vmem = pltpu.VMEM
    dma = pltpu.SemaphoreType.DMA
    weights = [
        vmem((2, z.block, D) if w in BY_ROWS else (B,) + shape, bf16)
        for w, shape in enumerate(z.weights)
    ]
    firsts = [
        vmem((z.block, D) if w in BY_ROWS else (Z,) + shape, bf16)
        for w, shape in enumerate(z.weights)
    ]
    seconds = [vmem((Z - 1,) + shape, bf16) for shape in z.weights]
    lane = [
        vmem((n, 2, 2, part, D), bf16),
        vmem((n, 2, part, D), bf16),
        vmem((n, part, D), bf16),
        vmem((n, part, D), bf16),
    ]
    scratch = (
        weights
        + firsts
        + seconds
        + [vmem(full, bf16)] * 4
        + lane
        + lane
        + [
            vmem((Z,) + z.weights[OC], bf16),
            vmem((Z,) + z.weights[OS], bf16),
            vmem((S,) + z.weights[OC], bf16),
            vmem((S,) + z.weights[OS], bf16),
            vmem((z.image_rows, z.image_width), bf16),
            vmem((z.keys - z.whole_rows, z.image_width), bf16),
            vmem((1, z.image_rows), jnp.int32),
            vmem((8, z.keys), f32),
            vmem(args[5].shape, bf16),
            vmem((B, 8, D), f32),
            vmem((8, D), f32),
            vmem((8, D), f32),
            vmem((S, 8, D), f32),
            vmem((z.tokens, D), bf16),
            vmem((z.tokens, C), bf16),
            vmem((z.keys, C), bf16),
            vmem((z.keys, C), bf16),
            vmem((z.tokens, C), bf16),
            vmem((z.tokens, 3 * C), bf16),
            vmem((z.tokens, C), bf16),
            vmem((z.tokens, z.hidden), bf16),
            vmem((z.tokens, z.hidden), bf16),
            vmem((C, z.keys), f32),
            vmem((C, z.keys), f32),
            vmem(own, bf16),
            vmem(own, f32),
            vmem(own, f32),
            vmem((Z, 2, z.block, D), bf16),
            vmem((Z, 2, z.block, D), bf16),
            vmem((2, 2, z.block, D), bf16),
            dma((33,)),
            dma((len(GATHER), 3)),
            dma((len(GATHER), Z)),
            dma((len(GATHER), Z)),
            dma((len(GATHER), Z)),
            dma((len(SCATTER),)),
            dma((len(SCATTER),)),
            dma((len(SCATTER), 3)),
            dma((len(SCATTER), Z)),
            dma((len(SCATTER), 3)),
            dma((len(SCATTER), 3)),
            dma((len(SCATTER),)),
            dma((2, S - 1)),
            dma((2, S)),
            dma((2, S - 1)),
            dma((2, S)),
            dma((2, 3)),
            dma((2, 3)),
            dma((n, 3)),
            dma((n, 3)),
            dma((2, n, 2)),
            dma((2, n, 2)),
            dma((B - 1,)),
            dma((B,)),
            dma((S - 1,)),
            dma((S,)),
            dma((B - 1,)),
            dma((B,)),
            dma((2 + n,)),
        ]
    )
    shape = jax.ShapeDtypeStruct
    outs = [shape(own, bf16), shape(own, f32), shape((B, 8, D), f32)] + [
        shape((S,) + size, bf16) for size in z.weights
    ]
    anywhere = pl.BlockSpec(memory_space=pl.ANY)
    scalars = pl.BlockSpec(memory_space=pltpu.SMEM)
    return pl.pallas_call(
        functools.partial(whole_layer, z),
        out_shape=outs,
        in_specs=[anywhere] * 4 + [scalars] + [anywhere] * (len(args) - 5),
        out_specs=[anywhere] * len(outs),
        scratch_shapes=scratch,
        compiler_params=pltpu.CompilerParams(
            collective_id=0, has_side_effects=True, vmem_limit_bytes=LIMIT
        ),
        name="whole_layer",
    )(*args)


def finish(z, camera, output, grad_tokens, table, *refs):
    grads, outs = refs[:7], refs[7:]
    gate_t = refs[-1]
    step = pl.program_id(0)
    outs[0][...] = output[...]
    outs[1][...] = grad_tokens[...]

    @pl.when(step == 0)
    def _():
        own = camera[...].astype(f32)
        gate_t[...] = (own * jax.nn.sigmoid(own)).astype(bf16).astype(f32).T

    lanes = z.block // z.seq
    gate = gate_t[pl.ds(pl.multiple_of(step * lanes, 8), lanes), :]
    for k in range(6):
        outs[2][:, k * z.width : (k + 1) * z.width] = jnp.dot(
            gate, table[:, k, :], precision=highest, preferred_element_type=f32
        )

    def across(w, out, groups):
        width = grads[w].shape[2] // groups
        for j in range(z.seq):
            for g in range(groups):
                column = (g * z.seq + j) * width
                out[:, column : column + width] = grads[w][j, :, g * width : (g + 1) * width].astype(f32)

    across(Q, outs[3], 1)
    across(KV, outs[4], 2)
    outs[5][...] = grads[OC][0].astype(f32)
    across(QKV, outs[6], 3)
    outs[7][...] = grads[OS][0].astype(f32)
    across(UP, outs[8], z.batch)
    outs[9][...] = grads[DOWN][0].astype(f32)


def finish_call(z, camera, output, grad_tokens, table, *grads):
    S, D = z.seq, z.width
    n = z.chunks // S
    few = z.block // S
    few_image = z.image_block // S
    own = pl.BlockSpec((n, z.part, D), lambda i: (i, 0, 0))
    whole = pl.BlockSpec(table.shape, lambda i: (0, 0, 0))

    def quarter(w):
        if w in (OC, OS, DOWN):
            return pl.BlockSpec((1,) + grads[w].shape[1:], lambda i: (i, 0, 0))
        return pl.BlockSpec((S, grads[w].shape[1] // S, grads[w].shape[2]), lambda i: (0, i, 0))

    def rows(count, width):
        return pl.BlockSpec((count, width), lambda i: (i, 0))

    sizes = (
        (few, z.block, 6 * D),
        (few, z.block, D),
        (few_image, z.image_block, 2 * D),
        (few, z.block, D),
        (few, z.block, 3 * D),
        (few, z.block, D),
        (few, z.block, S * z.hidden),
        (z.hidden // z.batch, S * z.hidden // z.batch, D),
    )
    results = pl.pallas_call(
        functools.partial(finish, z),
        grid=(S,),
        out_shape=[
            jax.ShapeDtypeStruct(output.shape, bf16),
            jax.ShapeDtypeStruct(grad_tokens.shape, f32),
        ]
        + [jax.ShapeDtypeStruct((count, width), f32) for _, count, width in sizes],
        in_specs=[pl.BlockSpec(camera.shape, lambda i: (0, 0)), own, own, whole]
        + [quarter(w) for w in range(7)],
        out_specs=[own, own] + [rows(block, width) for block, _, width in sizes],
        scratch_shapes=[pltpu.VMEM((camera.shape[1], camera.shape[0]), f32)],
        compiler_params=pltpu.CompilerParams(vmem_limit_bytes=LIMIT),
        name="finish",
    )(camera, output, grad_tokens, table, *grads)
    output, grad_tokens, *rest = results
    return (output.reshape(1, z.own, D), grad_tokens.reshape(1, z.own, D), *rest)


def local_kernel(sizes, *inputs):
    (
        tokens,
        cotangent,
        image_tokens,
        image_lengths,
        key_mask,
        camera,
        modulation,
        q_cross,
        kv_image,
        out_cross,
        qkv_self,
        out_self,
        mlp_in,
        mlp_out,
    ) = inputs
    z = sizes
    n, part, D, C, S, B = z.chunks, z.part, z.width, z.columns, z.seq, z.batch
    results = layer_call(
        z,
        (
            tokens[0].reshape(n, part, D),
            cotangent[0].reshape(n, part, D),
            image_tokens[0],
            key_mask,
            image_lengths,
            camera,
            modulation,
            q_cross,
            kv_image,
            out_cross,
            qkv_self,
            out_self,
            mlp_in,
            mlp_out,
        ),
    )
    return finish_call(z, camera, *results)


def fits(mesh, inputs):
    batch, seq = mesh.shape["batch"], mesh.shape["seq"]
    own, width = inputs[0].shape[1:]
    return (
        batch == 8
        and seq == 4
        and own % 64 == 0
        and width == HEADS * HEAD_DIM
        and (width // seq) % 128 == 0
        and (inputs[12].shape[1] // seq // batch) % 128 == 0
    )


def choose(mesh, *inputs):
    if not fits(mesh, inputs):
        return local(*inputs)
    return local_kernel(Sizes(mesh.shape, inputs), *inputs)


def solution(mesh):
    return jax.shard_map(
        functools.partial(choose, mesh),
        mesh=mesh,
        in_specs=(
            P("batch", "seq", None),
            P("batch", "seq", None),
            P("batch", None, None),
            P("batch"),
            P("batch", None),
            P(None, "batch"),
            P("batch", None),
            P("batch", None),
            P("batch", None),
            P("batch", None),
            P("batch", None),
            P("batch", None),
            P("batch", None),
            P("batch", None),
        ),
        out_specs=(
            P("batch", "seq", None),
            P("batch", "seq", None),
            P("batch", None),
            P("batch", None),
            P("batch", None),
            P("batch", None),
            P("batch", None),
            P("batch", None),
            P("batch", None),
            P("batch", None),
        ),
        check_vma=False,
    )
```

```python
import functools

import jax
import jax.numpy as jnp
from jax import lax
from jax.experimental import pallas as pl
from jax.experimental.pallas import tpu as pltpu
from jax.sharding import PartitionSpec as P

HEADS = 16
HEAD_DIM = 64


epsilon = 1e-06
group_heads = 4
highest = lax.Precision.HIGHEST
LIMIT = 64 * 1024 * 1024 - 64 * 1024


def modulated_norm(values, shift, scale):
    center = values - jnp.mean(values, axis=-1, keepdims=True)
    normed = center * lax.rsqrt(jnp.mean(center * center, axis=-1, keepdims=True) + epsilon)
    return normed * (1.0 + scale) + shift


def product(left, right):
    return jnp.dot(left, right, preferred_element_type=jnp.float32)


def contract_rows(left, right):
    return lax.dot_general(
        left, right, (((0,), (0,)), ((), ())), preferred_element_type=jnp.float32
    )


def times_transposed(left, right):
    return lax.dot_general(
        left, right, (((1,), (1,)), ((), ())), preferred_element_type=jnp.float32
    )


def split_heads(values):
    rows = values.shape[0]
    grouped = values.reshape(rows, HEADS // group_heads, group_heads, HEAD_DIM)
    return grouped.transpose(1, 2, 0, 3)


def join_heads(values):
    groups, inner, rows, depth = values.shape
    return values.transpose(2, 0, 1, 3).reshape(rows, groups * inner * depth)


def scores_of(query_group, key_group, valid):
    scores = jnp.einsum(
        "hqd,hkd->hqk", query_group, key_group, preferred_element_type=jnp.float32
    ) * HEAD_DIM ** (-0.5)
    return jnp.where(valid[None, None, :], scores, -1000000000.0)


def attend_forward(query, key_rows, value_rows, valid):

    def one_group(pieces):
        query_group, key_group, value_group = pieces
        scores = scores_of(query_group, key_group, valid)
        top = jnp.max(scores, axis=-1, keepdims=True)
        expo = jnp.exp(scores - top)
        total = jnp.sum(expo, axis=-1, keepdims=True)
        probs = (expo / total).astype(jnp.bfloat16)
        result = jnp.einsum("hqk,hkd->hqd", probs, value_group, preferred_element_type=jnp.float32)
        return (result, top, total)

    results, tops, totals = lax.map(
        one_group, (split_heads(query), split_heads(key_rows), split_heads(value_rows))
    )
    return (join_heads(results), (tops, totals))


def attend_backward(query, key_rows, value_rows, valid, stats, grad_output):
    tops, totals = stats

    def one_group(pieces):
        query_group, key_group, value_group, top, total, grad_group = pieces
        scores = scores_of(query_group, key_group, valid)
        probs = jnp.exp(scores - top) / total
        grad_probs = jnp.einsum(
            "hqd,hkd->hqk", grad_group, value_group, preferred_element_type=jnp.float32
        )
        inner = jnp.sum(probs * grad_probs, axis=-1, keepdims=True)
        grad_scores = (probs * (grad_probs - inner)).astype(jnp.bfloat16)
        factor = HEAD_DIM ** (-0.5)
        grad_query = (
            jnp.einsum("hqk,hkd->hqd", grad_scores, key_group, preferred_element_type=jnp.float32)
            * factor
        )
        grad_keys = (
            jnp.einsum("hqk,hqd->hkd", grad_scores, query_group, preferred_element_type=jnp.float32)
            * factor
        )
        grad_values = jnp.einsum(
            "hqk,hqd->hkd",
            probs.astype(jnp.bfloat16),
            grad_group,
            preferred_element_type=jnp.float32,
        )
        return (grad_query, inner, grad_keys, grad_values)

    results = lax.map(
        one_group,
        (
            split_heads(query),
            split_heads(key_rows),
            split_heads(value_rows),
            tops,
            totals,
            split_heads(grad_output),
        ),
    )
    return (join_heads(results[0]), results[1], join_heads(results[2]), join_heads(results[3]))


def local(
    tokens,
    cotangent,
    image_tokens,
    image_lengths,
    key_mask,
    camera,
    modulation,
    q_cross,
    kv_image,
    out_cross,
    qkv_self,
    out_self,
    mlp_in,
    mlp_out,
):
    q_full, kv_full, out_cross_full, qkv_full, out_self_full, mlp_in_full, mlp_out_full = (
        lax.all_gather(q_cross, "batch", axis=0, tiled=True),
        lax.all_gather(kv_image, "batch", axis=0, tiled=True),
        lax.all_gather(out_cross, "batch", axis=0, tiled=True),
        lax.all_gather(qkv_self, "batch", axis=0, tiled=True),
        lax.all_gather(out_self, "batch", axis=0, tiled=True),
        lax.all_gather(mlp_in, "batch", axis=0, tiled=True),
        lax.all_gather(mlp_out, "batch", axis=0, tiled=True),
    )
    camera_gate = jax.nn.silu(camera.astype(jnp.float32)).astype(jnp.bfloat16)
    modulation_all = lax.psum(product(camera_gate, modulation), "batch")
    object_index = lax.axis_index("batch")
    width = tokens.shape[2]
    shifts = lax.dynamic_index_in_dim(modulation_all, object_index, 0, keepdims=False).reshape(
        6, width
    )
    stream = tokens[0].astype(jnp.float32)
    image_rows = image_tokens[0]
    positions = jnp.arange(image_rows.shape[0], dtype=jnp.int32)
    valid = (positions < image_lengths[0]) & ((key_mask[0] == 1) | (positions == 0))
    everywhere = jnp.ones((lax.axis_size("seq") * stream.shape[0],), dtype=jnp.bool_)
    normed_cross, cross_pullback = jax.vjp(modulated_norm, stream, shifts[0], shifts[1])
    normed_cross = normed_cross.astype(jnp.bfloat16)
    query_cross = product(normed_cross, q_full).astype(jnp.bfloat16)
    image_kv = product(image_rows, kv_full)
    image_keys = image_kv[:, :width].astype(jnp.bfloat16)
    image_values = image_kv[:, width:].astype(jnp.bfloat16)
    attended_cross, cross_stats = attend_forward(query_cross, image_keys, image_values, valid)
    attended_cross = attended_cross.astype(jnp.bfloat16)
    after_cross = stream + product(attended_cross, out_cross_full)
    normed_self, self_pullback = jax.vjp(modulated_norm, after_cross, shifts[2], shifts[3])
    normed_self = normed_self.astype(jnp.bfloat16)
    packed = product(normed_self, qkv_full).astype(jnp.bfloat16)
    query_self = packed[:, :width]
    key_local = packed[:, width : 2 * width]
    value_local = packed[:, 2 * width :]
    key_whole, value_whole = (
        lax.all_gather(key_local, "seq", axis=0, tiled=True),
        lax.all_gather(value_local, "seq", axis=0, tiled=True),
    )
    attended_self, self_stats = attend_forward(query_self, key_whole, value_whole, everywhere)
    attended_self = attended_self.astype(jnp.bfloat16)
    after_self = after_cross + product(attended_self, out_self_full)
    normed_mlp, mlp_pullback = jax.vjp(modulated_norm, after_self, shifts[4], shifts[5])
    normed_mlp = normed_mlp.astype(jnp.bfloat16)
    up_rows = product(normed_mlp, mlp_in_full)
    hidden, gelu_pullback = jax.vjp(jax.nn.gelu, up_rows)
    hidden = hidden.astype(jnp.bfloat16)
    output = after_self + product(hidden, mlp_out_full)
    grad_stream = cotangent[0].astype(jnp.float32)
    grad_branch = grad_stream.astype(jnp.bfloat16)
    grad_mlp_out = contract_rows(hidden, grad_branch)
    (grad_up,) = gelu_pullback(times_transposed(grad_branch, mlp_out_full))
    grad_up = grad_up.astype(jnp.bfloat16)
    grad_mlp_in = contract_rows(normed_mlp, grad_up)
    grad_from, shift_mlp, scale_mlp = mlp_pullback(times_transposed(grad_up, mlp_in_full))
    grad_stream = grad_stream + grad_from
    grad_branch = grad_stream.astype(jnp.bfloat16)
    grad_out_self = contract_rows(attended_self, grad_branch)
    grad_attended = times_transposed(grad_branch, out_self_full).astype(jnp.bfloat16)
    grad_query, inner_local, key_terms, value_terms = attend_backward(
        query_self, key_whole, value_whole, everywhere, self_stats, grad_attended
    )
    grad_key, grad_value = (
        lax.psum_scatter(key_terms, "seq", scatter_dimension=0, tiled=True),
        lax.psum_scatter(value_terms, "seq", scatter_dimension=0, tiled=True),
    )
    grad_packed = jnp.concatenate([grad_query, grad_key, grad_value], axis=1).astype(jnp.bfloat16)
    grad_qkv_self = contract_rows(normed_self, grad_packed)
    grad_from, shift_self, scale_self = self_pullback(times_transposed(grad_packed, qkv_full))
    grad_stream = grad_stream + grad_from
    grad_branch = grad_stream.astype(jnp.bfloat16)
    grad_out_cross = contract_rows(attended_cross, grad_branch)
    grad_attended = times_transposed(grad_branch, out_cross_full).astype(jnp.bfloat16)
    grad_query, inner_cross, key_terms, value_terms = attend_backward(
        query_cross, image_keys, image_values, valid, cross_stats, grad_attended
    )
    image_float = image_rows.astype(jnp.float32)
    image_key_grad, image_value_grad = (
        lax.psum_scatter(
            key_terms.astype(jnp.bfloat16), "seq", scatter_dimension=1, tiled=True
        ).astype(jnp.float32),
        lax.psum_scatter(
            value_terms.astype(jnp.bfloat16), "seq", scatter_dimension=1, tiled=True
        ).astype(jnp.float32),
    )
    block_width = image_key_grad.shape[1]
    column_start = lax.axis_index("seq") * block_width
    image_grads = jnp.concatenate([image_key_grad, image_value_grad], axis=1)
    kv_block = lax.dot_general(
        image_float,
        image_grads,
        (((0,), (0,)), ((), ())),
        precision=highest,
        preferred_element_type=jnp.float32,
    )
    grad_kv_image = jnp.zeros((image_rows.shape[1], 2 * width), jnp.float32)
    grad_kv_image = lax.dynamic_update_slice(
        grad_kv_image, kv_block[:, :block_width], (jnp.int32(0), column_start)
    )
    grad_kv_image = lax.dynamic_update_slice(
        grad_kv_image, kv_block[:, block_width:], (jnp.int32(0), column_start + width)
    )
    grad_query = grad_query.astype(jnp.bfloat16)
    grad_q_cross = contract_rows(normed_cross, grad_query)
    grad_from, shift_cross, scale_cross = cross_pullback(times_transposed(grad_query, q_full))
    grad_input = grad_stream + grad_from
    grad_row = jnp.concatenate(
        [shift_cross, scale_cross, shift_self, scale_self, shift_mlp, scale_mlp]
    )
    grad_table = lax.dynamic_update_slice(
        jnp.zeros(modulation_all.shape, jnp.float32),
        grad_row[None, :],
        (object_index, jnp.int32(0)),
    )
    grad_table = lax.psum(grad_table, ("batch", "seq"))
    grad_modulation = lax.dot_general(
        camera_gate.astype(jnp.float32),
        grad_table,
        (((0,), (0,)), ((), ())),
        precision=highest,
        preferred_element_type=jnp.float32,
    )
    terms = (
        grad_q_cross,
        grad_kv_image,
        grad_out_cross,
        grad_qkv_self,
        grad_out_self,
        grad_mlp_in,
        grad_mlp_out,
    )
    shares = (
        lax.psum_scatter(
            terms[0].astype(jnp.bfloat16), "batch", scatter_dimension=0, tiled=True
        ).astype(jnp.float32),
        lax.psum_scatter(
            terms[1].astype(jnp.bfloat16), "batch", scatter_dimension=0, tiled=True
        ).astype(jnp.float32),
        lax.psum_scatter(
            terms[2].astype(jnp.bfloat16), "batch", scatter_dimension=0, tiled=True
        ).astype(jnp.float32),
        lax.psum_scatter(
            terms[3].astype(jnp.bfloat16), "batch", scatter_dimension=0, tiled=True
        ).astype(jnp.float32),
        lax.psum_scatter(
            terms[4].astype(jnp.bfloat16), "batch", scatter_dimension=0, tiled=True
        ).astype(jnp.float32),
        lax.psum_scatter(
            terms[5].astype(jnp.bfloat16), "batch", scatter_dimension=0, tiled=True
        ).astype(jnp.float32),
        lax.psum_scatter(
            terms[6].astype(jnp.bfloat16), "batch", scatter_dimension=0, tiled=True
        ).astype(jnp.float32),
    )
    totals = (
        lax.psum(shares[0].astype(jnp.bfloat16), "seq").astype(jnp.float32),
        lax.psum(shares[1].astype(jnp.bfloat16), "seq").astype(jnp.float32),
        lax.psum(shares[2].astype(jnp.bfloat16), "seq").astype(jnp.float32),
        lax.psum(shares[3].astype(jnp.bfloat16), "seq").astype(jnp.float32),
        lax.psum(shares[4].astype(jnp.bfloat16), "seq").astype(jnp.float32),
        lax.psum(shares[5].astype(jnp.bfloat16), "seq").astype(jnp.float32),
        lax.psum(shares[6].astype(jnp.bfloat16), "seq").astype(jnp.float32),
    )
    return (
        output.astype(jnp.bfloat16)[None],
        grad_input[None],
        grad_modulation,
        totals[0],
        totals[1],
        totals[2],
        totals[3],
        totals[4],
        totals[5],
        totals[6],
    )


bf16 = jnp.bfloat16
f32 = jnp.float32
MESH = pl.DeviceIdType.MESH
BELOW = -3.0e38


def nn(a, b):
    return jnp.dot(a, b, preferred_element_type=f32)


def nt(a, b):
    return lax.dot_general(a, b, (((1,), (1,)), ((), ())), preferred_element_type=f32)


def tn(a, b):
    return lax.dot_general(a, b, (((0,), (0,)), ((), ())), preferred_element_type=f32)


def one_head(pair, side):
    lane = lax.broadcasted_iota(jnp.int32, pair.shape, 1)
    return jnp.where(lane // HEAD_DIM == side, pair, jnp.zeros_like(pair))


def two_heads(first, second):
    lane = lax.broadcasted_iota(jnp.int32, first.shape, 1)
    return jnp.where(lane < HEAD_DIM, first, second)


def softmax_rows(scores, mask):
    if mask is not None:
        scores = jnp.where(mask[0:1, :] > 0.5, scores, mask[1:2, :])
    expo = jnp.exp(scores - jnp.max(scores, axis=-1, keepdims=True))
    return expo * (1.0 / jnp.sum(expo, axis=-1, keepdims=True))


def norm_stats(rows):
    center = rows - jnp.mean(rows, axis=-1, keepdims=True)
    inverse = lax.rsqrt(jnp.mean(center * center, axis=-1, keepdims=True) + epsilon)
    return center * inverse, inverse


def norm_forward(rows, shift, scale):
    return norm_stats(rows)[0] * (1.0 + scale) + shift


def norm_backward(rows, scale, grad):
    normed, inverse = norm_stats(rows)
    inner = grad * (1.0 + scale)
    mean_inner = jnp.mean(inner, axis=-1, keepdims=True)
    mean_cross = jnp.mean(inner * normed, axis=-1, keepdims=True)
    grad_rows = inverse * (inner - mean_inner - normed * mean_cross)
    return (
        grad_rows,
        jnp.sum(grad, axis=0, keepdims=True),
        jnp.sum(grad * normed, axis=0, keepdims=True),
    )


Q, KV, OC, QKV, OS, UP, DOWN, CAMERA, TABLE, TOKENS, OWN, IMAGE, COTANGENT = range(13)


GATHER = (
    (KV, 0, 1),
    (Q, 0, 1),
    (OC, 0, 1),
    (QKV, 0, 2),
    (QKV, 1, 2),
    (OS, 0, 1),
    (UP, 0, 4),
    (UP, 1, 4),
    (UP, 2, 4),
    (UP, 3, 4),
    (DOWN, 0, 4),
    (DOWN, 1, 4),
    (DOWN, 2, 4),
    (DOWN, 3, 4),
)
SCATTER = (
    (DOWN, 0, 4),
    (DOWN, 1, 4),
    (DOWN, 2, 4),
    (DOWN, 3, 4),
    (UP, 0, 4),
    (UP, 1, 4),
    (UP, 2, 4),
    (UP, 3, 4),
    (OS, 0, 1),
    (QKV, 0, 2),
    (QKV, 1, 2),
    (OC, 0, 1),
    (Q, 0, 1),
    (KV, 0, 1),
)
BY_ROWS = (OC, OS)
AHEAD = 2


class Sizes:
    def __init__(self, mesh_shape, inputs):
        self.batch, self.seq = mesh_shape["batch"], mesh_shape["seq"]
        self.own, self.width = inputs[0].shape[1:]
        self.image_rows, self.image_width = inputs[2].shape[1:]
        self.chunks = 4
        self.part = self.own // self.chunks
        self.rows = self.seq * self.part
        self.tokens = self.seq * self.own
        self.columns = self.width // self.seq
        self.hidden = inputs[12].shape[1] // self.seq
        self.keys = -(-self.image_rows // 128) * 128
        self.whole_rows = self.image_rows // 128 * 128
        self.block = self.width // self.batch
        self.image_block = self.image_width // self.batch
        self.weights = (
            (self.block, self.columns),
            (self.image_block, 2 * self.columns),
            (self.block // self.seq, self.width),
            (self.block, 3 * self.columns),
            (self.block // self.seq, self.width),
            (self.block, self.hidden),
            (self.hidden // self.batch, self.width),
        )


class Refs:
    def __init__(self, refs):
        rest = iter(refs)
        self.tokens = next(rest)
        self.cotangent = next(rest)
        self.image = next(rest)
        self.marks = next(rest)
        self.lengths = next(rest)
        self.camera = next(rest)
        self.modulation = next(rest)
        self.q_cross = next(rest)
        self.kv_image = next(rest)
        self.out_cross = next(rest)
        self.qkv_self = next(rest)
        self.out_self = next(rest)
        self.mlp_in = next(rest)
        self.mlp_out = next(rest)
        self.output = next(rest)
        self.grad_tokens = next(rest)
        self.table = next(rest)
        self.gout = [next(rest) for _ in range(7)]
        self.weights = [next(rest) for _ in range(7)]
        self.firsts = [next(rest) for _ in range(7)]
        self.seconds = [next(rest) for _ in range(7)]
        self.buf_a = next(rest)
        self.buf_b = next(rest)
        self.buf_h2 = next(rest)
        self.buf_b2 = next(rest)
        self.part_main = next(rest)
        self.core_main = next(rest)
        self.send_main = next(rest)
        self.line_main = next(rest)
        self.part_side = next(rest)
        self.core_side = next(rest)
        self.send_side = next(rest)
        self.line_side = next(rest)
        self.turn_in = [next(rest) for _ in range(2)]
        self.turn_out = [next(rest) for _ in range(2)]
        self.image_all = next(rest)
        self.tail = next(rest)
        self.marks_own = next(rest)
        self.mask_all = next(rest)
        self.camera_own = next(rest)
        self.mods_all = next(rest)
        self.mods = next(rest)
        self.sums = next(rest)
        self.sums_seq = next(rest)
        self.normed1 = next(rest)
        self.query1 = next(rest)
        self.key1 = next(rest)
        self.value1 = next(rest)
        self.att1 = next(rest)
        self.packed2 = next(rest)
        self.att2 = next(rest)
        self.hidden = next(rest)
        self.grad_up = next(rest)
        self.grad_key = next(rest)
        self.grad_value = next(rest)
        self.x0 = next(rest)
        self.x1 = next(rest)
        self.x2 = next(rest)
        self.dx = next(rest)
        self.grads_a = next(rest)
        self.grads_b = next(rest)
        self.grads_c = next(rest)
        self.sem_load = next(rest)
        self.sem_wz_s = next(rest)
        self.sem_wz_r = next(rest)
        self.sem_wx_s = next(rest)
        self.sem_wx_r = next(rest)
        self.sem_gx_s = next(rest)
        self.sem_gx_r = next(rest)
        self.sem_gz_s = next(rest)
        self.sem_gz_r = next(rest)
        self.sem_gs_s = next(rest)
        self.sem_gs_r = next(rest)
        self.sem_own = next(rest)
        self.sem_ti_s = next(rest)
        self.sem_ti_r = next(rest)
        self.sem_to_s = next(rest)
        self.sem_to_r = next(rest)
        self.sem_in_s = next(rest)
        self.sem_in_r = next(rest)
        self.sem_ag_s = next(rest)
        self.sem_ag_r = next(rest)
        self.sem_rs_s = next(rest)
        self.sem_rs_r = next(rest)
        self.sem_m_s = next(rest)
        self.sem_m_r = next(rest)
        self.sem_d_s = next(rest)
        self.sem_d_r = next(rest)
        self.sem_t_s = next(rest)
        self.sem_t_r = next(rest)
        self.sem_out = next(rest)


def whole_layer(z, *refs):
    r = Refs(refs)
    W, FIRST, SECOND, GOUT = r.weights, r.firsts, r.seconds, r.gout
    n, S, B = z.chunks, z.seq, z.batch
    part, rows, D, C = z.part, z.rows, z.width, z.columns
    Z = B // 2
    b = lax.axis_index("batch")
    s = lax.axis_index("seq")
    zz = b // 2
    x = lax.rem(b, 2)
    y = s // 2
    c = lax.rem(s, 2)
    other_x = 1 - x
    other_c = 1 - c
    other_y = 1 - y
    x_peer = (2 * zz + other_x, s)
    core_peer = (b, 2 * y + other_c)
    line_peer = (b, 2 * other_y + c)
    line_slot = 2 * other_y + c
    core_slot = 2 * y + other_c
    far_slot = 2 * other_y + other_c

    def z_of(j):
        return lax.rem(zz + j, Z)

    def remote(src, dst, send, recv, device):
        return pltpu.make_async_remote_copy(
            src_ref=src,
            dst_ref=dst,
            send_sem=send,
            recv_sem=recv,
            device_id=device,
            device_id_type=MESH,
        )

    def arrived(dst, send, recv, device):
        remote(dst, dst, send, recv, device).wait_recv()

    barrier = pltpu.get_barrier_semaphore()
    for j in range(1, B):
        pl.semaphore_signal(barrier, inc=1, device_id=(lax.rem(b + j, B), s), device_id_type=MESH)
    for j in range(1, S):
        pl.semaphore_signal(barrier, inc=1, device_id=(b, lax.rem(s + j, S)), device_id_type=MESH)

    loads = {}

    def load(key, src, dst):
        count = sum(len(copies) for copies in loads.values())
        copy = pltpu.make_async_copy(src, dst, r.sem_load.at[count])
        loads.setdefault(key, []).append(copy)
        copy.start()

    def col(index, width):
        return pl.ds(pl.multiple_of(index * width, 128), width)

    wide = z.hidden // B
    for j in range(2):
        load(
            KV,
            r.kv_image.at[:, pl.ds(pl.multiple_of(j * D + s * C, 128), C)],
            W[KV].at[b, :, pl.ds(j * C, C)],
        )
    load(Q, r.q_cross.at[:, col(s, C)], W[Q].at[b])
    load(TOKENS, r.tokens, r.buf_a.at[:, s])
    load(CAMERA, r.camera, r.camera_own)
    for k in range(6):
        load(TABLE, r.modulation.at[:, pl.ds(k * D, D)], r.hidden.at[pl.ds(k * z.block, z.block)])
    few = z.block // S
    load(OC, r.out_cross.at[pl.ds(pl.multiple_of(s * few, 16), few)], r.turn_in[0].at[zz])
    for j in range(3):
        load(
            QKV,
            r.qkv_self.at[:, pl.ds(pl.multiple_of(j * D + s * C, 128), C)],
            W[QKV].at[b, :, pl.ds(j * C, C)],
        )
    load(OS, r.out_self.at[pl.ds(pl.multiple_of(s * few, 16), few)], r.turn_in[1].at[zz])
    load(IMAGE, r.image, r.image_all)
    load(IMAGE, r.marks, r.marks_own)
    for j in range(B):
        load(
            UP,
            r.mlp_in.at[:, pl.ds(pl.multiple_of(j * (z.hidden * S // B) + s * wide, 128), wide)],
            W[UP].at[b, :, pl.ds(j * wide, wide)],
        )
    load(DOWN, r.mlp_out.at[pl.ds(pl.multiple_of(s * wide, 128), wide), :], W[DOWN].at[b])
    load(COTANGENT, r.cotangent, r.buf_b.at[:, s])
    load(OWN, r.tokens, r.x0)

    pl.semaphore_wait(barrier, B - 1 + S - 1)

    def loaded(key):
        for copy in loads[key]:
            copy.wait()

    def rows_of(piece):
        w, which, parts = piece
        count = z.weights[w][0] // parts
        return w, pl.ds(which * count, count)

    def turned(w):
        return 0 if w == OC else 1

    def quarter(index):
        return pl.ds(pl.multiple_of(index * few, 16), few)

    def z_place(k, from_z):
        w, span = rows_of(GATHER[k])
        return r.turn_in[turned(w)].at[from_z] if w in BY_ROWS else W[w].at[2 * from_z + x, span]

    def z_send(k, j):
        place = z_place(k, zz)
        return remote(
            place, place, r.sem_wz_s.at[k, j - 1], r.sem_wz_r.at[k, zz], (2 * z_of(j) + x, s)
        )

    def x_send(k, from_z):
        w, span = rows_of(GATHER[k])
        place, mark = (W[w].at[x], 0) if w in BY_ROWS else (z_place(k, from_z), from_z)
        return remote(place, place, r.sem_wx_s.at[k, mark], r.sem_wx_r.at[k, mark], x_peer)

    def turn_send(w, j):
        to = lax.rem(s + j, S)
        return remote(
            r.turn_in[turned(w)].at[to],
            W[w].at[x, quarter(s)],
            r.sem_ti_s.at[turned(w), j - 1],
            r.sem_ti_r.at[turned(w), s],
            (b, to),
        )

    def z_near(j):
        return (zz != Z - 1) if j == 1 else (zz != 0)

    def z_far(k):
        place = z_place(k, z_of(2))
        return remote(
            place,
            place,
            r.sem_wz_s.at[k, Z - 1],
            r.sem_wz_r.at[k, z_of(2)],
            (2 * (Z - 1) * (zz - 1) + x, s),
        )

    def between():
        return (zz == 1) | (zz == 2)

    def weight_start(k):
        if k >= len(GATHER):
            return
        w, which, _ = GATHER[k]
        if which == 0:
            loaded(w)
        z_send(k, 2).start()
        for j in (1, 3):
            pl.when(z_near(j))(z_send(k, j).start)
        if w not in BY_ROWS:
            x_send(k, zz).start()

    def weight_came(k, j):
        w, _ = rows_of(GATHER[k])
        from_z = z_of(j)
        arrived(
            z_place(k, from_z), r.sem_wz_s.at[k, 0], r.sem_wz_r.at[k, from_z], (2 * from_z + x, s)
        )
        if w not in BY_ROWS:
            x_send(k, from_z).start()

    def weight_far(k):
        for j in (1, 3):
            pl.when(jnp.logical_not(z_near(j)))(functools.partial(weight_came, k, j))

    def weight_pass(k):
        w, _ = rows_of(GATHER[k])
        weight_came(k, 2)
        pl.when(between())(z_far(k).start)
        for j in (1, 3):
            pl.when(z_near(j))(functools.partial(weight_came, k, j))
        weight_start(k + AHEAD)
        if k and GATHER[k - 1][0] not in BY_ROWS:
            weight_far(k - 1)
        if w in BY_ROWS:
            weight_far(k)
            for j in range(1, S):
                turn_send(w, j).start()
            W[w][x, quarter(s), :] = r.turn_in[turned(w)][s]

    def weight_turn(k):
        w, _ = rows_of(GATHER[k])
        for j in range(1, S):
            m = lax.rem(s + j, S)
            arrived(
                W[w].at[x, quarter(m)], r.sem_ti_s.at[turned(w), 0], r.sem_ti_r.at[turned(w), m], (b, m)
            )
        x_send(k, zz).start()

    def weight_wait(w):
        for k in range(len(GATHER)):
            if GATHER[k][0] != w:
                continue
            _, span = rows_of(GATHER[k])
            if w in BY_ROWS:
                arrived(W[w].at[other_x], r.sem_wx_s.at[k, 0], r.sem_wx_r.at[k, 0], x_peer)
                continue
            for from_z in range(Z):
                place = W[w].at[2 * from_z + other_x, span]
                arrived(place, r.sem_wx_s.at[k, 0], r.sem_wx_r.at[k, from_z], x_peer)

    def weight_drain(k):
        w, _ = rows_of(GATHER[k])
        z_send(k, 2).wait_send()
        for j in (1, 3):
            pl.when(z_near(j))(z_send(k, j).wait_send)
        pl.when(between())(z_far(k).wait_send)
        if w in BY_ROWS:
            x_send(k, zz).wait_send()
            for j in range(1, S):
                turn_send(w, j).wait_send()
        else:
            for j in range(Z):
                x_send(k, z_of(j)).wait_send()

    def give(buf, i, k):
        slot, peer = [(s, core_peer), (s, line_peer), (line_slot, core_peer)][k]
        return remote(
            buf.at[i, slot], buf.at[i, slot], r.sem_ag_s.at[i, k], r.sem_ag_r.at[i, k], peer
        )

    def gather_start(buf, i):
        give(buf, i, 1).start()
        give(buf, i, 0).start()

    def gather_pass(buf, i):
        arrived(buf.at[i, line_slot], r.sem_ag_s.at[i, 1], r.sem_ag_r.at[i, 1], line_peer)
        give(buf, i, 2).start()

    def gather_wait(buf, i):
        arrived(buf.at[i, core_slot], r.sem_ag_s.at[i, 0], r.sem_ag_r.at[i, 0], core_peer)
        arrived(buf.at[i, far_slot], r.sem_ag_s.at[i, 2], r.sem_ag_r.at[i, 2], core_peer)
        for k in range(3):
            give(buf, i, k).wait_send()

    def give_input(buf, m, k):
        slot, peer = [(s, core_peer), (s, line_peer), (line_slot, core_peer)][k]
        return remote(
            buf.at[:, slot], buf.at[:, slot], r.sem_in_s.at[m, k], r.sem_in_r.at[m, k], peer
        )

    def input_start(buf, m):
        give_input(buf, m, 1).start()
        give_input(buf, m, 0).start()

    def input_pass(buf, m):
        arrived(buf.at[:, line_slot], r.sem_in_s.at[m, 1], r.sem_in_r.at[m, 1], line_peer)
        give_input(buf, m, 2).start()

    def input_wait(buf, m):
        arrived(buf.at[:, core_slot], r.sem_in_s.at[m, 0], r.sem_in_r.at[m, 0], core_peer)
        arrived(buf.at[:, far_slot], r.sem_in_s.at[m, 2], r.sem_in_r.at[m, 2], core_peer)
        for k in range(3):
            give_input(buf, m, k).wait_send()

    lanes = (
        (r.part_main, r.core_main, r.send_main, r.line_main),
        (r.part_side, r.core_side, r.send_side, r.line_side),
    )

    def sum_core(lane, i):
        mine, core, _, _ = lanes[lane]
        return remote(
            mine.at[i, :, other_c],
            core.at[i],
            r.sem_rs_s.at[lane, i, 0],
            r.sem_rs_r.at[lane, i, 0],
            core_peer,
        )

    def sum_line(lane, i):
        _, _, send, line = lanes[lane]
        return remote(
            send.at[i],
            line.at[i],
            r.sem_rs_s.at[lane, i, 1],
            r.sem_rs_r.at[lane, i, 1],
            line_peer,
        )

    def sum_start(lane, i, value):
        lanes[lane][0][i] = value.astype(bf16).reshape(2, 2, part, D)
        sum_core(lane, i).start()

    def sum_pass(lane, i):
        mine, core, send, _ = lanes[lane]
        sum_core(lane, i).wait_recv()
        send[i] = (mine[i, other_y, c].astype(f32) + core[i, other_y].astype(f32)).astype(bf16)
        sum_line(lane, i).start()

    def sum_end(lane, i):
        mine, core, _, line = lanes[lane]
        sum_line(lane, i).wait_recv()
        total = mine[i, y, c].astype(f32) + core[i, y].astype(f32) + line[i].astype(f32)
        sum_core(lane, i).wait_send()
        sum_line(lane, i).wait_send()
        return total

    def grad_place(w):
        return {
            Q: r.grads_a.at[:, :, :, pl.ds(0, C)],
            KV: r.grads_a.at[:, :, pl.ds(0, z.image_block), pl.ds(C, 2 * C)],
            OC: r.grads_c.at[0],
            QKV: r.grads_b.at[:, :, :, pl.ds(0, 3 * C)],
            OS: r.grads_c.at[1],
            UP: r.grads_a,
            DOWN: r.grads_b,
        }[w]

    def first_of(k):
        w, span = rows_of(SCATTER[k])
        return r.turn_out[turned(w)].at[zz] if w in BY_ROWS else FIRST[w].at[zz, span]

    def grad_x(k):
        w, span = rows_of(SCATTER[k])
        place = grad_place(w)
        src = place.at[other_x] if w in BY_ROWS else place.at[:, other_x, span]
        dst = FIRST[w] if w in BY_ROWS else FIRST[w].at[:, span]
        return remote(src, dst, r.sem_gx_s.at[k], r.sem_gx_r.at[k], x_peer)

    def turn_back(w, j):
        to = lax.rem(s + j, S)
        return remote(
            FIRST[w].at[quarter(to)],
            r.turn_out[turned(w)].at[s],
            r.sem_to_s.at[turned(w), j - 1],
            r.sem_to_r.at[turned(w), s],
            (b, to),
        )

    def grad_z(k, j):
        w, span = rows_of(SCATTER[k])
        to = z_of(j)
        src = r.turn_out[turned(w)].at[to] if w in BY_ROWS else FIRST[w].at[to, span]
        return remote(
            src,
            SECOND[w].at[Z - j - 1, span],
            r.sem_gz_s.at[k, j - 1],
            r.sem_gz_r.at[k, zz],
            (2 * to + x, s),
        )

    def shared(k, origin):
        w, span = rows_of(SCATTER[k])
        return GOUT[w].at[origin, span]

    def grad_s(k, way):
        mine = shared(k, line_slot) if way == 2 else first_of(k)
        origin = line_slot if way == 2 else s
        peer = line_peer if way == 1 else core_peer
        return remote(mine, shared(k, origin), r.sem_gs_s.at[k, way], r.sem_gs_r.at[k, way], peer)

    def grad_own(k):
        return pltpu.make_async_copy(first_of(k), shared(k, s), r.sem_own.at[k])

    def grad_relay(k):
        arrived(shared(k, line_slot), r.sem_gs_s.at[k, 1], r.sem_gs_r.at[k, 1], line_peer)
        grad_s(k, 2).start()

    def grad_start(k):
        grad_x(k).start()

    def grad_pass(k):
        w, span = rows_of(SCATTER[k])
        grad_x(k).wait_recv()
        place = grad_place(w)
        if w in BY_ROWS:
            FIRST[w][...] = (FIRST[w][...].astype(f32) + place[x].astype(f32)).astype(bf16)
            for j in range(1, S):
                turn_back(w, j).start()
            r.turn_out[turned(w)][s] = FIRST[w][quarter(s), :]
        else:
            for m in range(Z):
                term = FIRST[w][m, span].astype(f32) + place[m, x, span].astype(f32)
                FIRST[w][m, span] = term.astype(bf16)
            for j in range(1, Z):
                grad_z(k, j).start()
        grad_x(k).wait_send()

    def grad_turn(k):
        w, _ = rows_of(SCATTER[k])
        for j in range(1, S):
            m = lax.rem(s + j, S)
            arrived(
                r.turn_out[turned(w)].at[m],
                r.sem_to_s.at[turned(w), 0],
                r.sem_to_r.at[turned(w), m],
                (b, m),
            )
        for j in range(1, Z):
            grad_z(k, j).start()

    def grad_end(k):
        w, span = rows_of(SCATTER[k])
        mine = first_of(k)
        total = mine[...].astype(f32)
        for j in range(1, Z):
            m = z_of(j)
            term = SECOND[w].at[j - 1, span]
            arrived(term, r.sem_gz_s.at[k, 0], r.sem_gz_r.at[k, m], (2 * m + x, s))
            total = total + term[...].astype(f32)
        mine[...] = total.astype(bf16)
        grad_s(k, 1).start()
        grad_s(k, 0).start()
        grad_own(k).start()
        for j in range(1, Z):
            grad_z(k, j).wait_send()

    def grad_drain(k):
        w, _ = rows_of(SCATTER[k])
        arrived(shared(k, core_slot), r.sem_gs_s.at[k, 0], r.sem_gs_r.at[k, 0], core_peer)
        arrived(shared(k, far_slot), r.sem_gs_s.at[k, 2], r.sem_gs_r.at[k, 2], core_peer)
        for way in range(3):
            grad_s(k, way).wait_send()
        grad_own(k).wait()
        if w in BY_ROWS:
            for j in range(1, S):
                turn_back(w, j).wait_send()

    def mods_send(j):
        to = lax.rem(b + j, B)
        return remote(
            r.x2.at[0, pl.ds(pl.multiple_of(8 * to, 8), 8)],
            r.mods_all.at[b],
            r.sem_m_s.at[j - 1],
            r.sem_m_r.at[b],
            (to, s),
        )

    for k in range(AHEAD):
        weight_start(k)
    loaded(TOKENS)
    input_start(r.buf_a, 0)
    loaded(CAMERA)
    loaded(TABLE)
    camera = r.camera_own[...].astype(f32)
    gate = (camera * jax.nn.sigmoid(camera)).astype(bf16)
    for k in range(6):
        term = nn(gate, r.hidden[k * z.block : (k + 1) * z.block, :])
        for o in range(B):
            r.x2[0, 8 * o + k : 8 * o + k + 1, :] = term[o : o + 1, :]
    for j in range(1, B):
        mods_send(j).start()
    loaded(COTANGENT)
    input_start(r.buf_b, 1)
    loaded(IMAGE)
    loaded(OWN)
    places = lax.broadcasted_iota(jnp.int32, (1, z.image_rows), 1)
    valid = (places < r.lengths[0]) & ((r.marks_own[...] == 1) | (places == 0))
    places = lax.broadcasted_iota(jnp.int32, (1, z.keys), 1)
    r.mask_all[0:1, :] = jnp.zeros((1, z.keys), f32)
    r.mask_all[0:1, : z.image_rows] = jnp.where(valid, 1.0, 0.0)
    r.mask_all[1:2, :] = jnp.where(places < z.image_rows, -1000000000.0, BELOW)
    rest = z.image_rows - z.whole_rows
    last = r.image_all[z.whole_rows :, :]
    padding = jnp.zeros((z.keys - z.image_rows, z.image_width), bf16)
    r.tail[...] = jnp.concatenate([last, padding], axis=0) if rest else padding

    mods = r.x2[0, pl.ds(pl.multiple_of(8 * b, 8), 8)]
    for j in range(1, B):
        k = lax.rem(b + j, B)
        arrived(r.mods_all.at[k], r.sem_m_s.at[0], r.sem_m_r.at[k], (k, s))
        mods = mods + r.mods_all[k]
    r.mods[...] = mods
    for j in range(1, B):
        mods_send(j).wait_send()

    def mod(k):
        return r.mods[k : k + 1, :]

    def chunk(i):
        return pl.ds(pl.multiple_of(i * rows, rows), rows)

    scale_q = HEAD_DIM ** (-0.5)
    input_pass(r.buf_a, 0)
    weight_pass(0)
    weight_pass(1)
    input_wait(r.buf_a, 0)

    def normalize(i, _):
        rows_in = r.buf_a[i].reshape(rows, D).astype(f32)
        r.normed1[chunk(i), :] = norm_forward(rows_in, mod(0), mod(1)).astype(bf16)
        return 0

    lax.fori_loop(0, n, normalize, 0)
    weight_wait(KV)

    def project_rows(block, part_rows):
        both = nn(block, W[KV][...].reshape(z.image_width, 2 * C))
        r.key1[part_rows, :] = both[:, :C].astype(bf16)
        r.value1[part_rows, :] = both[:, C:].astype(bf16)

    def project_image(k, _):
        part_rows = pl.ds(pl.multiple_of(k * 128, 128), 128)
        project_rows(r.image_all[part_rows, :], part_rows)
        return 0

    lax.fori_loop(0, z.whole_rows // 128, project_image, 0)
    project_rows(r.tail[...], pl.ds(z.whole_rows, z.keys - z.whole_rows))
    weight_pass(2)
    weight_wait(Q)

    def project_query(i):
        query = nn(r.normed1[chunk(i), :], W[Q][...].reshape(D, C)).astype(bf16)
        r.query1[chunk(i), :] = (query * scale_q).astype(bf16)

    def attend(i, query, key, value, att, mask):
        for p in range(C // 128):
            lane = slice(128 * p, 128 * p + 128)
            pair = query(i, lane)
            keys, values = key(lane), value(lane)
            result = []
            for side in range(2):
                probs = softmax_rows(nt(one_head(pair, side), keys), mask).astype(bf16)
                result.append(nn(probs, values))
            att[chunk(i), lane] = two_heads(*result).astype(bf16)

    def attend_back(i, query, key, value, grad, mask, grad_query):
        query_t = query(i, slice(0, C)).T
        grad_t = grad.T
        for p in range(C // 128):
            lane = slice(128 * p, 128 * p + 128)
            pair, grad_pair = query(i, lane), grad[:, lane]
            keys, values = key(lane), value(lane)
            result = []
            for side in range(2):
                head = slice(128 * p + HEAD_DIM * side, 128 * p + HEAD_DIM * (side + 1))
                probs = softmax_rows(nt(one_head(pair, side), keys), mask)
                grad_probs = nt(one_head(grad_pair, side), values)
                inner = jnp.sum(probs * grad_probs, axis=-1, keepdims=True)
                scores = (probs * (grad_probs - inner)).astype(bf16)
                count = keys.shape[0]
                value_term = nn(grad_t[head, :], probs.astype(bf16))
                key_term = nn(query_t[head, :], scores)
                r.grad_value[head, :count] += value_term
                r.grad_key[head, :count] += key_term
                result.append(nn(scores, keys))
            grad_query[chunk(i), lane] = (two_heads(*result) * scale_q).astype(bf16)

    cross = (
        lambda i, lane: r.query1[chunk(i), lane],
        lambda lane: r.key1[:, lane],
        lambda lane: r.value1[:, lane],
    )

    def plus(lane, offset):
        return slice(lane.start + offset, lane.stop + offset)

    own = (
        lambda i, lane: r.packed2[chunk(i), lane],
        lambda lane: r.packed2[:, plus(lane, C)],
        lambda lane: r.packed2[:, plus(lane, 2 * C)],
    )
    mask_rows = r.mask_all

    def at(i, value, stage):
        pl.when(i == value)(stage)

    def run(calls):
        for call, *values in calls:
            call(*values)

    def pipeline(ticks, *stages):
        last = max(offset for offset, _ in stages)

        def body(step, _):
            for when, calls in ticks.items():
                at(step, when, functools.partial(run, calls))
            for offset, stage in stages:
                i = step - offset

                @pl.when((i >= 0) & (i < n))
                def _():
                    stage(i)

            return 0

        lax.fori_loop(0, n + last, body, 0)

    def cross_forward(i):
        project_query(i)
        attend(i, *cross, r.att1, mask_rows)
        at(i, 0, functools.partial(run, [(weight_turn, 2), (weight_wait, OC)]))
        sum_start(0, i, nn(r.att1[chunk(i), :], W[OC][...].reshape(C, D)))

    def after_cross(i):
        total = r.x0[i].astype(f32) + sum_end(0, i)
        r.x1[i] = total
        r.buf_h2[i, s] = norm_forward(total, mod(2), mod(3)).astype(bf16)
        gather_start(r.buf_h2, i)

    def project_self(i):
        at(i, 0, functools.partial(weight_wait, QKV))
        gather_wait(r.buf_h2, i)
        packed = nn(r.buf_h2[i].reshape(rows, D), W[QKV][...].reshape(D, 3 * C)).astype(bf16)
        r.packed2[chunk(i), :C] = (packed[:, :C] * scale_q).astype(bf16)
        r.packed2[chunk(i), C:] = packed[:, C:]

    pipeline(
        {
            1: [(weight_pass, 3)],
            2: [(weight_pass, 4)],
            3: [(weight_pass, 5)],
            4: [(weight_pass, 6)],
            5: [(weight_turn, 5), (weight_pass, 7)],
            6: [(weight_pass, 8)],
            7: [(weight_pass, 9)],
        },
        (0, cross_forward),
        (1, lambda i: sum_pass(0, i)),
        (2, after_cross),
        (3, lambda i: gather_pass(r.buf_h2, i)),
        (4, project_self),
    )

    weight_wait(OS)
    input_pass(r.buf_b, 1)
    input_wait(r.buf_b, 1)
    r.sums[...] = jnp.zeros_like(r.sums)

    def clear_keys():
        r.grad_key[...] = jnp.zeros_like(r.grad_key)
        r.grad_value[...] = jnp.zeros_like(r.grad_value)

    clear_keys()

    def output_copy(i):
        return pltpu.make_async_copy(
            r.part_side.at[i, 0, 0], r.output.at[i], r.sem_out.at[2 + i]
        )

    def self_forward(i):
        attend(i, *own, r.att2, None)
        sum_start(0, i, nn(r.att2[chunk(i), :], W[OS][...].reshape(C, D)))

    def after_self(i):
        total = r.x1[i] + sum_end(0, i)
        r.x2[i] = total
        r.buf_a[i, s] = norm_forward(total, mod(4), mod(5)).astype(bf16)
        gather_start(r.buf_a, i)

    def feed(i):
        at(i, 0, functools.partial(run, [(weight_far, 13), (weight_wait, UP), (weight_wait, DOWN)]))
        gather_wait(r.buf_a, i)
        rows_in = r.buf_a[i].reshape(rows, D)
        grad_out = r.buf_b[i].reshape(rows, D)
        up = W[UP]
        down = W[DOWN]
        forward = backward = None
        pieces = 2
        wide_piece = z.hidden // pieces
        for k in range(pieces):
            lane = slice(k * wide_piece, (k + 1) * wide_piece)
            up_piece = up[:, :, lane].reshape(D, wide_piece)
            down_piece = down[k * (B // pieces) : (k + 1) * (B // pieces)].reshape(wide_piece, D)
            u = nn(rows_in, up_piece)
            square = u * u
            root = 0.7978845608028654
            tanh = jnp.tanh(root * u * (1.0 + 0.044715 * square))
            half = 0.5 * (1.0 + tanh)
            hidden = (u * half).astype(bf16)
            slope = half + 0.5 * u * (1.0 - tanh * tanh) * (root * (1.0 + 0.134145 * square))
            grad_up = (nt(grad_out, down_piece) * slope).astype(bf16)
            r.hidden[chunk(i), lane] = hidden
            r.grad_up[chunk(i), lane] = grad_up
            first = nn(hidden, down_piece)
            second = nt(grad_up, up_piece)
            forward = first if forward is None else forward + first
            backward = second if backward is None else backward + second
        sum_start(0, i, backward)
        sum_start(1, i, forward)

    def keep_sums(k, shift, scale):
        r.sums[k : k + 1, :] += shift
        r.sums[k + 1 : k + 2, :] += scale

    def after_feed(i):
        stream = r.x2[i]
        grad, shift, scale = norm_backward(stream, mod(5), sum_end(0, i))
        keep_sums(4, shift, scale)
        grad = r.buf_b[i, s].astype(f32) + grad
        r.buf_b2[i, s] = grad.astype(bf16)
        gather_start(r.buf_b2, i)
        r.dx[i] = grad

    def layer_output(i):
        total = r.x2[i] + sum_end(1, i)
        r.part_side[i, 0, 0] = total.astype(bf16)
        output_copy(i).start()

    def self_back(i):
        gather_wait(r.buf_b2, i)
        grad = nt(r.buf_b2[i].reshape(rows, D), W[OS][...].reshape(C, D)).astype(bf16)
        attend_back(i, *own, grad, None, r.grad_up)

    def grads_into(place, lhs, rhs, width):
        def one(o, _):
            value = tn(lhs(col(o, z.block)), rhs()).astype(bf16)
            place[o // 2, lax.rem(o, 2), :, :width] = value
            return 0

        lax.fori_loop(0, B, one, 0)

    def whole(buf):
        return lambda lane: buf[:, :, :, lane].reshape(z.tokens, z.block)

    def feed_grads():
        grads_into(
            r.grads_b,
            lambda lane: r.hidden[:, lane],
            lambda: r.buf_b[...].reshape(z.tokens, D),
            D,
        )
        for k in range(3):
            grad_start(k)
        grads_into(r.grads_a, whole(r.buf_a), lambda: r.grad_up[...], z.hidden)

    pipeline(
        {
            0: [(weight_pass, 10)],
            1: [(weight_pass, 11)],
            2: [(weight_pass, 12)],
            4: [(weight_pass, 13)],
            9: [(grad_pass, 0), (grad_start, 3)],
            10: [(grad_pass, 1), (grad_start, 4)],
            11: [(grad_pass, 2), (grad_start, 5)],
        },
        (0, self_forward),
        (1, lambda i: sum_pass(0, i)),
        (2, after_self),
        (3, lambda i: gather_pass(r.buf_a, i)),
        (4, feed),
        (4, lambda i: at(i, n - 1, feed_grads)),
        (5, lambda i: sum_pass(0, i)),
        (6, after_feed),
        (7, lambda i: gather_pass(r.buf_b2, i)),
        (8, self_back),
        (8, lambda i: sum_pass(1, i)),
    )

    r.grad_up[:, C : 2 * C] = r.grad_key[:, : z.tokens].T.astype(bf16)
    r.grad_up[:, 2 * C : 3 * C] = r.grad_value[:, : z.tokens].T.astype(bf16)

    clear_keys()

    def self_down(i):
        sum_start(0, i, nt(r.grad_up[chunk(i), : 3 * C], W[QKV][...].reshape(D, 3 * C)))

        @functools.partial(at, i, 0)
        def _():
            value = tn(r.att2[...], r.buf_b2[...].reshape(z.tokens, D)).astype(bf16)
            r.grads_c[1] = value.reshape(2, z.block, D)

        @functools.partial(at, i, n - 1)
        def _():
            grads_into(r.grads_b, whole(r.buf_h2), lambda: r.grad_up[:, : 3 * C], 3 * C)

    def after_self_down(i):
        grad, shift, scale = norm_backward(r.x1[i], mod(3), sum_end(0, i))
        keep_sums(2, shift, scale)
        grad = r.dx[i] + grad
        r.dx[i] = grad
        r.buf_b[i, s] = grad.astype(bf16)
        gather_start(r.buf_b, i)

    def cross_back(i):
        gather_wait(r.buf_b, i)
        grad = nt(r.buf_b[i].reshape(rows, D), W[OC][...].reshape(C, D)).astype(bf16)

        @functools.partial(at, i, n - 1)
        def _():
            value = tn(r.att1[...], r.buf_b[...].reshape(z.tokens, D)).astype(bf16)
            r.grads_c[0] = value.reshape(2, z.block, D)
            grad_start(11)

        attend_back(i, *cross, grad, mask_rows, r.hidden)
        sum_start(0, i, nt(r.hidden[chunk(i), :C], W[Q][...].reshape(D, C)))

    def after_cross_back(i):
        grad, shift, scale = norm_backward(r.x0[i].astype(f32), mod(1), sum_end(0, i))
        keep_sums(0, shift, scale)
        r.dx[i] += grad

    def last_grads():
        grads_into(r.grads_a, lambda lane: r.normed1[:, lane], lambda: r.hidden[:, :C], C)
        grad_start(12)
        for side, rest in enumerate((r.grad_key[...], r.grad_value[...])):
            total = None
            for _ in range(3):
                term = rest.astype(bf16)
                rest = rest - term.astype(f32)
                product_term = nn(term[:, : z.whole_rows], r.image_all[: z.whole_rows, :])
                product_term = product_term + nn(term[:, z.whole_rows :], r.tail[...])
                total = product_term if total is None else total + product_term
            value = total.T.astype(bf16)
            for o in range(B):
                r.grads_a[o // 2, o % 2, : z.image_block, C + side * C : C + (side + 1) * C] = value[
                    o * z.image_block : (o + 1) * z.image_block
                ]
        grad_start(13)

    pipeline(
        {
            0: [(grad_pass, 3), (grad_start, 6), (grad_end, 0)],
            1: [(grad_pass, 4), (grad_start, 7), (grad_end, 1)],
            3: [(grad_pass, 5), (grad_start, 8)],
            4: [(grad_pass, 6), (grad_end, 2), (grad_start, 9)],
            5: [(grad_pass, 7), (grad_end, 3), (grad_start, 10)],
            6: [(grad_pass, 8), (grad_end, 4), (grad_end, 5)],
            7: [(grad_turn, 8), (grad_pass, 9), (grad_end, 6), (grad_relay, 0), (grad_relay, 1)],
            8: [(grad_pass, 10), (grad_end, 7), (grad_relay, 2), (grad_relay, 3)],
            9: [(grad_end, 8), (grad_end, 9), (grad_relay, 4), (grad_relay, 5)],
        },
        (0, self_down),
        (1, lambda i: sum_pass(0, i)),
        (2, after_self_down),
        (3, lambda i: gather_pass(r.buf_b, i)),
        (3, layer_output),
        (4, cross_back),
        (4, lambda i: at(i, n - 1, last_grads)),
        (5, lambda i: sum_pass(0, i)),
        (6, after_cross_back),
    )
    grad_copy = pltpu.make_async_copy(r.dx, r.grad_tokens, r.sem_out.at[0])
    grad_copy.start()

    def sums_send(j):
        return remote(
            r.sums, r.sums_seq.at[s], r.sem_d_s.at[j - 1], r.sem_d_r.at[s], (b, lax.rem(s + j, S))
        )

    for j in range(1, S):
        sums_send(j).start()
    run([(grad_pass, 11), (grad_end, 10)])
    total = r.sums[...]
    for j in range(1, S):
        k = lax.rem(s + j, S)
        arrived(r.sums_seq.at[k], r.sem_d_s.at[0], r.sem_d_r.at[k], (b, k))
        total = total + r.sums_seq[k]
    r.mods_all[b] = total

    def table_send(j):
        return remote(
            r.mods_all.at[b],
            r.mods_all.at[b],
            r.sem_t_s.at[j - 1],
            r.sem_t_r.at[b],
            (lax.rem(b + j, B), s),
        )

    for j in range(1, B):
        table_send(j).start()
    run([(grad_pass, 12), (grad_turn, 11), (grad_pass, 13)])
    for j in range(1, B):
        k = lax.rem(b + j, B)
        arrived(r.mods_all.at[k], r.sem_t_s.at[0], r.sem_t_r.at[k], (k, s))
    table_copy = pltpu.make_async_copy(r.mods_all, r.table, r.sem_out.at[1])
    table_copy.start()
    run([(grad_end, 11), (grad_end, 12), (grad_end, 13)])
    run([(grad_relay, k) for k in range(6, len(SCATTER))])
    for j in range(1, S):
        sums_send(j).wait_send()
    for j in range(1, B):
        table_send(j).wait_send()
    for k in range(len(GATHER)):
        weight_drain(k)
    for k in range(len(SCATTER)):
        grad_drain(k)
    for i in range(n):
        output_copy(i).wait()
    grad_copy.wait()
    table_copy.wait()


def layer_call(z, args):
    n, part, D, C, S, B = z.chunks, z.part, z.width, z.columns, z.seq, z.batch
    Z = B // 2
    own = (n, part, D)
    full = (n, S, part, D)
    vmem = pltpu.VMEM
    dma = pltpu.SemaphoreType.DMA
    weights = [
        vmem((2, z.block, D) if w in BY_ROWS else (B,) + shape, bf16)
        for w, shape in enumerate(z.weights)
    ]
    firsts = [
        vmem((z.block, D) if w in BY_ROWS else (Z,) + shape, bf16)
        for w, shape in enumerate(z.weights)
    ]
    seconds = [vmem((Z - 1,) + shape, bf16) for shape in z.weights]
    lane = [
        vmem((n, 2, 2, part, D), bf16),
        vmem((n, 2, part, D), bf16),
        vmem((n, part, D), bf16),
        vmem((n, part, D), bf16),
    ]
    scratch = (
        weights
        + firsts
        + seconds
        + [vmem(full, bf16)] * 4
        + lane
        + lane
        + [
            vmem((Z,) + z.weights[OC], bf16),
            vmem((Z,) + z.weights[OS], bf16),
            vmem((S,) + z.weights[OC], bf16),
            vmem((S,) + z.weights[OS], bf16),
            vmem((z.image_rows, z.image_width), bf16),
            vmem((z.keys - z.whole_rows, z.image_width), bf16),
            vmem((1, z.image_rows), jnp.int32),
            vmem((8, z.keys), f32),
            vmem(args[5].shape, bf16),
            vmem((B, 8, D), f32),
            vmem((8, D), f32),
            vmem((8, D), f32),
            vmem((S, 8, D), f32),
            vmem((z.tokens, D), bf16),
            vmem((z.tokens, C), bf16),
            vmem((z.keys, C), bf16),
            vmem((z.keys, C), bf16),
            vmem((z.tokens, C), bf16),
            vmem((z.tokens, 3 * C), bf16),
            vmem((z.tokens, C), bf16),
            vmem((z.tokens, z.hidden), bf16),
            vmem((z.tokens, z.hidden), bf16),
            vmem((C, z.keys), f32),
            vmem((C, z.keys), f32),
            vmem(own, bf16),
            vmem(own, f32),
            vmem(own, f32),
            vmem(own, f32),
            vmem((Z, 2, z.block, D), bf16),
            vmem((Z, 2, z.block, D), bf16),
            vmem((2, 2, z.block, D), bf16),
            dma((33,)),
            dma((len(GATHER), Z)),
            dma((len(GATHER), Z)),
            dma((len(GATHER), Z)),
            dma((len(GATHER), Z)),
            dma((len(SCATTER),)),
            dma((len(SCATTER),)),
            dma((len(SCATTER), 3)),
            dma((len(SCATTER), Z)),
            dma((len(SCATTER), 3)),
            dma((len(SCATTER), 3)),
            dma((len(SCATTER),)),
            dma((2, S - 1)),
            dma((2, S)),
            dma((2, S - 1)),
            dma((2, S)),
            dma((2, 3)),
            dma((2, 3)),
            dma((n, 3)),
            dma((n, 3)),
            dma((2, n, 2)),
            dma((2, n, 2)),
            dma((B - 1,)),
            dma((B,)),
            dma((S - 1,)),
            dma((S,)),
            dma((B - 1,)),
            dma((B,)),
            dma((2 + n,)),
        ]
    )
    shape = jax.ShapeDtypeStruct
    outs = [shape(own, bf16), shape(own, f32), shape((B, 8, D), f32)] + [
        shape((S,) + size, bf16) for size in z.weights
    ]
    anywhere = pl.BlockSpec(memory_space=pl.ANY)
    scalars = pl.BlockSpec(memory_space=pltpu.SMEM)
    return pl.pallas_call(
        functools.partial(whole_layer, z),
        out_shape=outs,
        in_specs=[anywhere] * 4 + [scalars] + [anywhere] * (len(args) - 5),
        out_specs=[anywhere] * len(outs),
        scratch_shapes=scratch,
        compiler_params=pltpu.CompilerParams(
            collective_id=0, has_side_effects=True, vmem_limit_bytes=LIMIT
        ),
        name="whole_layer",
    )(*args)


def finish(z, camera, output, grad_tokens, table, *refs):
    grads, outs = refs[:7], refs[7:]
    gate_t = refs[-1]
    step = pl.program_id(0)
    outs[0][...] = output[...]
    outs[1][...] = grad_tokens[...]

    @pl.when(step == 0)
    def _():
        own = camera[...].astype(f32)
        gate_t[...] = (own * jax.nn.sigmoid(own)).astype(bf16).astype(f32).T

    lanes = z.block // z.seq
    gate = gate_t[pl.ds(pl.multiple_of(step * lanes, 8), lanes), :]
    for k in range(6):
        outs[2][:, k * z.width : (k + 1) * z.width] = jnp.dot(
            gate, table[:, k, :], precision=highest, preferred_element_type=f32
        )

    def across(w, out, groups):
        width = grads[w].shape[2] // groups
        for j in range(z.seq):
            for g in range(groups):
                column = (g * z.seq + j) * width
                out[:, column : column + width] = grads[w][j, :, g * width : (g + 1) * width].astype(f32)

    across(Q, outs[3], 1)
    across(KV, outs[4], 2)
    outs[5][...] = grads[OC][0].astype(f32)
    across(QKV, outs[6], 3)
    outs[7][...] = grads[OS][0].astype(f32)
    across(UP, outs[8], z.batch)
    outs[9][...] = grads[DOWN][0].astype(f32)


def finish_call(z, camera, output, grad_tokens, table, *grads):
    S, D = z.seq, z.width
    n = z.chunks // S
    few = z.block // S
    few_image = z.image_block // S
    own = pl.BlockSpec((n, z.part, D), lambda i: (i, 0, 0))
    whole = pl.BlockSpec(table.shape, lambda i: (0, 0, 0))

    def quarter(w):
        if w in (OC, OS, DOWN):
            return pl.BlockSpec((1,) + grads[w].shape[1:], lambda i: (i, 0, 0))
        return pl.BlockSpec((S, grads[w].shape[1] // S, grads[w].shape[2]), lambda i: (0, i, 0))

    def rows(count, width):
        return pl.BlockSpec((count, width), lambda i: (i, 0))

    sizes = (
        (few, z.block, 6 * D),
        (few, z.block, D),
        (few_image, z.image_block, 2 * D),
        (few, z.block, D),
        (few, z.block, 3 * D),
        (few, z.block, D),
        (few, z.block, S * z.hidden),
        (z.hidden // z.batch, S * z.hidden // z.batch, D),
    )
    results = pl.pallas_call(
        functools.partial(finish, z),
        grid=(S,),
        out_shape=[
            jax.ShapeDtypeStruct(output.shape, bf16),
            jax.ShapeDtypeStruct(grad_tokens.shape, f32),
        ]
        + [jax.ShapeDtypeStruct((count, width), f32) for _, count, width in sizes],
        in_specs=[pl.BlockSpec(camera.shape, lambda i: (0, 0)), own, own, whole]
        + [quarter(w) for w in range(7)],
        out_specs=[own, own] + [rows(block, width) for block, _, width in sizes],
        scratch_shapes=[pltpu.VMEM((camera.shape[1], camera.shape[0]), f32)],
        compiler_params=pltpu.CompilerParams(vmem_limit_bytes=LIMIT),
        name="finish",
    )(camera, output, grad_tokens, table, *grads)
    output, grad_tokens, *rest = results
    return (output.reshape(1, z.own, D), grad_tokens.reshape(1, z.own, D), *rest)


def local_kernel(sizes, *inputs):
    (
        tokens,
        cotangent,
        image_tokens,
        image_lengths,
        key_mask,
        camera,
        modulation,
        q_cross,
        kv_image,
        out_cross,
        qkv_self,
        out_self,
        mlp_in,
        mlp_out,
    ) = inputs
    z = sizes
    n, part, D, C, S, B = z.chunks, z.part, z.width, z.columns, z.seq, z.batch
    results = layer_call(
        z,
        (
            tokens[0].reshape(n, part, D),
            cotangent[0].reshape(n, part, D),
            image_tokens[0],
            key_mask,
            image_lengths,
            camera,
            modulation,
            q_cross,
            kv_image,
            out_cross,
            qkv_self,
            out_self,
            mlp_in,
            mlp_out,
        ),
    )
    return finish_call(z, camera, *results)


def fits(mesh, inputs):
    batch, seq = mesh.shape["batch"], mesh.shape["seq"]
    own, width = inputs[0].shape[1:]
    return (
        batch == 8
        and seq == 4
        and own % 64 == 0
        and width == HEADS * HEAD_DIM
        and (width // seq) % 128 == 0
        and (inputs[12].shape[1] // seq // batch) % 128 == 0
    )


def choose(mesh, *inputs):
    if not fits(mesh, inputs):
        return local(*inputs)
    return local_kernel(Sizes(mesh.shape, inputs), *inputs)


def solution(mesh):
    return jax.shard_map(
        functools.partial(choose, mesh),
        mesh=mesh,
        in_specs=(
            P("batch", "seq", None),
            P("batch", "seq", None),
            P("batch", None, None),
            P("batch"),
            P("batch", None),
            P(None, "batch"),
            P("batch", None),
            P("batch", None),
            P("batch", None),
            P("batch", None),
            P("batch", None),
            P("batch", None),
            P("batch", None),
            P("batch", None),
        ),
        out_specs=(
            P("batch", "seq", None),
            P("batch", "seq", None),
            P("batch", None),
            P("batch", None),
            P("batch", None),
            P("batch", None),
            P("batch", None),
            P("batch", None),
            P("batch", None),
            P("batch", None),
        ),
        check_vma=False,
    )
```

```python
import functools

import jax
import jax.numpy as jnp
from jax import lax
from jax.experimental import pallas as pl
from jax.experimental.pallas import tpu as pltpu
from jax.sharding import PartitionSpec as P

HEADS = 16
HEAD_DIM = 64


epsilon = 1e-06
group_heads = 4
highest = lax.Precision.HIGHEST
LIMIT = 64 * 1024 * 1024 - 64 * 1024


def modulated_norm(values, shift, scale):
    center = values - jnp.mean(values, axis=-1, keepdims=True)
    normed = center * lax.rsqrt(jnp.mean(center * center, axis=-1, keepdims=True) + epsilon)
    return normed * (1.0 + scale) + shift


def product(left, right):
    return jnp.dot(left, right, preferred_element_type=jnp.float32)


def contract_rows(left, right):
    return lax.dot_general(
        left, right, (((0,), (0,)), ((), ())), preferred_element_type=jnp.float32
    )


def times_transposed(left, right):
    return lax.dot_general(
        left, right, (((1,), (1,)), ((), ())), preferred_element_type=jnp.float32
    )


def split_heads(values):
    rows = values.shape[0]
    grouped = values.reshape(rows, HEADS // group_heads, group_heads, HEAD_DIM)
    return grouped.transpose(1, 2, 0, 3)


def join_heads(values):
    groups, inner, rows, depth = values.shape
    return values.transpose(2, 0, 1, 3).reshape(rows, groups * inner * depth)


def scores_of(query_group, key_group, valid):
    scores = jnp.einsum(
        "hqd,hkd->hqk", query_group, key_group, preferred_element_type=jnp.float32
    ) * HEAD_DIM ** (-0.5)
    return jnp.where(valid[None, None, :], scores, -1000000000.0)


def attend_forward(query, key_rows, value_rows, valid):

    def one_group(pieces):
        query_group, key_group, value_group = pieces
        scores = scores_of(query_group, key_group, valid)
        top = jnp.max(scores, axis=-1, keepdims=True)
        expo = jnp.exp(scores - top)
        total = jnp.sum(expo, axis=-1, keepdims=True)
        probs = (expo / total).astype(jnp.bfloat16)
        result = jnp.einsum("hqk,hkd->hqd", probs, value_group, preferred_element_type=jnp.float32)
        return (result, top, total)

    results, tops, totals = lax.map(
        one_group, (split_heads(query), split_heads(key_rows), split_heads(value_rows))
    )
    return (join_heads(results), (tops, totals))


def attend_backward(query, key_rows, value_rows, valid, stats, grad_output):
    tops, totals = stats

    def one_group(pieces):
        query_group, key_group, value_group, top, total, grad_group = pieces
        scores = scores_of(query_group, key_group, valid)
        probs = jnp.exp(scores - top) / total
        grad_probs = jnp.einsum(
            "hqd,hkd->hqk", grad_group, value_group, preferred_element_type=jnp.float32
        )
        inner = jnp.sum(probs * grad_probs, axis=-1, keepdims=True)
        grad_scores = (probs * (grad_probs - inner)).astype(jnp.bfloat16)
        factor = HEAD_DIM ** (-0.5)
        grad_query = (
            jnp.einsum("hqk,hkd->hqd", grad_scores, key_group, preferred_element_type=jnp.float32)
            * factor
        )
        grad_keys = (
            jnp.einsum("hqk,hqd->hkd", grad_scores, query_group, preferred_element_type=jnp.float32)
            * factor
        )
        grad_values = jnp.einsum(
            "hqk,hqd->hkd",
            probs.astype(jnp.bfloat16),
            grad_group,
            preferred_element_type=jnp.float32,
        )
        return (grad_query, inner, grad_keys, grad_values)

    results = lax.map(
        one_group,
        (
            split_heads(query),
            split_heads(key_rows),
            split_heads(value_rows),
            tops,
            totals,
            split_heads(grad_output),
        ),
    )
    return (join_heads(results[0]), results[1], join_heads(results[2]), join_heads(results[3]))


def local(
    tokens,
    cotangent,
    image_tokens,
    image_lengths,
    key_mask,
    camera,
    modulation,
    q_cross,
    kv_image,
    out_cross,
    qkv_self,
    out_self,
    mlp_in,
    mlp_out,
):
    q_full, kv_full, out_cross_full, qkv_full, out_self_full, mlp_in_full, mlp_out_full = (
        lax.all_gather(q_cross, "batch", axis=0, tiled=True),
        lax.all_gather(kv_image, "batch", axis=0, tiled=True),
        lax.all_gather(out_cross, "batch", axis=0, tiled=True),
        lax.all_gather(qkv_self, "batch", axis=0, tiled=True),
        lax.all_gather(out_self, "batch", axis=0, tiled=True),
        lax.all_gather(mlp_in, "batch", axis=0, tiled=True),
        lax.all_gather(mlp_out, "batch", axis=0, tiled=True),
    )
    camera_gate = jax.nn.silu(camera.astype(jnp.float32)).astype(jnp.bfloat16)
    modulation_all = lax.psum(product(camera_gate, modulation), "batch")
    object_index = lax.axis_index("batch")
    width = tokens.shape[2]
    shifts = lax.dynamic_index_in_dim(modulation_all, object_index, 0, keepdims=False).reshape(
        6, width
    )
    stream = tokens[0].astype(jnp.float32)
    image_rows = image_tokens[0]
    positions = jnp.arange(image_rows.shape[0], dtype=jnp.int32)
    valid = (positions < image_lengths[0]) & ((key_mask[0] == 1) | (positions == 0))
    everywhere = jnp.ones((lax.axis_size("seq") * stream.shape[0],), dtype=jnp.bool_)
    normed_cross, cross_pullback = jax.vjp(modulated_norm, stream, shifts[0], shifts[1])
    normed_cross = normed_cross.astype(jnp.bfloat16)
    query_cross = product(normed_cross, q_full).astype(jnp.bfloat16)
    image_kv = product(image_rows, kv_full)
    image_keys = image_kv[:, :width].astype(jnp.bfloat16)
    image_values = image_kv[:, width:].astype(jnp.bfloat16)
    attended_cross, cross_stats = attend_forward(query_cross, image_keys, image_values, valid)
    attended_cross = attended_cross.astype(jnp.bfloat16)
    after_cross = stream + product(attended_cross, out_cross_full)
    normed_self, self_pullback = jax.vjp(modulated_norm, after_cross, shifts[2], shifts[3])
    normed_self = normed_self.astype(jnp.bfloat16)
    packed = product(normed_self, qkv_full).astype(jnp.bfloat16)
    query_self = packed[:, :width]
    key_local = packed[:, width : 2 * width]
    value_local = packed[:, 2 * width :]
    key_whole, value_whole = (
        lax.all_gather(key_local, "seq", axis=0, tiled=True),
        lax.all_gather(value_local, "seq", axis=0, tiled=True),
    )
    attended_self, self_stats = attend_forward(query_self, key_whole, value_whole, everywhere)
    attended_self = attended_self.astype(jnp.bfloat16)
    after_self = after_cross + product(attended_self, out_self_full)
    normed_mlp, mlp_pullback = jax.vjp(modulated_norm, after_self, shifts[4], shifts[5])
    normed_mlp = normed_mlp.astype(jnp.bfloat16)
    up_rows = product(normed_mlp, mlp_in_full)
    hidden, gelu_pullback = jax.vjp(jax.nn.gelu, up_rows)
    hidden = hidden.astype(jnp.bfloat16)
    output = after_self + product(hidden, mlp_out_full)
    grad_stream = cotangent[0].astype(jnp.float32)
    grad_branch = grad_stream.astype(jnp.bfloat16)
    grad_mlp_out = contract_rows(hidden, grad_branch)
    (grad_up,) = gelu_pullback(times_transposed(grad_branch, mlp_out_full))
    grad_up = grad_up.astype(jnp.bfloat16)
    grad_mlp_in = contract_rows(normed_mlp, grad_up)
    grad_from, shift_mlp, scale_mlp = mlp_pullback(times_transposed(grad_up, mlp_in_full))
    grad_stream = grad_stream + grad_from
    grad_branch = grad_stream.astype(jnp.bfloat16)
    grad_out_self = contract_rows(attended_self, grad_branch)
    grad_attended = times_transposed(grad_branch, out_self_full).astype(jnp.bfloat16)
    grad_query, inner_local, key_terms, value_terms = attend_backward(
        query_self, key_whole, value_whole, everywhere, self_stats, grad_attended
    )
    grad_key, grad_value = (
        lax.psum_scatter(key_terms, "seq", scatter_dimension=0, tiled=True),
        lax.psum_scatter(value_terms, "seq", scatter_dimension=0, tiled=True),
    )
    grad_packed = jnp.concatenate([grad_query, grad_key, grad_value], axis=1).astype(jnp.bfloat16)
    grad_qkv_self = contract_rows(normed_self, grad_packed)
    grad_from, shift_self, scale_self = self_pullback(times_transposed(grad_packed, qkv_full))
    grad_stream = grad_stream + grad_from
    grad_branch = grad_stream.astype(jnp.bfloat16)
    grad_out_cross = contract_rows(attended_cross, grad_branch)
    grad_attended = times_transposed(grad_branch, out_cross_full).astype(jnp.bfloat16)
    grad_query, inner_cross, key_terms, value_terms = attend_backward(
        query_cross, image_keys, image_values, valid, cross_stats, grad_attended
    )
    image_float = image_rows.astype(jnp.float32)
    image_key_grad, image_value_grad = (
        lax.psum_scatter(
            key_terms.astype(jnp.bfloat16), "seq", scatter_dimension=1, tiled=True
        ).astype(jnp.float32),
        lax.psum_scatter(
            value_terms.astype(jnp.bfloat16), "seq", scatter_dimension=1, tiled=True
        ).astype(jnp.float32),
    )
    block_width = image_key_grad.shape[1]
    column_start = lax.axis_index("seq") * block_width
    image_grads = jnp.concatenate([image_key_grad, image_value_grad], axis=1)
    kv_block = lax.dot_general(
        image_float,
        image_grads,
        (((0,), (0,)), ((), ())),
        precision=highest,
        preferred_element_type=jnp.float32,
    )
    grad_kv_image = jnp.zeros((image_rows.shape[1], 2 * width), jnp.float32)
    grad_kv_image = lax.dynamic_update_slice(
        grad_kv_image, kv_block[:, :block_width], (jnp.int32(0), column_start)
    )
    grad_kv_image = lax.dynamic_update_slice(
        grad_kv_image, kv_block[:, block_width:], (jnp.int32(0), column_start + width)
    )
    grad_query = grad_query.astype(jnp.bfloat16)
    grad_q_cross = contract_rows(normed_cross, grad_query)
    grad_from, shift_cross, scale_cross = cross_pullback(times_transposed(grad_query, q_full))
    grad_input = grad_stream + grad_from
    grad_row = jnp.concatenate(
        [shift_cross, scale_cross, shift_self, scale_self, shift_mlp, scale_mlp]
    )
    grad_table = lax.dynamic_update_slice(
        jnp.zeros(modulation_all.shape, jnp.float32),
        grad_row[None, :],
        (object_index, jnp.int32(0)),
    )
    grad_table = lax.psum(grad_table, ("batch", "seq"))
    grad_modulation = lax.dot_general(
        camera_gate.astype(jnp.float32),
        grad_table,
        (((0,), (0,)), ((), ())),
        precision=highest,
        preferred_element_type=jnp.float32,
    )
    terms = (
        grad_q_cross,
        grad_kv_image,
        grad_out_cross,
        grad_qkv_self,
        grad_out_self,
        grad_mlp_in,
        grad_mlp_out,
    )
    shares = (
        lax.psum_scatter(
            terms[0].astype(jnp.bfloat16), "batch", scatter_dimension=0, tiled=True
        ).astype(jnp.float32),
        lax.psum_scatter(
            terms[1].astype(jnp.bfloat16), "batch", scatter_dimension=0, tiled=True
        ).astype(jnp.float32),
        lax.psum_scatter(
            terms[2].astype(jnp.bfloat16), "batch", scatter_dimension=0, tiled=True
        ).astype(jnp.float32),
        lax.psum_scatter(
            terms[3].astype(jnp.bfloat16), "batch", scatter_dimension=0, tiled=True
        ).astype(jnp.float32),
        lax.psum_scatter(
            terms[4].astype(jnp.bfloat16), "batch", scatter_dimension=0, tiled=True
        ).astype(jnp.float32),
        lax.psum_scatter(
            terms[5].astype(jnp.bfloat16), "batch", scatter_dimension=0, tiled=True
        ).astype(jnp.float32),
        lax.psum_scatter(
            terms[6].astype(jnp.bfloat16), "batch", scatter_dimension=0, tiled=True
        ).astype(jnp.float32),
    )
    totals = (
        lax.psum(shares[0].astype(jnp.bfloat16), "seq").astype(jnp.float32),
        lax.psum(shares[1].astype(jnp.bfloat16), "seq").astype(jnp.float32),
        lax.psum(shares[2].astype(jnp.bfloat16), "seq").astype(jnp.float32),
        lax.psum(shares[3].astype(jnp.bfloat16), "seq").astype(jnp.float32),
        lax.psum(shares[4].astype(jnp.bfloat16), "seq").astype(jnp.float32),
        lax.psum(shares[5].astype(jnp.bfloat16), "seq").astype(jnp.float32),
        lax.psum(shares[6].astype(jnp.bfloat16), "seq").astype(jnp.float32),
    )
    return (
        output.astype(jnp.bfloat16)[None],
        grad_input[None],
        grad_modulation,
        totals[0],
        totals[1],
        totals[2],
        totals[3],
        totals[4],
        totals[5],
        totals[6],
    )


bf16 = jnp.bfloat16
f32 = jnp.float32
MESH = pl.DeviceIdType.MESH
BELOW = -3.0e38


def nn(a, b):
    return jnp.dot(a, b, preferred_element_type=f32)


def nt(a, b):
    return lax.dot_general(a, b, (((1,), (1,)), ((), ())), preferred_element_type=f32)


def tn(a, b):
    return lax.dot_general(a, b, (((0,), (0,)), ((), ())), preferred_element_type=f32)


def one_head(pair, side):
    lane = lax.broadcasted_iota(jnp.int32, pair.shape, 1)
    return jnp.where(lane // HEAD_DIM == side, pair, jnp.zeros_like(pair))


def two_heads(first, second):
    lane = lax.broadcasted_iota(jnp.int32, first.shape, 1)
    return jnp.where(lane < HEAD_DIM, first, second)


def softmax_rows(scores, mask):
    if mask is not None:
        scores = jnp.where(mask[0:1, :] > 0.5, scores, mask[1:2, :])
    expo = jnp.exp(scores - jnp.max(scores, axis=-1, keepdims=True))
    return expo * (1.0 / jnp.sum(expo, axis=-1, keepdims=True))


def norm_stats(rows):
    center = rows - jnp.mean(rows, axis=-1, keepdims=True)
    inverse = lax.rsqrt(jnp.mean(center * center, axis=-1, keepdims=True) + epsilon)
    return center * inverse, inverse


def norm_forward(rows, shift, scale):
    return norm_stats(rows)[0] * (1.0 + scale) + shift


def norm_backward(rows, scale, grad):
    normed, inverse = norm_stats(rows)
    inner = grad * (1.0 + scale)
    mean_inner = jnp.mean(inner, axis=-1, keepdims=True)
    mean_cross = jnp.mean(inner * normed, axis=-1, keepdims=True)
    grad_rows = inverse * (inner - mean_inner - normed * mean_cross)
    return (
        grad_rows,
        jnp.sum(grad, axis=0, keepdims=True),
        jnp.sum(grad * normed, axis=0, keepdims=True),
    )


Q, KV, OC, QKV, OS, UP, DOWN, CAMERA, TABLE, TOKENS, OWN, IMAGE, COTANGENT = range(13)


GATHER = (
    (KV, 0, 1),
    (Q, 0, 1),
    (OC, 0, 1),
    (QKV, 0, 2),
    (QKV, 1, 2),
    (OS, 0, 1),
    (UP, 0, 4),
    (UP, 1, 4),
    (UP, 2, 4),
    (UP, 3, 4),
    (DOWN, 0, 4),
    (DOWN, 1, 4),
    (DOWN, 2, 4),
    (DOWN, 3, 4),
)
SCATTER = (
    (DOWN, 0, 4),
    (DOWN, 1, 4),
    (DOWN, 2, 4),
    (DOWN, 3, 4),
    (UP, 0, 4),
    (UP, 1, 4),
    (UP, 2, 4),
    (UP, 3, 4),
    (OS, 0, 1),
    (QKV, 0, 2),
    (QKV, 1, 2),
    (OC, 0, 1),
    (Q, 0, 2),
    (Q, 1, 2),
    (KV, 0, 3),
    (KV, 1, 3),
    (KV, 2, 3),
)
BY_ROWS = (OC, OS)
AHEAD = 2
EARLY = (3, 4, 6, 7, 8, 9)


class Sizes:
    def __init__(self, mesh_shape, inputs):
        self.batch, self.seq = mesh_shape["batch"], mesh_shape["seq"]
        self.own, self.width = inputs[0].shape[1:]
        self.image_rows, self.image_width = inputs[2].shape[1:]
        self.chunks = 4
        self.part = self.own // self.chunks
        self.rows = self.seq * self.part
        self.tokens = self.seq * self.own
        self.columns = self.width // self.seq
        self.hidden = inputs[12].shape[1] // self.seq
        self.keys = -(-self.image_rows // 128) * 128
        self.whole_rows = self.image_rows // 128 * 128
        self.block = self.width // self.batch
        self.image_block = self.image_width // self.batch
        self.weights = (
            (self.block, self.columns),
            (self.image_block, 2 * self.columns),
            (self.block // self.seq, self.width),
            (self.block, 3 * self.columns),
            (self.block // self.seq, self.width),
            (self.block, self.hidden),
            (self.hidden // self.batch, self.width),
        )


class Refs:
    def __init__(self, refs):
        rest = iter(refs)
        self.tokens = next(rest)
        self.cotangent = next(rest)
        self.image = next(rest)
        self.marks = next(rest)
        self.lengths = next(rest)
        self.camera = next(rest)
        self.modulation = next(rest)
        self.q_cross = next(rest)
        self.kv_image = next(rest)
        self.out_cross = next(rest)
        self.qkv_self = next(rest)
        self.out_self = next(rest)
        self.mlp_in = next(rest)
        self.mlp_out = next(rest)
        self.output = next(rest)
        self.grad_tokens = next(rest)
        self.table = next(rest)
        self.gout = [next(rest) for _ in range(7)]
        self.weights = [next(rest) for _ in range(7)]
        self.firsts = [next(rest) for _ in range(7)]
        self.seconds = [next(rest) for _ in range(7)]
        self.buf_a = next(rest)
        self.buf_b = next(rest)
        self.buf_h2 = next(rest)
        self.buf_b2 = next(rest)
        self.part_main = next(rest)
        self.core_main = next(rest)
        self.send_main = next(rest)
        self.line_main = next(rest)
        self.part_side = next(rest)
        self.core_side = next(rest)
        self.send_side = next(rest)
        self.line_side = next(rest)
        self.turn_in = [next(rest) for _ in range(2)]
        self.turn_out = [next(rest) for _ in range(2)]
        self.image_all = next(rest)
        self.tail = next(rest)
        self.marks_own = next(rest)
        self.mask_all = next(rest)
        self.camera_own = next(rest)
        self.mods_all = next(rest)
        self.mods = next(rest)
        self.sums = next(rest)
        self.sums_seq = next(rest)
        self.normed1 = next(rest)
        self.query1 = next(rest)
        self.key1 = next(rest)
        self.value1 = next(rest)
        self.att1 = next(rest)
        self.packed2 = next(rest)
        self.att2 = next(rest)
        self.hidden = next(rest)
        self.grad_up = next(rest)
        self.grad_key = next(rest)
        self.grad_value = next(rest)
        self.x0 = next(rest)
        self.x1 = next(rest)
        self.x2 = next(rest)
        self.dx = next(rest)
        self.grads_a = next(rest)
        self.grads_b = next(rest)
        self.grads_c = next(rest)
        self.sem_load = next(rest)
        self.sem_wz_s = next(rest)
        self.sem_wz_r = next(rest)
        self.sem_wx_s = next(rest)
        self.sem_wx_r = next(rest)
        self.sem_gx_s = next(rest)
        self.sem_gx_r = next(rest)
        self.sem_gz_s = next(rest)
        self.sem_gz_r = next(rest)
        self.sem_gs_s = next(rest)
        self.sem_gs_r = next(rest)
        self.sem_own = next(rest)
        self.sem_ti_s = next(rest)
        self.sem_ti_r = next(rest)
        self.sem_to_s = next(rest)
        self.sem_to_r = next(rest)
        self.sem_in_s = next(rest)
        self.sem_in_r = next(rest)
        self.sem_ag_s = next(rest)
        self.sem_ag_r = next(rest)
        self.sem_rs_s = next(rest)
        self.sem_rs_r = next(rest)
        self.sem_m_s = next(rest)
        self.sem_m_r = next(rest)
        self.sem_d_s = next(rest)
        self.sem_d_r = next(rest)
        self.sem_t_s = next(rest)
        self.sem_t_r = next(rest)
        self.sem_out = next(rest)


def whole_layer(z, *refs):
    r = Refs(refs)
    W, FIRST, SECOND, GOUT = r.weights, r.firsts, r.seconds, r.gout
    n, S, B = z.chunks, z.seq, z.batch
    part, rows, D, C = z.part, z.rows, z.width, z.columns
    Z = B // 2
    b = lax.axis_index("batch")
    s = lax.axis_index("seq")
    zz = b // 2
    x = lax.rem(b, 2)
    y = s // 2
    c = lax.rem(s, 2)
    other_x = 1 - x
    other_c = 1 - c
    other_y = 1 - y
    x_peer = (2 * zz + other_x, s)
    core_peer = (b, 2 * y + other_c)
    line_peer = (b, 2 * other_y + c)
    line_slot = 2 * other_y + c
    core_slot = 2 * y + other_c
    far_slot = 2 * other_y + other_c

    def z_of(j):
        return lax.rem(zz + j, Z)

    def remote(src, dst, send, recv, device):
        return pltpu.make_async_remote_copy(
            src_ref=src,
            dst_ref=dst,
            send_sem=send,
            recv_sem=recv,
            device_id=device,
            device_id_type=MESH,
        )

    def arrived(dst, send, recv, device):
        remote(dst, dst, send, recv, device).wait_recv()

    barrier = pltpu.get_barrier_semaphore()
    for j in range(1, B):
        pl.semaphore_signal(barrier, inc=1, device_id=(lax.rem(b + j, B), s), device_id_type=MESH)
    for j in range(1, S):
        pl.semaphore_signal(barrier, inc=1, device_id=(b, lax.rem(s + j, S)), device_id_type=MESH)

    loads = {}

    def load(key, src, dst):
        count = sum(len(copies) for copies in loads.values())
        copy = pltpu.make_async_copy(src, dst, r.sem_load.at[count])
        loads.setdefault(key, []).append(copy)
        copy.start()

    def col(index, width):
        return pl.ds(pl.multiple_of(index * width, 128), width)

    wide = z.hidden // B
    for j in range(2):
        load(
            KV,
            r.kv_image.at[:, pl.ds(pl.multiple_of(j * D + s * C, 128), C)],
            W[KV].at[b, :, pl.ds(j * C, C)],
        )
    load(Q, r.q_cross.at[:, col(s, C)], W[Q].at[b])
    load(TOKENS, r.tokens, r.buf_a.at[:, s])
    load(CAMERA, r.camera, r.camera_own)
    for k in range(6):
        load(TABLE, r.modulation.at[:, pl.ds(k * D, D)], r.hidden.at[pl.ds(k * z.block, z.block)])
    few = z.block // S
    load(OC, r.out_cross.at[pl.ds(pl.multiple_of(s * few, 16), few)], r.turn_in[0].at[zz])
    for j in range(3):
        load(
            QKV,
            r.qkv_self.at[:, pl.ds(pl.multiple_of(j * D + s * C, 128), C)],
            W[QKV].at[b, :, pl.ds(j * C, C)],
        )
    load(OS, r.out_self.at[pl.ds(pl.multiple_of(s * few, 16), few)], r.turn_in[1].at[zz])
    load(IMAGE, r.image, r.image_all)
    load(IMAGE, r.marks, r.marks_own)
    for j in range(B):
        load(
            UP,
            r.mlp_in.at[:, pl.ds(pl.multiple_of(j * (z.hidden * S // B) + s * wide, 128), wide)],
            W[UP].at[b, :, pl.ds(j * wide, wide)],
        )
    load(DOWN, r.mlp_out.at[pl.ds(pl.multiple_of(s * wide, 128), wide), :], W[DOWN].at[b])
    load(COTANGENT, r.cotangent, r.buf_b.at[:, s])
    load(OWN, r.tokens, r.x0)

    pl.semaphore_wait(barrier, B - 1 + S - 1)

    def loaded(key):
        for copy in loads[key]:
            copy.wait()

    def rows_of(piece):
        w, which, parts = piece
        count = z.weights[w][0] // parts
        return w, pl.ds(which * count, count)

    def turned(w):
        return 0 if w == OC else 1

    def quarter(index):
        return pl.ds(pl.multiple_of(index * few, 16), few)

    def z_place(k, from_z):
        w, span = rows_of(GATHER[k])
        return r.turn_in[turned(w)].at[from_z] if w in BY_ROWS else W[w].at[2 * from_z + x, span]

    def z_send(k, j):
        place = z_place(k, zz)
        return remote(
            place, place, r.sem_wz_s.at[k, j - 1], r.sem_wz_r.at[k, zz], (2 * z_of(j) + x, s)
        )

    def x_send(k, from_z):
        w, span = rows_of(GATHER[k])
        place, mark = (W[w].at[x], 0) if w in BY_ROWS else (z_place(k, from_z), from_z)
        return remote(place, place, r.sem_wx_s.at[k, mark], r.sem_wx_r.at[k, mark], x_peer)

    def turn_send(w, j):
        to = lax.rem(s + j, S)
        return remote(
            r.turn_in[turned(w)].at[to],
            W[w].at[x, quarter(s)],
            r.sem_ti_s.at[turned(w), j - 1],
            r.sem_ti_r.at[turned(w), s],
            (b, to),
        )

    def z_near(j):
        return (zz != Z - 1) if j == 1 else (zz != 0)

    def z_far(k):
        place = z_place(k, z_of(2))
        return remote(
            place,
            place,
            r.sem_wz_s.at[k, Z - 1],
            r.sem_wz_r.at[k, z_of(2)],
            (2 * (Z - 1) * (zz - 1) + x, s),
        )

    def between():
        return (zz == 1) | (zz == 2)

    def weight_start(k):
        if k >= len(GATHER):
            return
        w, which, _ = GATHER[k]
        if which == 0 and k not in EARLY:
            loaded(w)
        z_send(k, 2).start()
        for j in (1, 3):
            pl.when(z_near(j))(z_send(k, j).start)
        if w not in BY_ROWS and k not in EARLY:
            x_send(k, zz).start()

    def weight_came(k, j):
        w, _ = rows_of(GATHER[k])
        from_z = z_of(j)
        arrived(
            z_place(k, from_z), r.sem_wz_s.at[k, 0], r.sem_wz_r.at[k, from_z], (2 * from_z + x, s)
        )
        if w not in BY_ROWS:
            x_send(k, from_z).start()

    def weight_far(k):
        for j in (1, 3):
            pl.when(jnp.logical_not(z_near(j)))(functools.partial(weight_came, k, j))

    def weight_pass(k):
        w, _ = rows_of(GATHER[k])
        weight_came(k, 2)
        pl.when(between())(z_far(k).start)
        for j in (1, 3):
            pl.when(z_near(j))(functools.partial(weight_came, k, j))
        weight_start(k + AHEAD)
        if k and GATHER[k - 1][0] not in BY_ROWS:
            weight_far(k - 1)
        if w in BY_ROWS:
            weight_far(k)
            for j in range(1, S):
                turn_send(w, j).start()
            W[w][x, quarter(s), :] = r.turn_in[turned(w)][s]

    def weight_turn(k):
        w, _ = rows_of(GATHER[k])
        for j in range(1, S):
            m = lax.rem(s + j, S)
            arrived(
                W[w].at[x, quarter(m)], r.sem_ti_s.at[turned(w), 0], r.sem_ti_r.at[turned(w), m], (b, m)
            )
        x_send(k, zz).start()

    def weight_wait(w):
        for k in range(len(GATHER)):
            if GATHER[k][0] != w:
                continue
            _, span = rows_of(GATHER[k])
            if w in BY_ROWS:
                arrived(W[w].at[other_x], r.sem_wx_s.at[k, 0], r.sem_wx_r.at[k, 0], x_peer)
                continue
            for from_z in range(Z):
                place = W[w].at[2 * from_z + other_x, span]
                arrived(place, r.sem_wx_s.at[k, 0], r.sem_wx_r.at[k, from_z], x_peer)

    def weight_drain(k):
        w, _ = rows_of(GATHER[k])
        z_send(k, 2).wait_send()
        for j in (1, 3):
            pl.when(z_near(j))(z_send(k, j).wait_send)
        pl.when(between())(z_far(k).wait_send)
        if w in BY_ROWS:
            x_send(k, zz).wait_send()
            for j in range(1, S):
                turn_send(w, j).wait_send()
        else:
            for j in range(Z):
                x_send(k, z_of(j)).wait_send()

    def give(buf, i, k):
        slot, peer = [(s, core_peer), (s, line_peer), (line_slot, core_peer)][k]
        return remote(
            buf.at[i, slot], buf.at[i, slot], r.sem_ag_s.at[i, k], r.sem_ag_r.at[i, k], peer
        )

    def gather_start(buf, i):
        give(buf, i, 1).start()
        give(buf, i, 0).start()

    def gather_pass(buf, i):
        arrived(buf.at[i, line_slot], r.sem_ag_s.at[i, 1], r.sem_ag_r.at[i, 1], line_peer)
        give(buf, i, 2).start()

    def gather_wait(buf, i):
        arrived(buf.at[i, core_slot], r.sem_ag_s.at[i, 0], r.sem_ag_r.at[i, 0], core_peer)
        arrived(buf.at[i, far_slot], r.sem_ag_s.at[i, 2], r.sem_ag_r.at[i, 2], core_peer)
        for k in range(3):
            give(buf, i, k).wait_send()

    def give_input(buf, m, k):
        slot, peer = [(s, core_peer), (s, line_peer), (line_slot, core_peer)][k]
        return remote(
            buf.at[:, slot], buf.at[:, slot], r.sem_in_s.at[m, k], r.sem_in_r.at[m, k], peer
        )

    def input_start(buf, m):
        give_input(buf, m, 1).start()
        give_input(buf, m, 0).start()

    def input_pass(buf, m):
        arrived(buf.at[:, line_slot], r.sem_in_s.at[m, 1], r.sem_in_r.at[m, 1], line_peer)
        give_input(buf, m, 2).start()

    def input_wait(buf, m):
        arrived(buf.at[:, core_slot], r.sem_in_s.at[m, 0], r.sem_in_r.at[m, 0], core_peer)
        arrived(buf.at[:, far_slot], r.sem_in_s.at[m, 2], r.sem_in_r.at[m, 2], core_peer)
        for k in range(3):
            give_input(buf, m, k).wait_send()

    lanes = (
        (r.part_main, r.core_main, r.send_main, r.line_main),
        (r.part_side, r.core_side, r.send_side, r.line_side),
    )

    def sum_core(lane, i):
        mine, core, _, _ = lanes[lane]
        return remote(
            mine.at[i, :, other_c],
            core.at[i],
            r.sem_rs_s.at[lane, i, 0],
            r.sem_rs_r.at[lane, i, 0],
            core_peer,
        )

    def sum_line(lane, i):
        _, _, send, line = lanes[lane]
        return remote(
            send.at[i],
            line.at[i],
            r.sem_rs_s.at[lane, i, 1],
            r.sem_rs_r.at[lane, i, 1],
            line_peer,
        )

    def sum_start(lane, i, value):
        lanes[lane][0][i] = value.astype(bf16).reshape(2, 2, part, D)
        sum_core(lane, i).start()

    def sum_pass(lane, i):
        mine, core, send, _ = lanes[lane]
        sum_core(lane, i).wait_recv()
        send[i] = (mine[i, other_y, c].astype(f32) + core[i, other_y].astype(f32)).astype(bf16)
        sum_line(lane, i).start()

    def sum_end(lane, i):
        mine, core, _, line = lanes[lane]
        sum_line(lane, i).wait_recv()
        total = mine[i, y, c].astype(f32) + core[i, y].astype(f32) + line[i].astype(f32)
        sum_core(lane, i).wait_send()
        sum_line(lane, i).wait_send()
        return total

    def grad_place(w):
        return {
            Q: r.grads_a.at[:, :, :, pl.ds(0, C)],
            KV: r.grads_a.at[:, :, pl.ds(0, z.image_block), pl.ds(C, 2 * C)],
            OC: r.grads_c.at[0],
            QKV: r.grads_b.at[:, :, :, pl.ds(0, 3 * C)],
            OS: r.grads_c.at[1],
            UP: r.grads_a,
            DOWN: r.grads_b,
        }[w]

    def first_of(k):
        w, span = rows_of(SCATTER[k])
        return r.turn_out[turned(w)].at[zz] if w in BY_ROWS else FIRST[w].at[zz, span]

    def grad_x(k):
        w, span = rows_of(SCATTER[k])
        place = grad_place(w)
        src = place.at[other_x] if w in BY_ROWS else place.at[:, other_x, span]
        dst = FIRST[w] if w in BY_ROWS else FIRST[w].at[:, span]
        return remote(src, dst, r.sem_gx_s.at[k], r.sem_gx_r.at[k], x_peer)

    def turn_back(w, j):
        to = lax.rem(s + j, S)
        return remote(
            FIRST[w].at[quarter(to)],
            r.turn_out[turned(w)].at[s],
            r.sem_to_s.at[turned(w), j - 1],
            r.sem_to_r.at[turned(w), s],
            (b, to),
        )

    def grad_z(k, j):
        w, span = rows_of(SCATTER[k])
        to = z_of(j)
        src = r.turn_out[turned(w)].at[to] if w in BY_ROWS else FIRST[w].at[to, span]
        return remote(
            src,
            SECOND[w].at[Z - j - 1, span],
            r.sem_gz_s.at[k, j - 1],
            r.sem_gz_r.at[k, zz],
            (2 * to + x, s),
        )

    def shared(k, origin):
        w, span = rows_of(SCATTER[k])
        return GOUT[w].at[origin, span]

    def grad_s(k, way):
        mine = shared(k, line_slot) if way == 2 else first_of(k)
        origin = line_slot if way == 2 else s
        peer = line_peer if way == 1 else core_peer
        return remote(mine, shared(k, origin), r.sem_gs_s.at[k, way], r.sem_gs_r.at[k, way], peer)

    def grad_own(k):
        return pltpu.make_async_copy(first_of(k), shared(k, s), r.sem_own.at[k])

    def grad_relay(k):
        arrived(shared(k, line_slot), r.sem_gs_s.at[k, 1], r.sem_gs_r.at[k, 1], line_peer)
        grad_s(k, 2).start()

    def grad_start(k):
        grad_x(k).start()

    def grad_pass(k):
        w, span = rows_of(SCATTER[k])
        grad_x(k).wait_recv()
        place = grad_place(w)
        if w in BY_ROWS:
            FIRST[w][...] = (FIRST[w][...].astype(f32) + place[x].astype(f32)).astype(bf16)
            for j in range(1, S):
                turn_back(w, j).start()
            r.turn_out[turned(w)][s] = FIRST[w][quarter(s), :]
        else:
            for m in range(Z):
                term = FIRST[w][m, span].astype(f32) + place[m, x, span].astype(f32)
                FIRST[w][m, span] = term.astype(bf16)
            for j in range(1, Z):
                grad_z(k, j).start()
        grad_x(k).wait_send()

    def grad_turn(k):
        w, _ = rows_of(SCATTER[k])
        for j in range(1, S):
            m = lax.rem(s + j, S)
            arrived(
                r.turn_out[turned(w)].at[m],
                r.sem_to_s.at[turned(w), 0],
                r.sem_to_r.at[turned(w), m],
                (b, m),
            )
        for j in range(1, Z):
            grad_z(k, j).start()

    def grad_end(k):
        w, span = rows_of(SCATTER[k])
        mine = first_of(k)
        total = mine[...].astype(f32)
        for j in range(1, Z):
            m = z_of(j)
            term = SECOND[w].at[j - 1, span]
            arrived(term, r.sem_gz_s.at[k, 0], r.sem_gz_r.at[k, m], (2 * m + x, s))
            total = total + term[...].astype(f32)
        mine[...] = total.astype(bf16)
        grad_s(k, 1).start()
        grad_s(k, 0).start()
        grad_own(k).start()
        for j in range(1, Z):
            grad_z(k, j).wait_send()

    def grad_drain(k):
        w, _ = rows_of(SCATTER[k])
        arrived(shared(k, core_slot), r.sem_gs_s.at[k, 0], r.sem_gs_r.at[k, 0], core_peer)
        arrived(shared(k, far_slot), r.sem_gs_s.at[k, 2], r.sem_gs_r.at[k, 2], core_peer)
        for way in range(3):
            grad_s(k, way).wait_send()
        grad_own(k).wait()
        if w in BY_ROWS:
            for j in range(1, S):
                turn_back(w, j).wait_send()

    def mods_send(j):
        to = lax.rem(b + j, B)
        return remote(
            r.x2.at[0, pl.ds(pl.multiple_of(8 * to, 8), 8)],
            r.mods_all.at[b],
            r.sem_m_s.at[j - 1],
            r.sem_m_r.at[b],
            (to, s),
        )

    for k in range(AHEAD):
        weight_start(k)
    loaded(TOKENS)
    input_start(r.buf_a, 0)
    loaded(CAMERA)
    loaded(TABLE)
    camera = r.camera_own[...].astype(f32)
    gate = (camera * jax.nn.sigmoid(camera)).astype(bf16)
    for k in range(6):
        term = nn(gate, r.hidden[k * z.block : (k + 1) * z.block, :])
        for o in range(B):
            r.x2[0, 8 * o + k : 8 * o + k + 1, :] = term[o : o + 1, :]
    for j in range(1, B):
        mods_send(j).start()
    for k in EARLY:
        if GATHER[k][1] == 0:
            loaded(GATHER[k][0])
        x_send(k, zz).start()
    loaded(COTANGENT)
    input_start(r.buf_b, 1)
    loaded(IMAGE)
    loaded(OWN)
    places = lax.broadcasted_iota(jnp.int32, (1, z.image_rows), 1)
    valid = (places < r.lengths[0]) & ((r.marks_own[...] == 1) | (places == 0))
    places = lax.broadcasted_iota(jnp.int32, (1, z.keys), 1)
    r.mask_all[0:1, :] = jnp.zeros((1, z.keys), f32)
    r.mask_all[0:1, : z.image_rows] = jnp.where(valid, 1.0, 0.0)
    r.mask_all[1:2, :] = jnp.where(places < z.image_rows, -1000000000.0, BELOW)
    rest = z.image_rows - z.whole_rows
    last = r.image_all[z.whole_rows :, :]
    padding = jnp.zeros((z.keys - z.image_rows, z.image_width), bf16)
    r.tail[...] = jnp.concatenate([last, padding], axis=0) if rest else padding

    mods = r.x2[0, pl.ds(pl.multiple_of(8 * b, 8), 8)]
    for j in range(1, B):
        k = lax.rem(b + j, B)
        arrived(r.mods_all.at[k], r.sem_m_s.at[0], r.sem_m_r.at[k], (k, s))
        mods = mods + r.mods_all[k]
    r.mods[...] = mods
    for j in range(1, B):
        mods_send(j).wait_send()

    def mod(k):
        return r.mods[k : k + 1, :]

    def chunk(i):
        return pl.ds(pl.multiple_of(i * rows, rows), rows)

    scale_q = HEAD_DIM ** (-0.5)
    input_pass(r.buf_a, 0)
    weight_pass(0)
    weight_pass(1)
    input_wait(r.buf_a, 0)

    def normalize(i, _):
        rows_in = r.buf_a[i].reshape(rows, D).astype(f32)
        r.normed1[chunk(i), :] = norm_forward(rows_in, mod(0), mod(1)).astype(bf16)
        return 0

    lax.fori_loop(0, n, normalize, 0)
    weight_wait(KV)

    def project_rows(block, part_rows):
        both = nn(block, W[KV][...].reshape(z.image_width, 2 * C))
        r.key1[part_rows, :] = both[:, :C].astype(bf16)
        r.value1[part_rows, :] = both[:, C:].astype(bf16)

    def project_image(k, _):
        part_rows = pl.ds(pl.multiple_of(k * 128, 128), 128)
        project_rows(r.image_all[part_rows, :], part_rows)
        return 0

    lax.fori_loop(0, z.whole_rows // 128, project_image, 0)
    project_rows(r.tail[...], pl.ds(z.whole_rows, z.keys - z.whole_rows))
    weight_pass(2)
    weight_wait(Q)

    def project_query(i):
        query = nn(r.normed1[chunk(i), :], W[Q][...].reshape(D, C)).astype(bf16)
        r.query1[chunk(i), :] = (query * scale_q).astype(bf16)

    def attend(i, query, key, value, att, mask):
        for p in range(C // 128):
            lane = slice(128 * p, 128 * p + 128)
            pair = query(i, lane)
            keys, values = key(lane), value(lane)
            result = []
            for side in range(2):
                probs = softmax_rows(nt(one_head(pair, side), keys), mask).astype(bf16)
                result.append(nn(probs, values))
            att[chunk(i), lane] = two_heads(*result).astype(bf16)

    def attend_back(i, query, key, value, grad, mask, grad_query):
        query_t = query(i, slice(0, C)).T
        grad_t = grad.T
        for p in range(C // 128):
            lane = slice(128 * p, 128 * p + 128)
            pair, grad_pair = query(i, lane), grad[:, lane]
            keys, values = key(lane), value(lane)
            result = []
            for side in range(2):
                head = slice(128 * p + HEAD_DIM * side, 128 * p + HEAD_DIM * (side + 1))
                probs = softmax_rows(nt(one_head(pair, side), keys), mask)
                grad_probs = nt(one_head(grad_pair, side), values)
                inner = jnp.sum(probs * grad_probs, axis=-1, keepdims=True)
                scores = (probs * (grad_probs - inner)).astype(bf16)
                count = keys.shape[0]
                value_term = nn(grad_t[head, :], probs.astype(bf16))
                key_term = nn(query_t[head, :], scores)
                r.grad_value[head, :count] += value_term
                r.grad_key[head, :count] += key_term
                result.append(nn(scores, keys))
            grad_query[chunk(i), lane] = (two_heads(*result) * scale_q).astype(bf16)

    cross = (
        lambda i, lane: r.query1[chunk(i), lane],
        lambda lane: r.key1[:, lane],
        lambda lane: r.value1[:, lane],
    )

    def plus(lane, offset):
        return slice(lane.start + offset, lane.stop + offset)

    own = (
        lambda i, lane: r.packed2[chunk(i), lane],
        lambda lane: r.packed2[:, plus(lane, C)],
        lambda lane: r.packed2[:, plus(lane, 2 * C)],
    )
    mask_rows = r.mask_all

    def at(i, value, stage):
        pl.when(i == value)(stage)

    def run(calls):
        for call, *values in calls:
            call(*values)

    def pipeline(ticks, *stages):
        last = max(offset for offset, _ in stages)

        def body(step, _):
            for when, calls in ticks.items():
                at(step, when, functools.partial(run, calls))
            for offset, stage in stages:
                i = step - offset

                @pl.when((i >= 0) & (i < n))
                def _():
                    stage(i)

            return 0

        lax.fori_loop(0, n + last, body, 0)

    def cross_forward(i):
        project_query(i)
        attend(i, *cross, r.att1, mask_rows)
        at(i, 0, functools.partial(run, [(weight_turn, 2), (weight_wait, OC)]))
        sum_start(0, i, nn(r.att1[chunk(i), :], W[OC][...].reshape(C, D)))

    def after_cross(i):
        total = r.x0[i].astype(f32) + sum_end(0, i)
        r.x1[i] = total
        r.buf_h2[i, s] = norm_forward(total, mod(2), mod(3)).astype(bf16)
        gather_start(r.buf_h2, i)

    def project_self(i):
        at(i, 0, functools.partial(weight_wait, QKV))
        gather_wait(r.buf_h2, i)
        packed = nn(r.buf_h2[i].reshape(rows, D), W[QKV][...].reshape(D, 3 * C)).astype(bf16)
        r.packed2[chunk(i), :C] = (packed[:, :C] * scale_q).astype(bf16)
        r.packed2[chunk(i), C:] = packed[:, C:]

    pipeline(
        {
            1: [(weight_pass, 3)],
            2: [(weight_pass, 4)],
            3: [(weight_pass, 5)],
            4: [(weight_pass, 6)],
            5: [(weight_turn, 5), (weight_pass, 7)],
            6: [(weight_pass, 8)],
            7: [(weight_pass, 9)],
        },
        (0, cross_forward),
        (1, lambda i: sum_pass(0, i)),
        (2, after_cross),
        (3, lambda i: gather_pass(r.buf_h2, i)),
        (4, project_self),
    )

    weight_wait(OS)
    input_pass(r.buf_b, 1)
    input_wait(r.buf_b, 1)
    r.sums[...] = jnp.zeros_like(r.sums)

    def clear_keys():
        r.grad_key[...] = jnp.zeros_like(r.grad_key)
        r.grad_value[...] = jnp.zeros_like(r.grad_value)

    clear_keys()

    def output_copy(i):
        return pltpu.make_async_copy(
            r.part_side.at[i, 0, 0], r.output.at[i], r.sem_out.at[2 + i]
        )

    def self_forward(i):
        attend(i, *own, r.att2, None)
        sum_start(0, i, nn(r.att2[chunk(i), :], W[OS][...].reshape(C, D)))

    def after_self(i):
        total = r.x1[i] + sum_end(0, i)
        r.x2[i] = total
        r.buf_a[i, s] = norm_forward(total, mod(4), mod(5)).astype(bf16)
        gather_start(r.buf_a, i)

    def feed(i):
        at(i, 0, functools.partial(run, [(weight_far, 13), (weight_wait, UP), (weight_wait, DOWN)]))
        gather_wait(r.buf_a, i)
        rows_in = r.buf_a[i].reshape(rows, D)
        grad_out = r.buf_b[i].reshape(rows, D)
        up = W[UP]
        down = W[DOWN]
        forward = backward = None
        pieces = 2
        wide_piece = z.hidden // pieces
        for k in range(pieces):
            lane = slice(k * wide_piece, (k + 1) * wide_piece)
            up_piece = up[:, :, lane].reshape(D, wide_piece)
            down_piece = down[k * (B // pieces) : (k + 1) * (B // pieces)].reshape(wide_piece, D)
            u = nn(rows_in, up_piece)
            square = u * u
            root = 0.7978845608028654
            tanh = jnp.tanh(root * u * (1.0 + 0.044715 * square))
            half = 0.5 * (1.0 + tanh)
            hidden = (u * half).astype(bf16)
            slope = half + 0.5 * u * (1.0 - tanh * tanh) * (root * (1.0 + 0.134145 * square))
            grad_up = (nt(grad_out, down_piece) * slope).astype(bf16)
            r.hidden[chunk(i), lane] = hidden
            r.grad_up[chunk(i), lane] = grad_up
            first = nn(hidden, down_piece)
            second = nt(grad_up, up_piece)
            forward = first if forward is None else forward + first
            backward = second if backward is None else backward + second
        sum_start(0, i, backward)
        sum_start(1, i, forward)

    def keep_sums(k, shift, scale):
        r.sums[k : k + 1, :] += shift
        r.sums[k + 1 : k + 2, :] += scale

    def after_feed(i):
        stream = r.x2[i]
        grad, shift, scale = norm_backward(stream, mod(5), sum_end(0, i))
        keep_sums(4, shift, scale)
        grad = r.buf_b[i, s].astype(f32) + grad
        r.buf_b2[i, s] = grad.astype(bf16)
        gather_start(r.buf_b2, i)
        r.dx[i] = grad

    def layer_output(i):
        total = r.x2[i] + sum_end(1, i)
        r.part_side[i, 0, 0] = total.astype(bf16)
        output_copy(i).start()

    def self_back(i):
        gather_wait(r.buf_b2, i)
        grad = nt(r.buf_b2[i].reshape(rows, D), W[OS][...].reshape(C, D)).astype(bf16)
        attend_back(i, *own, grad, None, r.grad_up)

    def grads_into(place, lhs, rhs, width):
        def one(o, _):
            value = tn(lhs(col(o, z.block)), rhs()).astype(bf16)
            place[o // 2, lax.rem(o, 2), :, :width] = value
            return 0

        lax.fori_loop(0, B, one, 0)

    def whole(buf):
        return lambda lane: buf[:, :, :, lane].reshape(z.tokens, z.block)

    def feed_grads():
        grads_into(
            r.grads_b,
            lambda lane: r.hidden[:, lane],
            lambda: r.buf_b[...].reshape(z.tokens, D),
            D,
        )
        for k in range(3):
            grad_start(k)
        grads_into(r.grads_a, whole(r.buf_a), lambda: r.grad_up[...], z.hidden)

    pipeline(
        {
            0: [(weight_pass, 10)],
            1: [(weight_pass, 11)],
            2: [(weight_pass, 12)],
            4: [(weight_pass, 13)],
            9: [(grad_pass, 0), (grad_start, 3)],
            10: [(grad_pass, 1), (grad_start, 4)],
            11: [(grad_pass, 2), (grad_start, 5)],
        },
        (0, self_forward),
        (1, lambda i: sum_pass(0, i)),
        (2, after_self),
        (3, lambda i: gather_pass(r.buf_a, i)),
        (4, feed),
        (4, lambda i: at(i, n - 1, feed_grads)),
        (5, lambda i: sum_pass(0, i)),
        (6, after_feed),
        (7, lambda i: gather_pass(r.buf_b2, i)),
        (8, self_back),
        (8, lambda i: sum_pass(1, i)),
    )

    r.grad_up[:, C : 2 * C] = r.grad_key[:, : z.tokens].T.astype(bf16)
    r.grad_up[:, 2 * C : 3 * C] = r.grad_value[:, : z.tokens].T.astype(bf16)

    clear_keys()

    def self_down(i):
        sum_start(0, i, nt(r.grad_up[chunk(i), : 3 * C], W[QKV][...].reshape(D, 3 * C)))

        @functools.partial(at, i, 0)
        def _():
            value = tn(r.att2[...], r.buf_b2[...].reshape(z.tokens, D)).astype(bf16)
            r.grads_c[1] = value.reshape(2, z.block, D)

        @functools.partial(at, i, n - 1)
        def _():
            grads_into(r.grads_b, whole(r.buf_h2), lambda: r.grad_up[:, : 3 * C], 3 * C)

    def after_self_down(i):
        grad, shift, scale = norm_backward(r.x1[i], mod(3), sum_end(0, i))
        keep_sums(2, shift, scale)
        grad = r.dx[i] + grad
        r.dx[i] = grad
        r.buf_b[i, s] = grad.astype(bf16)
        gather_start(r.buf_b, i)

    def cross_back(i):
        gather_wait(r.buf_b, i)
        grad = nt(r.buf_b[i].reshape(rows, D), W[OC][...].reshape(C, D)).astype(bf16)

        @functools.partial(at, i, n - 1)
        def _():
            value = tn(r.att1[...], r.buf_b[...].reshape(z.tokens, D)).astype(bf16)
            r.grads_c[0] = value.reshape(2, z.block, D)
            grad_start(11)

        attend_back(i, *cross, grad, mask_rows, r.hidden)
        sum_start(0, i, nt(r.hidden[chunk(i), :C], W[Q][...].reshape(D, C)))

    def after_cross_back(i):
        grad, shift, scale = norm_backward(r.x0[i].astype(f32), mod(1), sum_end(0, i))
        keep_sums(0, shift, scale)
        r.dx[i] += grad

    def last_grads():
        grad_pass(11)
        grads_into(r.grads_a, lambda lane: r.normed1[:, lane], lambda: r.hidden[:, :C], C)
        grad_start(12)
        grad_start(13)
        for side, rest in enumerate((r.grad_key[...], r.grad_value[...])):
            total = None
            for _ in range(3):
                term = rest.astype(bf16)
                rest = rest - term.astype(f32)
                product_term = nn(term[:, : z.whole_rows], r.image_all[: z.whole_rows, :])
                product_term = product_term + nn(term[:, z.whole_rows :], r.tail[...])
                total = product_term if total is None else total + product_term
            value = total.T.astype(bf16)
            for o in range(B):
                r.grads_a[o // 2, o % 2, : z.image_block, C + side * C : C + (side + 1) * C] = value[
                    o * z.image_block : (o + 1) * z.image_block
                ]
        grad_start(14)
        grad_start(15)

    pipeline(
        {
            0: [(grad_pass, 3), (grad_start, 6), (grad_end, 0)],
            1: [(grad_pass, 4), (grad_start, 7), (grad_end, 1)],
            2: [(weight_drain, k) for k in range(len(GATHER))],
            3: [(grad_pass, 5), (grad_start, 8)],
            4: [(grad_pass, 6), (grad_end, 2), (grad_start, 9)],
            5: [(grad_pass, 7), (grad_end, 3), (grad_start, 10)],
            6: [(grad_pass, 8), (grad_end, 4), (grad_end, 5)],
            7: [(grad_turn, 8), (grad_pass, 9), (grad_end, 6), (grad_relay, 0), (grad_relay, 1)],
            8: [(grad_pass, 10), (grad_turn, 11), (grad_end, 7), (grad_relay, 2), (grad_relay, 3)],
            9: [(grad_pass, 12), (grad_pass, 13), (grad_end, 8), (grad_end, 9), (grad_relay, 4), (grad_relay, 5)],
        },
        (0, self_down),
        (1, lambda i: sum_pass(0, i)),
        (2, after_self_down),
        (3, lambda i: gather_pass(r.buf_b, i)),
        (3, layer_output),
        (4, cross_back),
        (4, lambda i: at(i, n - 1, last_grads)),
        (5, lambda i: sum_pass(0, i)),
        (6, after_cross_back),
    )
    grad_copy = pltpu.make_async_copy(r.dx, r.grad_tokens, r.sem_out.at[0])
    grad_copy.start()

    def sums_send(j):
        return remote(
            r.sums, r.sums_seq.at[s], r.sem_d_s.at[j - 1], r.sem_d_r.at[s], (b, lax.rem(s + j, S))
        )

    for j in range(1, S):
        sums_send(j).start()
    run([(grad_pass, 14), (grad_start, 16), (grad_end, 10)])
    total = r.sums[...]
    for j in range(1, S):
        k = lax.rem(s + j, S)
        arrived(r.sums_seq.at[k], r.sem_d_s.at[0], r.sem_d_r.at[k], (b, k))
        total = total + r.sums_seq[k]
    r.mods_all[b] = total

    def table_send(j):
        return remote(
            r.mods_all.at[b],
            r.mods_all.at[b],
            r.sem_t_s.at[j - 1],
            r.sem_t_r.at[b],
            (lax.rem(b + j, B), s),
        )

    for j in range(1, B):
        table_send(j).start()
    run([(grad_pass, 15), (grad_end, 11), (grad_end, 12), (grad_pass, 16), (grad_end, 13)])
    for j in range(1, B):
        k = lax.rem(b + j, B)
        arrived(r.mods_all.at[k], r.sem_t_s.at[0], r.sem_t_r.at[k], (k, s))
    table_copy = pltpu.make_async_copy(r.mods_all, r.table, r.sem_out.at[1])
    table_copy.start()
    run([(grad_end, 14), (grad_end, 15), (grad_end, 16)])
    run([(grad_relay, k) for k in range(6, len(SCATTER))])
    run([(grad_drain, k) for k in range(6)])
    for j in range(1, S):
        sums_send(j).wait_send()
    for j in range(1, B):
        table_send(j).wait_send()
    for k in range(6, len(SCATTER)):
        grad_drain(k)
    for i in range(n):
        output_copy(i).wait()
    grad_copy.wait()
    table_copy.wait()


def layer_call(z, args):
    n, part, D, C, S, B = z.chunks, z.part, z.width, z.columns, z.seq, z.batch
    Z = B // 2
    own = (n, part, D)
    full = (n, S, part, D)
    vmem = pltpu.VMEM
    dma = pltpu.SemaphoreType.DMA
    weights = [
        vmem((2, z.block, D) if w in BY_ROWS else (B,) + shape, bf16)
        for w, shape in enumerate(z.weights)
    ]
    firsts = [
        vmem((z.block, D) if w in BY_ROWS else (Z,) + shape, bf16)
        for w, shape in enumerate(z.weights)
    ]
    seconds = [vmem((Z - 1,) + shape, bf16) for shape in z.weights]
    lane = [
        vmem((n, 2, 2, part, D), bf16),
        vmem((n, 2, part, D), bf16),
        vmem((n, part, D), bf16),
        vmem((n, part, D), bf16),
    ]
    scratch = (
        weights
        + firsts
        + seconds
        + [vmem(full, bf16)] * 4
        + lane
        + lane
        + [
            vmem((Z,) + z.weights[OC], bf16),
            vmem((Z,) + z.weights[OS], bf16),
            vmem((S,) + z.weights[OC], bf16),
            vmem((S,) + z.weights[OS], bf16),
            vmem((z.image_rows, z.image_width), bf16),
            vmem((z.keys - z.whole_rows, z.image_width), bf16),
            vmem((1, z.image_rows), jnp.int32),
            vmem((8, z.keys), f32),
            vmem(args[5].shape, bf16),
            vmem((B, 8, D), f32),
            vmem((8, D), f32),
            vmem((8, D), f32),
            vmem((S, 8, D), f32),
            vmem((z.tokens, D), bf16),
            vmem((z.tokens, C), bf16),
            vmem((z.keys, C), bf16),
            vmem((z.keys, C), bf16),
            vmem((z.tokens, C), bf16),
            vmem((z.tokens, 3 * C), bf16),
            vmem((z.tokens, C), bf16),
            vmem((z.tokens, z.hidden), bf16),
            vmem((z.tokens, z.hidden), bf16),
            vmem((C, z.keys), f32),
            vmem((C, z.keys), f32),
            vmem(own, bf16),
            vmem(own, f32),
            vmem(own, f32),
            vmem(own, f32),
            vmem((Z, 2, z.block, D), bf16),
            vmem((Z, 2, z.block, D), bf16),
            vmem((2, 2, z.block, D), bf16),
            dma((33,)),
            dma((len(GATHER), Z)),
            dma((len(GATHER), Z)),
            dma((len(GATHER), Z)),
            dma((len(GATHER), Z)),
            dma((len(SCATTER),)),
            dma((len(SCATTER),)),
            dma((len(SCATTER), 3)),
            dma((len(SCATTER), Z)),
            dma((len(SCATTER), 3)),
            dma((len(SCATTER), 3)),
            dma((len(SCATTER),)),
            dma((2, S - 1)),
            dma((2, S)),
            dma((2, S - 1)),
            dma((2, S)),
            dma((2, 3)),
            dma((2, 3)),
            dma((n, 3)),
            dma((n, 3)),
            dma((2, n, 2)),
            dma((2, n, 2)),
            dma((B - 1,)),
            dma((B,)),
            dma((S - 1,)),
            dma((S,)),
            dma((B - 1,)),
            dma((B,)),
            dma((2 + n,)),
        ]
    )
    shape = jax.ShapeDtypeStruct
    outs = [shape(own, bf16), shape(own, f32), shape((B, 8, D), f32)] + [
        shape((S,) + size, bf16) for size in z.weights
    ]
    anywhere = pl.BlockSpec(memory_space=pl.ANY)
    scalars = pl.BlockSpec(memory_space=pltpu.SMEM)
    return pl.pallas_call(
        functools.partial(whole_layer, z),
        out_shape=outs,
        in_specs=[anywhere] * 4 + [scalars] + [anywhere] * (len(args) - 5),
        out_specs=[anywhere] * len(outs),
        scratch_shapes=scratch,
        compiler_params=pltpu.CompilerParams(
            collective_id=0, has_side_effects=True, vmem_limit_bytes=LIMIT
        ),
        name="whole_layer",
    )(*args)


def finish(z, camera, output, grad_tokens, table, *refs):
    grads, outs = refs[:7], refs[7:]
    gate_t = refs[-1]
    step = pl.program_id(0)
    outs[0][...] = output[...]
    outs[1][...] = grad_tokens[...]

    @pl.when(step == 0)
    def _():
        own = camera[...].astype(f32)
        gate_t[...] = (own * jax.nn.sigmoid(own)).astype(bf16).astype(f32).T

    lanes = z.block // z.seq
    gate = gate_t[pl.ds(pl.multiple_of(step * lanes, 8), lanes), :]
    for k in range(6):
        outs[2][:, k * z.width : (k + 1) * z.width] = jnp.dot(
            gate, table[:, k, :], precision=highest, preferred_element_type=f32
        )

    def across(w, out, groups):
        width = grads[w].shape[2] // groups
        for j in range(z.seq):
            for g in range(groups):
                column = (g * z.seq + j) * width
                out[:, column : column + width] = grads[w][j, :, g * width : (g + 1) * width].astype(f32)

    across(Q, outs[3], 1)
    across(KV, outs[4], 2)
    outs[5][...] = grads[OC][0].astype(f32)
    across(QKV, outs[6], 3)
    outs[7][...] = grads[OS][0].astype(f32)
    across(UP, outs[8], z.batch)
    outs[9][...] = grads[DOWN][0].astype(f32)


def finish_call(z, camera, output, grad_tokens, table, *grads):
    S, D = z.seq, z.width
    n = z.chunks // S
    few = z.block // S
    few_image = z.image_block // S
    own = pl.BlockSpec((n, z.part, D), lambda i: (i, 0, 0))
    whole = pl.BlockSpec(table.shape, lambda i: (0, 0, 0))

    def quarter(w):
        if w in (OC, OS, DOWN):
            return pl.BlockSpec((1,) + grads[w].shape[1:], lambda i: (i, 0, 0))
        return pl.BlockSpec((S, grads[w].shape[1] // S, grads[w].shape[2]), lambda i: (0, i, 0))

    def rows(count, width):
        return pl.BlockSpec((count, width), lambda i: (i, 0))

    sizes = (
        (few, z.block, 6 * D),
        (few, z.block, D),
        (few_image, z.image_block, 2 * D),
        (few, z.block, D),
        (few, z.block, 3 * D),
        (few, z.block, D),
        (few, z.block, S * z.hidden),
        (z.hidden // z.batch, S * z.hidden // z.batch, D),
    )
    results = pl.pallas_call(
        functools.partial(finish, z),
        grid=(S,),
        out_shape=[
            jax.ShapeDtypeStruct(output.shape, bf16),
            jax.ShapeDtypeStruct(grad_tokens.shape, f32),
        ]
        + [jax.ShapeDtypeStruct((count, width), f32) for _, count, width in sizes],
        in_specs=[pl.BlockSpec(camera.shape, lambda i: (0, 0)), own, own, whole]
        + [quarter(w) for w in range(7)],
        out_specs=[own, own] + [rows(block, width) for block, _, width in sizes],
        scratch_shapes=[pltpu.VMEM((camera.shape[1], camera.shape[0]), f32)],
        compiler_params=pltpu.CompilerParams(vmem_limit_bytes=LIMIT),
        name="finish",
    )(camera, output, grad_tokens, table, *grads)
    output, grad_tokens, *rest = results
    return (output.reshape(1, z.own, D), grad_tokens.reshape(1, z.own, D), *rest)


def local_kernel(sizes, *inputs):
    (
        tokens,
        cotangent,
        image_tokens,
        image_lengths,
        key_mask,
        camera,
        modulation,
        q_cross,
        kv_image,
        out_cross,
        qkv_self,
        out_self,
        mlp_in,
        mlp_out,
    ) = inputs
    z = sizes
    n, part, D, C, S, B = z.chunks, z.part, z.width, z.columns, z.seq, z.batch
    results = layer_call(
        z,
        (
            tokens[0].reshape(n, part, D),
            cotangent[0].reshape(n, part, D),
            image_tokens[0],
            key_mask,
            image_lengths,
            camera,
            modulation,
            q_cross,
            kv_image,
            out_cross,
            qkv_self,
            out_self,
            mlp_in,
            mlp_out,
        ),
    )
    return finish_call(z, camera, *results)


def fits(mesh, inputs):
    batch, seq = mesh.shape["batch"], mesh.shape["seq"]
    own, width = inputs[0].shape[1:]
    return (
        batch == 8
        and seq == 4
        and own % 64 == 0
        and width == HEADS * HEAD_DIM
        and (width // seq) % 128 == 0
        and (inputs[12].shape[1] // seq // batch) % 128 == 0
    )


def choose(mesh, *inputs):
    if not fits(mesh, inputs):
        return local(*inputs)
    return local_kernel(Sizes(mesh.shape, inputs), *inputs)


def solution(mesh):
    return jax.shard_map(
        functools.partial(choose, mesh),
        mesh=mesh,
        in_specs=(
            P("batch", "seq", None),
            P("batch", "seq", None),
            P("batch", None, None),
            P("batch"),
            P("batch", None),
            P(None, "batch"),
            P("batch", None),
            P("batch", None),
            P("batch", None),
            P("batch", None),
            P("batch", None),
            P("batch", None),
            P("batch", None),
            P("batch", None),
        ),
        out_specs=(
            P("batch", "seq", None),
            P("batch", "seq", None),
            P("batch", None),
            P("batch", None),
            P("batch", None),
            P("batch", None),
            P("batch", None),
            P("batch", None),
            P("batch", None),
            P("batch", None),
        ),
        check_vma=False,
    )
```
